32 devices in a mesh: rep: 4 (over x, core), dp: 2 (over y), fsdp: 4 (over z).
Axes of the slice: x: 2, y: 2, z: 4, core: 2. Of those that a mesh axis runs over, the one named last changes fastest.
Arguments:
- images: bfloat16 [96, 256, 1152], P(('rep', 'dp', 'fsdp')), may hold values from -6 to 6
- cotangent: bfloat16 [96, 256, 1152], P(('rep', 'dp', 'fsdp')), may hold values from -6 to 6
- counts: int32 [32], P(('rep', 'dp', 'fsdp')), may hold values from 2 to 3, as said below
- timesteps: int32 [96], P(('rep', 'dp', 'fsdp')), may hold values from 0 to 999
- labels: int32 [96], P(('rep', 'dp', 'fsdp')), may hold values from 0 to 1000
- label_table: bfloat16 [1001, 1152], replicated, may hold values from -6 to 6
- step_count: int32 [1], replicated, may hold values from 2 to 20
- w_ada: float32 [1152, 6912], P('fsdp'), may hold values from -0.1875 to 0.1875
- w_qkv: float32 [1152, 3456], P('fsdp'), may hold values from -0.1875 to 0.1875
- w_proj: float32 [1152, 1152], P('fsdp'), may hold values from -1 to 1
- w_fc1: float32 [1152, 4608], P('fsdp'), may hold values from -0.1875 to 0.1875
- w_fc2: float32 [4608, 1152], P('fsdp'), may hold values from -0.09375 to 0.09375
- biases: float32 [16128], P('fsdp'), may hold values from -0.9 to 0.9
- first_ada: float32 [4, 1152, 6912], P('rep', 'fsdp'), may hold values from -40 to 40
- first_qkv: float32 [4, 1152, 3456], P('rep', 'fsdp'), may hold values from -28 to 28
- first_proj: float32 [4, 1152, 1152], P('rep', 'fsdp'), may hold values from -8 to 8
- first_fc1: float32 [4, 1152, 4608], P('rep', 'fsdp'), may hold values from -16 to 16
- first_fc2: float32 [4, 4608, 1152], P('rep', 'fsdp'), may hold values from -32 to 32
- first_bias: float32 [4, 16128], P('rep', 'fsdp'), may hold values from -32 to 32
- second_ada: float32 [4, 1152, 6912], P('rep', 'fsdp'), may hold values from 92.16 to 1505.28
- second_qkv: float32 [4, 1152, 3456], P('rep', 'fsdp'), may hold values from 49.152 to 774.144
- second_proj: float32 [4, 1152, 1152], P('rep', 'fsdp'), may hold values from 4.3008 to 67.584
- second_fc1: float32 [4, 1152, 4608], P('rep', 'fsdp'), may hold values from 13.5168 to 215.04
- second_fc2: float32 [4, 4608, 1152], P('rep', 'fsdp'), may hold values from 67.584 to 1075.2
- second_bias: float32 [4, 16128], P('rep', 'fsdp'), may hold values from 67.584 to 1075.2
- outer_ada: float32 [1152, 6912], P('fsdp'), may hold values from -0.09375 to 0.09375
- outer_qkv: float32 [1152, 3456], P('fsdp'), may hold values from -0.09375 to 0.09375
- outer_proj: float32 [1152, 1152], P('fsdp'), may hold values from -0.5 to 0.5
- outer_fc1: float32 [1152, 4608], P('fsdp'), may hold values from -0.09375 to 0.09375
- outer_fc2: float32 [4608, 1152], P('fsdp'), may hold values from -0.046875 to 0.046875
- outer_bias: float32 [16128], P('fsdp'), may hold values from -0.5 to 0.5
Outputs:
- output: bfloat16 [96, 256, 1152], P(('rep', 'dp', 'fsdp'))
- input_grad: bfloat16 [96, 256, 1152], P(('rep', 'dp', 'fsdp'))
- grad_ada: float32 [4, 1152, 6912], P('rep', 'fsdp')
- grad_qkv: float32 [4, 1152, 3456], P('rep', 'fsdp')
- grad_proj: float32 [4, 1152, 1152], P('rep', 'fsdp')
- grad_fc1: float32 [4, 1152, 4608], P('rep', 'fsdp')
- grad_fc2: float32 [4, 4608, 1152], P('rep', 'fsdp')
- grad_bias: float32 [4, 16128], P('rep', 'fsdp')
- first_next_ada: float32 [4, 1152, 6912], P('rep', 'fsdp')
- first_next_qkv: float32 [4, 1152, 3456], P('rep', 'fsdp')
- first_next_proj: float32 [4, 1152, 1152], P('rep', 'fsdp')
- first_next_fc1: float32 [4, 1152, 4608], P('rep', 'fsdp')
- first_next_fc2: float32 [4, 4608, 1152], P('rep', 'fsdp')
- first_next_bias: float32 [4, 16128], P('rep', 'fsdp')
- second_next_ada: float32 [4, 1152, 6912], P('rep', 'fsdp')
- second_next_qkv: float32 [4, 1152, 3456], P('rep', 'fsdp')
- second_next_proj: float32 [4, 1152, 1152], P('rep', 'fsdp')
- second_next_fc1: float32 [4, 1152, 4608], P('rep', 'fsdp')
- second_next_fc2: float32 [4, 4608, 1152], P('rep', 'fsdp')
- second_next_bias: float32 [4, 16128], P('rep', 'fsdp')
- delta_ada: float32 [1152, 6912], P('fsdp')
- delta_qkv: float32 [1152, 3456], P('fsdp')
- delta_proj: float32 [1152, 1152], P('fsdp')
- delta_fc1: float32 [1152, 4608], P('fsdp')
- delta_fc2: float32 [4608, 1152], P('fsdp')
- delta_bias: float32 [16128], P('fsdp')
- outer_next_ada: float32 [1152, 6912], P('fsdp')
- outer_next_qkv: float32 [1152, 3456], P('fsdp')
- outer_next_proj: float32 [1152, 1152], P('fsdp')
- outer_next_fc1: float32 [1152, 4608], P('fsdp')
- outer_next_fc2: float32 [4608, 1152], P('fsdp')
- outer_next_bias: float32 [16128], P('fsdp')
- weight_ada: float32 [1152, 6912], P('fsdp')
- weight_qkv: float32 [1152, 3456], P('fsdp')
- weight_proj: float32 [1152, 1152], P('fsdp')
- weight_fc1: float32 [1152, 4608], P('fsdp')
- weight_fc2: float32 [4608, 1152], P('fsdp')
- weight_bias: float32 [16128], P('fsdp')
The draws below stay inside these ranges and needn't reach their ends.
Inputs may be any that keep to these rules, and one draw needn't show every extreme that they name: `counts`: A device's live images fill its first slots; in every draw some device has 3 live images and some has one fewer.
All inputs are finite; a program needn't handle non-finite values.
Results may differ from the reference program's by a relative error of at most 0.034.
The reference program's roundings to bfloat16 on the way count: a program that leaves them out, or rounds other values in their place, can miss the bound.
Values may be sent and summed in bfloat16 or wider, within the bound.
No kernel may reach another device: no remote copies, remote signals or barrier semaphores. Data moves between devices by JAX's collectives and lax.ppermute only.
A program may use at most 512 MiB of HBM per device.

```python
import math
import jax
import jax.numpy as jnp
from jax import lax

D = 1152
HEADS = 16
FF = 4608
NCLASS = 1001
SEQ = 256
SLOTS = 3
NB = 16128
IMAGES = 96
N_REP = 4
N_DP = 2
N_FSDP = 4


def draw_counts(key, part):
    device_count = N_REP * N_DP * N_FSDP
    base = jax.random.randint(key, (device_count,), SLOTS - 1, SLOTS + 1)
    spots = jax.random.permutation(jax.random.fold_in(key, 7), device_count)
    base = base.at[spots[0]].set(SLOTS)
    base = base.at[spots[1]].set(SLOTS - 1)
    return base.astype(jnp.int32)


def place_ends(values, own_key, low, high):
    longest = values.shape.index(max(values.shape))
    spots = []
    for shift in (0, 1):
        where = [jax.random.randint(jax.random.fold_in(own_key, axis), (), 0, length) for axis, length in enumerate(values.shape)]
        where[longest] = (where[longest] + shift) % values.shape[longest]
        spots.append(tuple(where))
    return values.at[spots[0]].set(low).at[spots[1]].set(high)


def block_levels(rng, dims, split, low, largest):
    loudness = 1.0
    for dim, parts in split:
        heights = jax.random.uniform(jax.random.fold_in(jax.random.fold_in(rng, 6), dim), (parts,), jnp.float32, low / len(split), largest / len(split))
        loudness = loudness * jnp.repeat(jnp.exp(heights), dims[dim] // parts).reshape((-1,) + (1,) * (len(dims) - 1 - dim))
    return loudness


def gaussian(key, dims, scale, bound, shards=(), kind=jnp.bfloat16):
    entries = jax.random.normal(key, dims, jnp.float32) * scale
    if len(shards) > 0:
        entries = block_levels(key, dims, shards, -0.22, 0.18) * entries
    return jnp.clip(entries, min=-bound, max=bound).astype(kind)


def setup_inputs(seed: int = 0) -> dict:
    key_of = jax.random.split(jax.random.key(seed), 32)
    return {
        "images": gaussian(key_of[0], (IMAGES, SEQ, D), 1.0, 6.0, ((0, 32),)),
        "cotangent": gaussian(key_of[1], (IMAGES, SEQ, D), 1.0, 6.0, ((0, 32),)),
        "counts": draw_counts(jax.random.fold_in(key_of[31], 71), 0),
        "timesteps": place_ends(jax.random.randint(key_of[3], (IMAGES,), 0, 1000), jax.random.fold_in(key_of[3], 1), 0, 999).astype(jnp.int32),
        "labels": place_ends(jax.random.randint(key_of[4], (IMAGES,), 0, NCLASS), jax.random.fold_in(key_of[4], 1), 0, NCLASS - 1).astype(jnp.int32),
        "label_table": gaussian(key_of[5], (NCLASS, D), 1.0, 6.0),
        "step_count": jax.random.randint(key_of[6], (1,), 2, 21).astype(jnp.int32),
        "w_ada": gaussian(key_of[7], (D, 6 * D), D ** -0.5, 0.1875, ((0, 4),), jnp.float32),
        "w_qkv": gaussian(key_of[8], (D, 3 * D), D ** -0.5, 0.1875, ((0, 4),), jnp.float32),
        "w_proj": gaussian(key_of[9], (D, D), (D // 32) ** -0.5, 1.0, ((0, 4),), jnp.float32),
        "w_fc1": gaussian(key_of[10], (D, FF), D ** -0.5, 0.1875, ((0, 4),), jnp.float32),
        "w_fc2": gaussian(key_of[11], (FF, D), FF ** -0.5, 0.09375, ((0, 4),), jnp.float32),
        "biases": gaussian(key_of[12], (NB,), 0.15, 0.9, ((0, 4),), jnp.float32),
        "first_ada": gaussian(key_of[13], (N_REP, D, 6 * D), (0.084 * (SEQ * SLOTS * N_DP * N_FSDP) ** 0.5), 40.0, ((0, 4), (1, 4)), jnp.float32),
        "first_qkv": gaussian(key_of[14], (N_REP, D, 3 * D), (0.06 * (SEQ * SLOTS * N_DP * N_FSDP) ** 0.5), 28.0, ((0, 4), (1, 4)), jnp.float32),
        "first_proj": gaussian(key_of[15], (N_REP, D, D), (0.018 * (SEQ * SLOTS * N_DP * N_FSDP) ** 0.5), 8.0, ((0, 4), (1, 4)), jnp.float32),
        "first_fc1": gaussian(key_of[16], (N_REP, D, FF), (0.032 * (SEQ * SLOTS * N_DP * N_FSDP) ** 0.5), 16.0, ((0, 4), (1, 4)), jnp.float32),
        "first_fc2": gaussian(key_of[17], (N_REP, FF, D), (0.07 * (SEQ * SLOTS * N_DP * N_FSDP) ** 0.5), 32.0, ((0, 4), (1, 4)), jnp.float32),
        "first_bias": gaussian(key_of[18], (N_REP, NB), (0.07 * (SEQ * SLOTS * N_DP * N_FSDP) ** 0.5), 32.0, ((0, 4), (1, 4)), jnp.float32),
        "second_ada": jnp.clip(jnp.exp(math.log(1505.28) - 2.793208 * jax.random.uniform(key_of[19], (N_REP, D, 6 * D), jnp.float32) ** block_levels(key_of[19], (N_REP, D, 6 * D), ((0, 4), (1, 4)), -0.2, 0.2)), 92.16, 1505.28),
        "second_qkv": jnp.clip(jnp.exp(math.log(774.144) - 2.7568403 * jax.random.uniform(key_of[20], (N_REP, D, 3 * D), jnp.float32) ** block_levels(key_of[20], (N_REP, D, 3 * D), ((0, 4), (1, 4)), -0.2, 0.2)), 49.152, 774.144),
        "second_proj": jnp.clip(jnp.exp(math.log(67.584) - 2.7545702 * jax.random.uniform(key_of[21], (N_REP, D, D), jnp.float32) ** block_levels(key_of[21], (N_REP, D, D), ((0, 4), (1, 4)), -0.2, 0.2)), 4.3008, 67.584),
        "second_fc1": jnp.clip(jnp.exp(math.log(215.04) - 2.7668907 * jax.random.uniform(key_of[22], (N_REP, D, FF), jnp.float32) ** block_levels(key_of[22], (N_REP, D, FF), ((0, 4), (1, 4)), -0.2, 0.2)), 13.5168, 215.04),
        "second_fc2": jnp.clip(jnp.exp(math.log(1075.2) - 2.7668907 * jax.random.uniform(key_of[23], (N_REP, FF, D), jnp.float32) ** block_levels(key_of[23], (N_REP, FF, D), ((0, 4), (1, 4)), -0.2, 0.2)), 67.584, 1075.2),
        "second_bias": jnp.clip(jnp.exp(math.log(1075.2) - 2.7668907 * jax.random.uniform(key_of[24], (N_REP, NB), jnp.float32) ** block_levels(key_of[24], (N_REP, NB), ((0, 4), (1, 4)), -0.2, 0.2)), 67.584, 1075.2),
        "outer_ada": gaussian(key_of[25], (D, 6 * D), (0.5 / D ** 0.5), 0.09375, ((0, 4),), jnp.float32),
        "outer_qkv": gaussian(key_of[26], (D, 3 * D), (0.5 / D ** 0.5), 0.09375, ((0, 4),), jnp.float32),
        "outer_proj": gaussian(key_of[27], (D, D), (0.5 / (D // 32) ** 0.5), 0.5, ((0, 4),), jnp.float32),
        "outer_fc1": gaussian(key_of[28], (D, FF), (0.5 / D ** 0.5), 0.09375, ((0, 4),), jnp.float32),
        "outer_fc2": gaussian(key_of[29], (FF, D), (0.5 / FF ** 0.5), 0.046875, ((0, 4),), jnp.float32),
        "outer_bias": gaussian(key_of[30], (NB,), 0.08, 0.5, ((0, 4),), jnp.float32),
    }


@jax.custom_vjp
def low(v):
    return lax.optimization_barrier(v.astype(jnp.bfloat16)).astype(jnp.float32)

@jax.custom_vjp
def low_back(v):
    return v

def low_keep(v):
    return (low(v), None)

def low_pass(kept, grad):
    return (grad,)

def back_keep(v):
    return (v, None)

def back_low(kept, grad):
    return (low(grad),)
low.defvjp(low_keep, low_pass)
low_back.defvjp(back_keep, back_low)
NORM_EPS = 1e-06
BETA_ONE = 0.9
BETA_TWO = 0.95
ADAM_EPS = 1e-08
WEIGHT_DECAY = 0.1
OUTER_RATE = 0.7
OUTER_MOMENTUM = 0.9

def normalize(values):
    center = values - lax.optimization_barrier(jnp.mean(values, axis=-1, keepdims=True))
    return center * lax.rsqrt(lax.optimization_barrier(jnp.mean(center * center, axis=-1, keepdims=True)) + NORM_EPS)

def time_embed(steps, width):
    half = width // 2
    frequency = jnp.exp(-math.log(10000.0) * jnp.arange(half).astype(jnp.float32) / half)
    angles = steps.astype(jnp.float32)[:, None] * frequency[None, :]
    return jnp.concatenate([jnp.cos(angles), jnp.sin(angles)], axis=1)

def learning_rates(width, hidden):
    return (2.0 / math.sqrt(width), 2.0 / math.sqrt(width), 2.0 / math.sqrt(width // 32), 2.0 / math.sqrt(width), 2.0 / math.sqrt(hidden), 0.3)

def device_block(params, images, style_rows, live):
    highest = lax.Precision.HIGHEST
    w_ada, w_qkv, w_proj, w_fc1, w_fc2, biases = params
    slots, length, width = images.shape
    hidden = w_fc1.shape[1]
    head_dim = width // HEADS
    b_ada = biases[:6 * width]
    b_query = biases[6 * width:7 * width]
    b_value = biases[7 * width:8 * width]
    b_proj = biases[8 * width:9 * width]
    b_fc1 = biases[9 * width:9 * width + hidden]
    b_fc2 = biases[9 * width + hidden:]
    modulation = low_back(jnp.dot(style_rows, w_ada, precision=highest) + b_ada)
    pieces = [modulation[:, None, index * width:(index + 1) * width] for index in range(6)]
    shift_one, scale_one, gate_one, shift_two, scale_two, gate_two = pieces
    attn_in = low(normalize(images) * (1.0 + scale_one) + shift_one)
    bias_packed = jnp.concatenate([b_query, jnp.zeros_like(b_query), b_value])
    packed = low(low_back(jnp.einsum('isd,de->ise', attn_in, w_qkv, precision=highest) + bias_packed))
    query = packed[:, :, :width].reshape(slots, length, HEADS, head_dim)
    keys = packed[:, :, width:2 * width].reshape(slots, length, HEADS, head_dim)
    values = packed[:, :, 2 * width:].reshape(slots, length, HEADS, head_dim)
    scores = low_back(jnp.einsum('iqhd,ikhd->ihqk', query, keys, precision=highest) / math.sqrt(head_dim))
    top = lax.optimization_barrier(jnp.max(scores, axis=-1, keepdims=True))
    raised = jnp.exp(scores - top)
    attention = low(raised / lax.optimization_barrier(jnp.sum(raised, axis=-1, keepdims=True)))
    attended = jnp.einsum('ihqk,ikhd->iqhd', attention, values, precision=highest).reshape(slots, length, width)
    attended = low(low_back(attended))
    attn_out = low_back(jnp.einsum('isd,de->ise', attended, w_proj, precision=highest) + b_proj)
    middle = images + gate_one * attn_out
    mlp_in = low(normalize(middle) * (1.0 + scale_two) + shift_two)
    hidden_pre = low_back(jnp.einsum('isd,df->isf', mlp_in, w_fc1, precision=highest) + b_fc1)
    activated = low(jax.nn.gelu(hidden_pre, approximate=True))
    mlp_out = low_back(jnp.einsum('isf,fd->isd', activated, w_fc2, precision=highest) + b_fc2)
    return (middle + gate_two * mlp_out) * live[:, None, None]

def reference(images, cotangent, counts, timesteps, labels, label_table, step_count, w_ada, w_qkv, w_proj, w_fc1, w_fc2, biases, first_ada, first_qkv, first_proj, first_fc1, first_fc2, first_bias, second_ada, second_qkv, second_proj, second_fc1, second_fc2, second_bias, outer_ada, outer_qkv, outer_proj, outer_fc1, outer_fc2, outer_bias):
    params = (w_ada, w_qkv, w_proj, w_fc1, w_fc2, biases)
    firsts = (first_ada, first_qkv, first_proj, first_fc1, first_fc2, first_bias)
    seconds = (second_ada, second_qkv, second_proj, second_fc1, second_fc2, second_bias)
    outers = (outer_ada, outer_qkv, outer_proj, outer_fc1, outer_fc2, outer_bias)
    device_count = counts.shape[0]
    total_images = images.shape[0]
    slots = total_images // device_count
    group_devices = device_count // N_REP
    positions = jnp.arange(total_images).astype(jnp.int32)
    owner = (positions // slots).astype(jnp.int32)
    live = (positions % slots < counts[owner]).astype(jnp.float32)
    condition = time_embed(timesteps, D) + label_table[labels].astype(jnp.float32)
    style = low(jax.nn.silu(condition))
    width = images.shape[2]
    length = images.shape[1]
    image_float = images.astype(jnp.float32).reshape(N_REP, group_devices, slots, length, width)
    cot_float = cotangent.astype(jnp.float32).reshape(N_REP, group_devices, slots, length, width)
    style_groups = style.reshape(N_REP, group_devices, slots, width)
    live_groups = live.reshape(N_REP, group_devices, slots)
    results = []
    image_grads = []
    group_grads = []
    for group in range(N_REP):
        style_here = style_groups[group]
        live_here = live_groups[group]

        def group_forward(weights, inputs):
            lowered = tuple((low(weight) for weight in weights))

            def one_device(pack):
                return device_block(lowered, pack[0], pack[1], pack[2])
            return lax.map(jax.checkpoint(one_device), (inputs, style_here, live_here))
        result, pullback = jax.vjp(group_forward, params, image_float[group])
        weight_grads, input_grads = pullback(cot_float[group])
        results.append(result.reshape(group_devices * slots, length, width))
        image_grads.append(input_grads.reshape(group_devices * slots, length, width))
        group_grads.append(weight_grads)
    output = jnp.concatenate(results, axis=0).astype(jnp.bfloat16)
    input_grad = jnp.concatenate(image_grads, axis=0).astype(jnp.bfloat16)
    power = step_count[0].astype(jnp.float32)
    fix_one = 1.0 - jnp.power(BETA_ONE, power)
    fix_two = 1.0 - jnp.power(BETA_TWO, power)
    rates = learning_rates(D, FF)
    grads_out = []
    firsts_out = []
    seconds_out = []
    deltas_out = []
    outers_out = []
    weights_out = []
    for index in range(6):
        gradient = jnp.stack([group_grads[group][index] for group in range(N_REP)])
        first_next = BETA_ONE * firsts[index] + (1.0 - BETA_ONE) * gradient
        second_next = BETA_TWO * seconds[index] + (1.0 - BETA_TWO) * gradient * gradient
        master = params[index][None]
        local = master - rates[index] * (first_next / fix_one / (jnp.sqrt(second_next / fix_two) + ADAM_EPS) + WEIGHT_DECAY * master)
        delta = lax.optimization_barrier(jnp.mean(master - local, axis=0))
        outer_next = OUTER_MOMENTUM * outers[index] + delta
        weight = params[index] - OUTER_RATE * (delta + OUTER_MOMENTUM * outer_next)
        grads_out.append(gradient)
        firsts_out.append(first_next)
        seconds_out.append(second_next)
        deltas_out.append(delta)
        outers_out.append(outer_next)
        weights_out.append(weight)
    return (output, input_grad, grads_out[0], grads_out[1], grads_out[2], grads_out[3], grads_out[4], grads_out[5], firsts_out[0], firsts_out[1], firsts_out[2], firsts_out[3], firsts_out[4], firsts_out[5], seconds_out[0], seconds_out[1], seconds_out[2], seconds_out[3], seconds_out[4], seconds_out[5], deltas_out[0], deltas_out[1], deltas_out[2], deltas_out[3], deltas_out[4], deltas_out[5], outers_out[0], outers_out[1], outers_out[2], outers_out[3], outers_out[4], outers_out[5], weights_out[0], weights_out[1], weights_out[2], weights_out[3], weights_out[4], weights_out[5])
```

```python
import math

import jax
import jax.numpy as jnp
from jax import lax
from jax.sharding import PartitionSpec as P

D = 1152
HEADS = 16
FF = 4608


NORM_EPS = 1e-06
BETA_ONE = 0.9
BETA_TWO = 0.95
ADAM_EPS = 1e-08
WEIGHT_DECAY = 0.1
OUTER_RATE = 0.7
OUTER_MOMENTUM = 0.9
FEW = 8

F32 = jnp.float32
BF16 = jnp.bfloat16


def dot(left, right):
    return jnp.dot(left, right, preferred_element_type=F32)


def dot_nt(left, right):
    return lax.dot_general(left, right, (((1,), (1,)), ((), ())), preferred_element_type=F32)


def dot_tn(left, right):
    return lax.dot_general(left, right, (((0,), (0,)), ((), ())), preferred_element_type=F32)


def time_embed(steps, width):
    half = width // 2
    frequency = jnp.exp(-math.log(10000.0) * jnp.arange(half).astype(F32) / half)
    angles = steps.astype(F32)[:, None] * frequency[None, :]
    return jnp.concatenate([jnp.cos(angles), jnp.sin(angles)], axis=1)


def learning_rates(width, hidden):
    return (
        2.0 / math.sqrt(width),
        2.0 / math.sqrt(width),
        2.0 / math.sqrt(width // 32),
        2.0 / math.sqrt(width),
        2.0 / math.sqrt(hidden),
        0.3,
    )


def shift_by(value, axis, step):
    size = lax.axis_size(axis)
    return lax.ppermute(value, axis, [(i, (i + step) % size) for i in range(size)])


def swap_with(value, axis, bit):
    size = lax.axis_size(axis)
    return lax.ppermute(value, axis, [(i, i ^ bit) for i in range(size)])


def gather_line(value, axis):
    size = lax.axis_size(axis)
    if size > FEW:
        return lax.all_gather(value, axis, axis=0)
    place = lax.axis_index(axis)
    result = jnp.zeros((size,) + value.shape, value.dtype)
    for step in range(size):
        piece = value if step == 0 else shift_by(value, axis, step)
        result = lax.dynamic_update_index_in_dim(result, piece, (place - step) % size, 0)
    return result


def scatter_line(value, axis):
    size = lax.axis_size(axis)
    if size > FEW:
        return lax.psum_scatter(value, axis, scatter_dimension=0, tiled=False)
    place = lax.axis_index(axis)
    total = lax.dynamic_index_in_dim(value, place, 0, keepdims=False)
    for step in range(1, size):
        piece = lax.dynamic_index_in_dim(value, (place + step) % size, 0, keepdims=False)
        total = total + shift_by(piece, axis, step)
    return total


def moments(values):
    center = values - jnp.mean(values, axis=-1, keepdims=True)
    inverse = lax.rsqrt(jnp.mean(center * center, axis=-1, keepdims=True) + NORM_EPS)
    return center * inverse, inverse


def norm_back(normed, inverse, upstream):
    first = jnp.mean(upstream, axis=-1, keepdims=True)
    second = jnp.mean(upstream * normed, axis=-1, keepdims=True)
    return (upstream - first - normed * second) * inverse


def gelu_pair(h):
    c = math.sqrt(2.0 / math.pi)
    inner = c * (h + 0.044715 * h * h * h)
    t = jnp.tanh(inner)
    value = 0.5 * h * (1.0 + t)
    slope = 0.5 * (1.0 + t) + 0.5 * h * (1.0 - t * t) * c * (1.0 + 3.0 * 0.044715 * h * h)
    return value, slope


def attention_forward(packed, slots, length):
    width = packed.shape[1] // 3
    head_dim = width // HEADS
    factor = 1.0 / math.sqrt(head_dim)
    split = packed.reshape(slots, length, 3, HEADS, head_dim)
    query, keys, values = split[:, :, 0], split[:, :, 1], split[:, :, 2]
    scores = jnp.einsum("iqhd,ikhd->ihqk", query, keys, preferred_element_type=F32) * factor
    top = jnp.max(scores, axis=-1, keepdims=True)
    raised = jnp.exp(scores - top)
    summed = jnp.sum(raised, axis=-1, keepdims=True)
    probs = (raised / summed).astype(BF16)
    log_total = top + jnp.log(summed)
    attended = jnp.einsum("ihqk,ikhd->iqhd", probs, values, preferred_element_type=F32)
    return attended.astype(BF16).reshape(slots * length, width), (query, keys, values, probs, log_total)


def attention_backward(saved, d_attended, slots, length):
    query, keys, values, probs, log_total = saved
    width = d_attended.shape[1]
    head_dim = width // HEADS
    factor = 1.0 / math.sqrt(head_dim)
    d_att = d_attended.reshape(slots, length, HEADS, head_dim)
    scores = jnp.einsum("iqhd,ikhd->ihqk", query, keys, preferred_element_type=F32) * factor
    weights = jnp.exp(scores - log_total)
    d_probs = jnp.einsum("iqhd,ikhd->ihqk", d_att, values, preferred_element_type=F32)
    d_scores = weights * (d_probs - jnp.sum(weights * d_probs, axis=-1, keepdims=True))
    d_scores = d_scores.astype(BF16)
    d_query = jnp.einsum("ihqk,ikhd->iqhd", d_scores, keys, preferred_element_type=F32) * factor
    d_keys = jnp.einsum("ihqk,iqhd->ikhd", d_scores, query, preferred_element_type=F32) * factor
    d_values = jnp.einsum("ihqk,iqhd->ikhd", probs, d_att, preferred_element_type=F32)
    pieces = [piece.astype(BF16).reshape(slots * length, width) for piece in (d_query, d_keys, d_values)]
    return jnp.concatenate(pieces, axis=1)


def own_half(value, index):
    return lax.dynamic_index_in_dim(value, index, 1, keepdims=False)


def body(
    images,
    cotangent,
    counts,
    timesteps,
    labels,
    label_table,
    step_count,
    w_ada,
    w_qkv,
    w_proj,
    w_fc1,
    w_fc2,
    biases,
    first_ada,
    first_qkv,
    first_proj,
    first_fc1,
    first_fc2,
    first_bias,
    second_ada,
    second_qkv,
    second_proj,
    second_fc1,
    second_fc2,
    second_bias,
    outer_ada,
    outer_qkv,
    outer_proj,
    outer_fc1,
    outer_fc2,
    outer_bias,
):
    masters = (w_ada, w_qkv, w_proj, w_fc1, w_fc2, biases)
    firsts = (first_ada, first_qkv, first_proj, first_fc1, first_fc2, first_bias)
    seconds = (second_ada, second_qkv, second_proj, second_fc1, second_fc2, second_bias)
    outers = (outer_ada, outer_qkv, outer_proj, outer_fc1, outer_fc2, outer_bias)
    slots, length, width = images.shape
    tokens = slots * length
    rows = w_qkv.shape[0]
    rows_two = w_fc2.shape[0]
    lines = lax.axis_size("fsdp")
    groups = lax.axis_size("rep")
    rep = lax.axis_index("rep")
    pair = lax.axis_index("dp")
    line = lax.axis_index("fsdp")
    half = rows // 2
    everyone = ("rep", "fsdp", "dp")

    def rows_of(weight):
        return lax.dynamic_slice_in_dim(weight, pair * half, half, axis=0).astype(BF16)

    attention_cut = jnp.concatenate([rows_of(w_qkv), rows_of(w_proj)], axis=1)
    attention_cut = lax.dynamic_slice_in_dim(attention_cut, rep * width, width, axis=1)
    gathered = lax.all_gather(attention_cut, everyone, axis=0, tiled=True).reshape(4, width, width)
    w_qkv_all = jnp.transpose(gathered[:3], (1, 0, 2)).reshape(width, 3 * width)
    w_proj_all = gathered[3]
    one_cut = lax.dynamic_slice(w_fc1, (pair * half, rep * width), (half, width)).astype(BF16)
    one_all = lax.all_gather(one_cut, everyone, axis=0, tiled=True).reshape(FF // width, width, width)
    w_fc1_all = jnp.transpose(one_all, (1, 0, 2)).reshape(width, FF)
    eighth = rows_two // (2 * groups)
    two_cut = lax.dynamic_slice_in_dim(w_fc2, (rep * 2 + pair) * eighth, eighth, axis=0).astype(BF16)
    w_fc2_all = lax.all_gather(two_cut, ("fsdp", "rep", "dp"), axis=0, tiled=True)

    live = (jnp.arange(slots) < counts[0]).astype(F32)
    condition = time_embed(timesteps, D) + jnp.take(label_table, labels, axis=0).astype(F32)
    style = jax.nn.silu(condition).astype(BF16)
    message = jnp.concatenate([style.reshape(-1), biases.astype(BF16)])
    heard = gather_line(message, "fsdp")
    bias_all = heard[:, slots * width :].reshape(-1).astype(F32)
    style_line = heard[:, : slots * width].reshape(lines * slots, width)
    style_cut = lax.dynamic_slice_in_dim(style_line, line * rows, rows, axis=1)
    mod_part = dot(style_cut, w_ada.astype(BF16))
    b_ada = bias_all[: 6 * width]
    b_query = bias_all[6 * width : 7 * width]
    b_value = bias_all[7 * width : 8 * width]
    b_proj = bias_all[8 * width : 9 * width]
    b_fc1 = bias_all[9 * width : 9 * width + FF]
    b_fc2 = bias_all[9 * width + FF :]
    modulation = scatter_line(mod_part.reshape(lines, slots, 6 * width), "fsdp") + b_ada

    def spread(index):
        return modulation[:, None, index * width : (index + 1) * width]

    shift_one, scale_one, gate_one, shift_two, scale_two, gate_two = (spread(i) for i in range(6))

    def flat(value):
        return value.reshape(tokens, value.shape[-1])

    def cube(value):
        return value.reshape(slots, length, value.shape[-1])

    residual = images.astype(F32)
    normed_one, inverse_one = moments(residual)
    attn_in = flat((normed_one * (1.0 + scale_one) + shift_one).astype(BF16))
    bias_packed = jnp.concatenate([b_query, jnp.zeros_like(b_query), b_value])
    packed = (dot(attn_in, w_qkv_all) + bias_packed).astype(BF16)
    attended, saved = attention_forward(packed, slots, length)
    attn_out = cube(dot(attended, w_proj_all) + b_proj)
    middle = residual + gate_one * attn_out
    normed_two, inverse_two = moments(middle)
    mlp_in = flat((normed_two * (1.0 + scale_two) + shift_two).astype(BF16))
    hidden = dot(mlp_in, w_fc1_all) + b_fc1
    activated_float, slope = gelu_pair(hidden)
    activated = activated_float.astype(BF16)

    upstream = cotangent.astype(F32) * live[:, None, None]
    d_mlp = flat((gate_two * upstream).astype(BF16))
    grad_two = dot_tn(activated, d_mlp).astype(BF16)
    d_hidden = (dot_nt(d_mlp, w_fc2_all) * slope).astype(BF16)
    grad_one = dot_tn(mlp_in, d_hidden).astype(BF16)

    def pair_first(gradient):
        parts = gradient.reshape(lines, 2, gradient.shape[0] // (2 * lines), gradient.shape[1])
        there = swap_with(own_half(parts, 1 - pair), "dp", 1)
        both = (own_half(parts, pair).astype(F32) + there.astype(F32)).astype(BF16)
        return lax.psum_scatter(
            both.reshape(-1, gradient.shape[1]), "fsdp", scatter_dimension=0, tiled=True
        )

    two_half = pair_first(grad_two)
    one_half = pair_first(grad_one)

    mlp_out = cube(dot(activated, w_fc2_all) + b_fc2)
    result = ((middle + gate_two * mlp_out) * live[:, None, None]).astype(BF16)
    d_gate_two = jnp.sum(upstream * mlp_out, axis=1)
    d_mlp_in = cube(dot_nt(d_hidden, w_fc1_all))
    d_shift_two = jnp.sum(d_mlp_in, axis=1)
    d_scale_two = jnp.sum(d_mlp_in * normed_two, axis=1)
    d_middle = upstream + norm_back(normed_two, inverse_two, d_mlp_in * (1.0 + scale_two))
    d_attn = flat((gate_one * d_middle).astype(BF16))
    d_gate_one = jnp.sum(d_middle * attn_out, axis=1)
    grad_proj = dot_tn(attended, d_attn).astype(BF16)
    proj_half = lax.psum_scatter(grad_proj, ("fsdp", "dp"), scatter_dimension=0, tiled=True)
    d_attended = dot_nt(d_attn, w_proj_all).astype(BF16)
    d_packed = attention_backward(saved, d_attended, slots, length)
    grad_qkv = dot_tn(attn_in, d_packed).astype(BF16)
    qkv_half = lax.psum_scatter(grad_qkv, ("fsdp", "dp"), scatter_dimension=0, tiled=True)
    d_attn_in = cube(dot_nt(d_packed, w_qkv_all))
    d_shift_one = jnp.sum(d_attn_in, axis=1)
    d_scale_one = jnp.sum(d_attn_in * normed_one, axis=1)
    d_residual = norm_back(normed_one, inverse_one, d_attn_in * (1.0 + scale_one))
    in_grad = (d_middle + d_residual).astype(BF16)
    d_modulation = jnp.concatenate(
        [d_shift_one, d_scale_one, d_gate_one, d_shift_two, d_scale_two, d_gate_two], axis=1
    ).astype(BF16)
    packed_sums = jnp.sum(d_packed.astype(F32), axis=0)
    bias_sums = jnp.concatenate(
        [
            packed_sums[:width],
            packed_sums[2 * width :],
            jnp.sum(d_attn.astype(F32), axis=0),
            jnp.sum(d_hidden.astype(F32), axis=0),
            jnp.sum(d_mlp.astype(F32), axis=0),
        ]
    ).astype(BF16)

    report = jnp.concatenate([style.reshape(-1), d_modulation.reshape(-1), bias_sums])
    report = jnp.stack([report, swap_with(report, "dp", 1)])
    reports = gather_line(report, "fsdp").reshape(2 * lines, -1)
    edge = slots * width
    style_group = reports[:, :edge].reshape(2 * lines * slots, width)
    mod_group = reports[:, edge : 7 * edge].reshape(2 * lines * slots, 6 * width)
    style_own = lax.dynamic_slice_in_dim(style_group, line * rows, rows, axis=1)
    grad_ada = dot_tn(style_own, mod_group)
    bias_group = jnp.concatenate(
        [
            jnp.sum(mod_group.astype(F32), axis=0),
            jnp.sum(reports[:, 7 * edge :].astype(F32), axis=0),
        ]
    )
    own_bias = biases.shape[0]
    grad_bias = lax.dynamic_slice_in_dim(bias_group, line * own_bias, own_bias, axis=0)

    def both_halves(piece):
        other = swap_with(piece, "dp", 1)
        first = jnp.where(pair == 0, piece, other)
        second = jnp.where(pair == 0, other, piece)
        return jnp.concatenate([first, second], axis=0).astype(F32)

    reduced = (
        grad_ada,
        both_halves(qkv_half),
        both_halves(proj_half),
        both_halves(one_half),
        both_halves(two_half),
        grad_bias,
    )

    power = step_count[0].astype(F32)
    fix_one = 1.0 - jnp.power(BETA_ONE, power)
    fix_two = 1.0 - jnp.power(BETA_TWO, power)
    rates = learning_rates(D, FF)
    firsts_out = []
    seconds_out = []
    local_deltas = []
    for index in range(6):
        gradient = reduced[index]
        first_next = BETA_ONE * firsts[index][0] + (1.0 - BETA_ONE) * gradient
        second_next = BETA_TWO * seconds[index][0] + (1.0 - BETA_TWO) * gradient * gradient
        master = masters[index]
        local = master - rates[index] * (
            first_next / fix_one / (jnp.sqrt(second_next / fix_two) + ADAM_EPS)
            + WEIGHT_DECAY * master
        )
        firsts_out.append(first_next[None])
        seconds_out.append(second_next[None])
        local_deltas.append((master - local).astype(BF16))

    def sum_groups(delta):
        if delta.ndim == 1:
            total = (delta.astype(F32) + swap_with(delta, "rep", 1).astype(F32)).astype(BF16)
            return total.astype(F32) + swap_with(total, "rep", 2).astype(F32)
        quarter = delta.shape[0] // 4
        columns = delta.shape[1]
        low = rep % 2
        mine = lax.dynamic_slice_in_dim(delta, pair * 2 * quarter, 2 * quarter, axis=0)
        mine = mine.reshape(2, quarter, columns)
        keep = lax.dynamic_index_in_dim(mine, low, 0, keepdims=False)
        give = lax.dynamic_index_in_dim(mine, 1 - low, 0, keepdims=False)
        total = (keep.astype(F32) + swap_with(give, "rep", 1).astype(F32)).astype(BF16)
        total = (total.astype(F32) + swap_with(total, "rep", 2).astype(F32)).astype(BF16)
        other = swap_with(total, "dp", 1)
        twin = jnp.stack([jnp.where(pair == 0, total, other), jnp.where(pair == 0, other, total)])
        twin_other = swap_with(twin, "rep", 1)
        first = jnp.where(low == 0, twin, twin_other)
        second = jnp.where(low == 0, twin_other, twin)
        return jnp.stack([first, second], axis=1).reshape(4 * quarter, columns).astype(F32)

    deltas_out = []
    outers_out = []
    weights_out = []
    for index in range(6):
        delta = sum_groups(local_deltas[index]) / groups
        outer_next = OUTER_MOMENTUM * outers[index] + delta
        deltas_out.append(delta)
        outers_out.append(outer_next)
        weights_out.append(masters[index] - OUTER_RATE * (delta + OUTER_MOMENTUM * outer_next))
    grads_out = tuple((gradient[None] for gradient in reduced))
    return (
        (cube(result) if result.ndim == 2 else result, in_grad)
        + grads_out
        + tuple(firsts_out)
        + tuple(seconds_out)
        + tuple(deltas_out)
        + tuple(outers_out)
        + tuple(weights_out)
    )


def solution(mesh):
    in_specs = (
        P(("rep", "dp", "fsdp"), None, None),
        P(("rep", "dp", "fsdp"), None, None),
        P(("rep", "dp", "fsdp")),
        P(("rep", "dp", "fsdp")),
        P(("rep", "dp", "fsdp")),
        P(),
        P(),
        P("fsdp", None),
        P("fsdp", None),
        P("fsdp", None),
        P("fsdp", None),
        P("fsdp", None),
        P("fsdp"),
        P("rep", "fsdp", None),
        P("rep", "fsdp", None),
        P("rep", "fsdp", None),
        P("rep", "fsdp", None),
        P("rep", "fsdp", None),
        P("rep", "fsdp"),
        P("rep", "fsdp", None),
        P("rep", "fsdp", None),
        P("rep", "fsdp", None),
        P("rep", "fsdp", None),
        P("rep", "fsdp", None),
        P("rep", "fsdp"),
        P("fsdp", None),
        P("fsdp", None),
        P("fsdp", None),
        P("fsdp", None),
        P("fsdp", None),
        P("fsdp"),
    )
    out_specs = (
        P(("rep", "dp", "fsdp"), None, None),
        P(("rep", "dp", "fsdp"), None, None),
        P("rep", "fsdp", None),
        P("rep", "fsdp", None),
        P("rep", "fsdp", None),
        P("rep", "fsdp", None),
        P("rep", "fsdp", None),
        P("rep", "fsdp"),
        P("rep", "fsdp", None),
        P("rep", "fsdp", None),
        P("rep", "fsdp", None),
        P("rep", "fsdp", None),
        P("rep", "fsdp", None),
        P("rep", "fsdp"),
        P("rep", "fsdp", None),
        P("rep", "fsdp", None),
        P("rep", "fsdp", None),
        P("rep", "fsdp", None),
        P("rep", "fsdp", None),
        P("rep", "fsdp"),
        P("fsdp", None),
        P("fsdp", None),
        P("fsdp", None),
        P("fsdp", None),
        P("fsdp", None),
        P("fsdp"),
        P("fsdp", None),
        P("fsdp", None),
        P("fsdp", None),
        P("fsdp", None),
        P("fsdp", None),
        P("fsdp"),
        P("fsdp", None),
        P("fsdp", None),
        P("fsdp", None),
        P("fsdp", None),
        P("fsdp", None),
        P("fsdp"),
    )
    return jax.shard_map(body, mesh=mesh, in_specs=in_specs, out_specs=out_specs, check_vma=False)
```

```python
import math

import jax
import jax.numpy as jnp
from jax import lax
from jax.experimental import pallas as pl
from jax.experimental.pallas import tpu as pltpu
from jax.sharding import PartitionSpec as P

D = 1152
HEADS = 16
FF = 4608


NORM_EPS = 1e-06
BETA_ONE = 0.9
BETA_TWO = 0.95
ADAM_EPS = 1e-08
WEIGHT_DECAY = 0.1
OUTER_RATE = 0.7
OUTER_MOMENTUM = 0.9
FEW = 8

F32 = jnp.float32
BF16 = jnp.bfloat16


def dot(left, right):
    return jnp.dot(left, right, preferred_element_type=F32)


def dot_nt(left, right):
    return lax.dot_general(left, right, (((1,), (1,)), ((), ())), preferred_element_type=F32)


def dot_tn(left, right):
    return lax.dot_general(left, right, (((0,), (0,)), ((), ())), preferred_element_type=F32)


def time_embed(steps, width):
    half = width // 2
    frequency = jnp.exp(-math.log(10000.0) * jnp.arange(half).astype(F32) / half)
    angles = steps.astype(F32)[:, None] * frequency[None, :]
    return jnp.concatenate([jnp.cos(angles), jnp.sin(angles)], axis=1)


def learning_rates(width, hidden):
    return (
        2.0 / math.sqrt(width),
        2.0 / math.sqrt(width),
        2.0 / math.sqrt(width // 32),
        2.0 / math.sqrt(width),
        2.0 / math.sqrt(hidden),
        0.3,
    )


def shift_by(value, axis, step):
    size = lax.axis_size(axis)
    return lax.ppermute(value, axis, [(i, (i + step) % size) for i in range(size)])


def swap_with(value, axis, bit):
    size = lax.axis_size(axis)
    return lax.ppermute(value, axis, [(i, i ^ bit) for i in range(size)])


def gather_line(value, axis):
    size = lax.axis_size(axis)
    if size > FEW:
        return lax.all_gather(value, axis, axis=0)
    place = lax.axis_index(axis)
    result = jnp.zeros((size,) + value.shape, value.dtype)
    for step in range(size):
        piece = value if step == 0 else shift_by(value, axis, step)
        result = lax.dynamic_update_index_in_dim(result, piece, (place - step) % size, 0)
    return result


def scatter_line(value, axis):
    size = lax.axis_size(axis)
    if size > FEW:
        return lax.psum_scatter(value, axis, scatter_dimension=0, tiled=False)
    place = lax.axis_index(axis)
    total = lax.dynamic_index_in_dim(value, place, 0, keepdims=False)
    for step in range(1, size):
        piece = lax.dynamic_index_in_dim(value, (place + step) % size, 0, keepdims=False)
        total = total + shift_by(piece, axis, step)
    return total


def moments(values):
    center = values - jnp.mean(values, axis=-1, keepdims=True)
    inverse = lax.rsqrt(jnp.mean(center * center, axis=-1, keepdims=True) + NORM_EPS)
    return center * inverse, inverse


def norm_back(normed, inverse, upstream):
    first = jnp.mean(upstream, axis=-1, keepdims=True)
    second = jnp.mean(upstream * normed, axis=-1, keepdims=True)
    return (upstream - first - normed * second) * inverse


def gelu_pair(h):
    c = math.sqrt(2.0 / math.pi)
    inner = c * (h + 0.044715 * h * h * h)
    t = jnp.tanh(inner)
    value = 0.5 * h * (1.0 + t)
    slope = 0.5 * (1.0 + t) + 0.5 * h * (1.0 - t * t) * c * (1.0 + 3.0 * 0.044715 * h * h)
    return value, slope


def head_window(head, head_dim):
    low = head * head_dim
    start = low // 128 * 128
    stop = -(-(low + head_dim) // 128) * 128
    return start, stop, low - start


def head_mask(shape, offset, head_dim):
    lane = lax.broadcasted_iota(jnp.int32, shape, 1)
    return (lane >= offset) & (lane < offset + head_dim)


def attention_forward_kernel(
    x_ref, cot_ref, mod_ref, bias_ref, weight_ref,
    attn_in_ref, packed_ref, attended_ref, log_ref, attn_ref, x1_ref, mlp_in_ref, d_mlp_ref, sums_ref,
    gather_ref,
):
    length, width = x_ref.shape
    head_dim = width // HEADS
    factor = 1.0 / math.sqrt(head_dim)
    residual = x_ref[...].astype(F32)
    normed, _ = moments(residual)
    attn_in_ref[...] = (normed * (1.0 + mod_ref[0, 1:2]) + mod_ref[0, 0:1]).astype(BF16)
    for unit in range(3):
        piece = dot(attn_in_ref[...], weight_ref[unit]) + bias_ref[unit : unit + 1]
        packed_ref[:, unit * width : (unit + 1) * width] = piece.astype(BF16)
    for head in range(HEADS):
        start, stop, offset = head_window(head, head_dim)
        mask = head_mask((length, stop - start), offset, head_dim)
        query = packed_ref[:, start:stop]
        query = jnp.where(mask, query, jnp.zeros_like(query))
        keys = packed_ref[:, width + start : width + stop]
        values = packed_ref[:, 2 * width + start : 2 * width + stop]
        scores = dot_nt(query, keys) * factor
        top = jnp.max(scores, axis=-1, keepdims=True)
        raised = jnp.exp(scores - top)
        summed = jnp.sum(raised, axis=-1, keepdims=True)
        probs = (raised * (1.0 / summed)).astype(BF16)
        log_ref[:, head : head + 1] = top + jnp.log(summed)
        out = dot(probs, values)
        if offset == 0:
            gather_ref[:, start:stop] = out
        else:
            gather_ref[:, start:stop] = jnp.where(mask, out, gather_ref[:, start:stop])
    attended_ref[...] = gather_ref[...].astype(BF16)
    attn = dot(attended_ref[...], weight_ref[3]) + bias_ref[3:4]
    attn_ref[...] = attn
    middle = residual + mod_ref[0, 2:3] * attn
    x1_ref[...] = middle
    normed_two, _ = moments(middle)
    mlp_in_ref[...] = (normed_two * (1.0 + mod_ref[0, 4:5]) + mod_ref[0, 3:4]).astype(BF16)
    d_mlp = (mod_ref[0, 5:6] * (cot_ref[...].astype(F32) * mod_ref[0, 6:7])).astype(BF16)
    d_mlp_ref[...] = d_mlp
    sums_ref[0, 0:1] = jnp.sum(d_mlp.astype(F32), axis=0, keepdims=True)


def rows_spec(length, width):
    return pl.BlockSpec((length, width), lambda i: (i, 0))


def whole_spec(shape):
    return pl.BlockSpec(shape, lambda i: (0,) * len(shape), pipeline_mode=pl.Buffered(1))


def lead_spec(rows, width):
    return pl.BlockSpec((1, rows, width), lambda i: (i, 0, 0))


def params(megabytes):
    return pltpu.CompilerParams(vmem_limit_bytes=megabytes << 20)


def attention_forward(x, cot, mod, bias, weights, slots, length, width):
    tokens = slots * length
    row = rows_spec(length, width)
    return pl.pallas_call(
        attention_forward_kernel,
        grid=(slots,),
        in_specs=[row, row, lead_spec(8, width), whole_spec((8, width)), whole_spec((4, width, width))],
        out_specs=[
            row, rows_spec(length, 3 * width), row, rows_spec(length, 128), row, row, row, row,
            lead_spec(8, width),
        ],
        out_shape=[
            jax.ShapeDtypeStruct((tokens, width), BF16),
            jax.ShapeDtypeStruct((tokens, 3 * width), BF16),
            jax.ShapeDtypeStruct((tokens, width), BF16),
            jax.ShapeDtypeStruct((tokens, 128), F32),
            jax.ShapeDtypeStruct((tokens, width), F32),
            jax.ShapeDtypeStruct((tokens, width), F32),
            jax.ShapeDtypeStruct((tokens, width), BF16),
            jax.ShapeDtypeStruct((tokens, width), BF16),
            jax.ShapeDtypeStruct((slots, 8, width), F32),
        ],
        scratch_shapes=[pltpu.VMEM((length, width), F32)],
        compiler_params=params(48),
        cost_estimate=pl.CostEstimate(
            flops=2 * tokens * width * width * 4, bytes_accessed=40 << 20, transcendentals=0
        ),
    )(x, cot, mod, bias, weights)


def hidden_kernel(mlp_in_ref, weight_ref, bias_ref, act_ref, slope_ref):
    step = 256

    def chunk(index, carry):
        here = pl.ds(pl.multiple_of(index * step, step), step)
        hidden = dot(mlp_in_ref[here, :], weight_ref[0]) + bias_ref[0:1]
        value, slope = gelu_pair(hidden)
        act_ref[here, :] = value.astype(BF16)
        slope_ref[here, :] = slope.astype(BF16)
        return carry

    lax.fori_loop(0, mlp_in_ref.shape[0] // step, chunk, 0)


def hidden_forward(mlp_in, weights, bias):
    tokens, width = mlp_in.shape
    units = weights.shape[0]
    column = pl.BlockSpec((tokens, width), lambda u: (0, u))
    return pl.pallas_call(
        hidden_kernel,
        grid=(units,),
        in_specs=[whole_spec((tokens, width)), lead_spec(width, width), pl.BlockSpec((1, width), lambda u: (0, u))],
        out_specs=[column, column],
        out_shape=[jax.ShapeDtypeStruct((tokens, units * width), BF16)] * 2,
        compiler_params=params(48),
        cost_estimate=pl.CostEstimate(
            flops=2 * tokens * width * width * units, bytes_accessed=26 << 20, transcendentals=0
        ),
    )(mlp_in, weights, bias)


def hidden_back_kernel(d_mlp_ref, weight_ref, slope_ref, d_hidden_ref, sums_ref):
    step = 256

    def chunk(index, carry):
        here = pl.ds(pl.multiple_of(index * step, step), step)
        d_hidden = dot_nt(d_mlp_ref[here, :], weight_ref[...]) * slope_ref[here, :].astype(F32)
        d_hidden = d_hidden.astype(BF16)
        d_hidden_ref[here, :] = d_hidden
        return carry + jnp.sum(d_hidden.astype(F32), axis=0, keepdims=True)

    zero = jnp.zeros((1, weight_ref.shape[0]), F32)
    sums_ref[0:1] = lax.fori_loop(0, d_mlp_ref.shape[0] // step, chunk, zero)


def hidden_back(d_mlp, weights, slope):
    tokens, width = d_mlp.shape
    units = weights.shape[0] // width
    column = pl.BlockSpec((tokens, width), lambda u: (0, u))
    return pl.pallas_call(
        hidden_back_kernel,
        grid=(units,),
        in_specs=[whole_spec((tokens, width)), rows_spec(width, width), column],
        out_specs=[column, pl.BlockSpec((8, width), lambda u: (0, u))],
        out_shape=[
            jax.ShapeDtypeStruct((tokens, units * width), BF16),
            jax.ShapeDtypeStruct((8, units * width), F32),
        ],
        compiler_params=params(48),
        cost_estimate=pl.CostEstimate(
            flops=2 * tokens * width * width * units, bytes_accessed=26 << 20, transcendentals=0
        ),
    )(d_mlp, weights, slope)


def mlp_rest_kernel(act_ref, two_ref, d_hidden_ref, one_ref, mlp_ref, d_in_ref):
    step = 256

    @pl.when(pl.program_id(0) == 0)
    def _():
        mlp_ref[...] = jnp.zeros_like(mlp_ref)
        d_in_ref[...] = jnp.zeros_like(d_in_ref)

    def chunk(index, carry):
        here = pl.ds(pl.multiple_of(index * step, step), step)
        mlp_ref[here, :] += dot(act_ref[here, :], two_ref[...])
        d_in_ref[here, :] += dot_nt(d_hidden_ref[here, :], one_ref[0])
        return carry

    lax.fori_loop(0, act_ref.shape[0] // step, chunk, 0)


def mlp_rest(act, two, d_hidden, one):
    tokens = act.shape[0]
    units, width = one.shape[:2]
    column = pl.BlockSpec((tokens, width), lambda u: (0, u))
    total = pl.BlockSpec((tokens, width), lambda u: (0, 0))
    return pl.pallas_call(
        mlp_rest_kernel,
        grid=(units,),
        in_specs=[column, rows_spec(width, width), column, lead_spec(width, width)],
        out_specs=[total, total],
        out_shape=[jax.ShapeDtypeStruct((tokens, width), F32)] * 2,
        compiler_params=params(48),
        cost_estimate=pl.CostEstimate(
            flops=4 * tokens * width * width * units, bytes_accessed=42 << 20, transcendentals=0
        ),
    )(act, two, d_hidden, one)


def middle_back_kernel(
    mlp_ref, bias_ref, d_in_ref, x1_ref, attn_ref, cot_ref, mod_ref, weight_ref,
    out_ref, d_mid_ref, d_attn_ref, d_att_ref, rows_ref,
):
    live = mod_ref[0, 6:7]
    gate_two = mod_ref[0, 5:6]
    upstream = cot_ref[...].astype(F32) * live
    middle = x1_ref[...]
    mlp = mlp_ref[...] + bias_ref[4:5]
    out_ref[...] = ((middle + gate_two * mlp) * live).astype(BF16)
    rows_ref[0, 5:6] = jnp.sum(upstream * mlp, axis=0, keepdims=True)
    normed, inverse = moments(middle)
    d_in = d_in_ref[...]
    rows_ref[0, 3:4] = jnp.sum(d_in, axis=0, keepdims=True)
    rows_ref[0, 4:5] = jnp.sum(d_in * normed, axis=0, keepdims=True)
    d_mid = upstream + norm_back(normed, inverse, d_in * (1.0 + mod_ref[0, 4:5]))
    d_mid_ref[...] = d_mid
    rows_ref[0, 2:3] = jnp.sum(d_mid * attn_ref[...], axis=0, keepdims=True)
    d_attn = (mod_ref[0, 2:3] * d_mid).astype(BF16)
    d_attn_ref[...] = d_attn
    rows_ref[0, 6:7] = jnp.sum(d_attn.astype(F32), axis=0, keepdims=True)
    d_att_ref[...] = dot_nt(d_attn_ref[...], weight_ref[0]).astype(BF16)


def middle_back(mlp, bias, d_in, x1, attn, cot, mod, weights, slots, length, width):
    tokens = slots * length
    row = rows_spec(length, width)
    proj = pl.BlockSpec((1, width, width), lambda i: (3, 0, 0), pipeline_mode=pl.Buffered(1))
    return pl.pallas_call(
        middle_back_kernel,
        grid=(slots,),
        in_specs=[row, whole_spec((8, width)), row, row, row, row, lead_spec(8, width), proj],
        out_specs=[row, row, row, row, lead_spec(8, width)],
        out_shape=[
            jax.ShapeDtypeStruct((tokens, width), BF16),
            jax.ShapeDtypeStruct((tokens, width), F32),
            jax.ShapeDtypeStruct((tokens, width), BF16),
            jax.ShapeDtypeStruct((tokens, width), BF16),
            jax.ShapeDtypeStruct((slots, 8, width), F32),
        ],
        compiler_params=params(48),
        cost_estimate=pl.CostEstimate(
            flops=2 * tokens * width * width, bytes_accessed=30 << 20, transcendentals=0
        ),
    )(mlp, bias, d_in, x1, attn, cot, mod, weights)


def attention_back_kernel(packed_ref, d_att_ref, log_ref, d_packed_ref, sums_ref, q_ref, k_ref, v_ref):
    length, width = d_att_ref.shape
    head_dim = width // HEADS
    factor = 1.0 / math.sqrt(head_dim)
    for head in range(HEADS):
        start, stop, offset = head_window(head, head_dim)
        mask = head_mask((length, stop - start), offset, head_dim)
        query = packed_ref[:, start:stop]
        query_one = jnp.where(mask, query, jnp.zeros_like(query))
        keys = packed_ref[:, width + start : width + stop]
        values = packed_ref[:, 2 * width + start : 2 * width + stop]
        d_att = d_att_ref[:, start:stop]
        d_att = jnp.where(mask, d_att, jnp.zeros_like(d_att))
        weights = jnp.exp(dot_nt(query_one, keys) * factor - log_ref[:, head : head + 1])
        d_probs = dot_nt(d_att, values)
        inner = jnp.sum(weights * d_probs, axis=-1, keepdims=True)
        d_scores = (weights * (d_probs - inner)).astype(BF16)
        probs = weights.astype(BF16)
        pieces = (
            (q_ref, dot(d_scores, keys) * factor),
            (k_ref, dot_tn(d_scores, query) * factor),
            (v_ref, dot_tn(probs, d_att)),
        )
        for ref, piece in pieces:
            if offset == 0:
                ref[:, start:stop] = piece
            else:
                ref[:, start:stop] = jnp.where(mask, piece, ref[:, start:stop])
    for unit, ref in enumerate((q_ref, k_ref, v_ref)):
        piece = ref[...].astype(BF16)
        d_packed_ref[:, unit * width : (unit + 1) * width] = piece
        sums_ref[0, unit : unit + 1] = jnp.sum(piece.astype(F32), axis=0, keepdims=True)


def attention_back(packed, d_att, log, slots, length, width):
    tokens = slots * length
    return pl.pallas_call(
        attention_back_kernel,
        grid=(slots,),
        in_specs=[rows_spec(length, 3 * width), rows_spec(length, width), rows_spec(length, 128)],
        out_specs=[rows_spec(length, 3 * width), lead_spec(8, width)],
        out_shape=[
            jax.ShapeDtypeStruct((tokens, 3 * width), BF16),
            jax.ShapeDtypeStruct((slots, 8, width), F32),
        ],
        scratch_shapes=[pltpu.VMEM((length, width), F32)] * 3,
        compiler_params=params(48),
        cost_estimate=pl.CostEstimate(
            flops=10 * tokens * length * 256 * HEADS, bytes_accessed=14 << 20, transcendentals=0
        ),
    )(packed, d_att, log)


def input_back_kernel(d_packed_ref, weight_ref, x_ref, d_mid_ref, mod_ref, grad_ref, rows_ref):
    width = x_ref.shape[1]
    d_in = dot_nt(d_packed_ref[:, :width], weight_ref[0])
    for unit in (1, 2):
        d_in = d_in + dot_nt(d_packed_ref[:, unit * width : (unit + 1) * width], weight_ref[unit])
    normed, inverse = moments(x_ref[...].astype(F32))
    rows_ref[0, 0:1] = jnp.sum(d_in, axis=0, keepdims=True)
    rows_ref[0, 1:2] = jnp.sum(d_in * normed, axis=0, keepdims=True)
    back = norm_back(normed, inverse, d_in * (1.0 + mod_ref[0, 1:2]))
    grad_ref[...] = (d_mid_ref[...] + back).astype(BF16)


def input_back(d_packed, weights, x, d_mid, mod, slots, length, width):
    tokens = slots * length
    row = rows_spec(length, width)
    return pl.pallas_call(
        input_back_kernel,
        grid=(slots,),
        in_specs=[
            rows_spec(length, 3 * width), whole_spec((3, width, width)), row, row, lead_spec(8, width),
        ],
        out_specs=[row, lead_spec(8, width)],
        out_shape=[
            jax.ShapeDtypeStruct((tokens, width), BF16),
            jax.ShapeDtypeStruct((slots, 8, width), F32),
        ],
        compiler_params=params(48),
        cost_estimate=pl.CostEstimate(
            flops=6 * tokens * width * width, bytes_accessed=20 << 20, transcendentals=0
        ),
    )(d_packed, weights, x, d_mid, mod)


def grad_kernel(left_ref, right_ref, grad_ref):
    step = grad_ref.shape[0] // 3

    def chunk(index, carry):
        here = pl.ds(pl.multiple_of(index * step, step), step)
        grad_ref[here, :] = dot_tn(left_ref[:, here], right_ref[...]).astype(BF16)
        return carry

    lax.fori_loop(0, 3, chunk, 0)


def grad_columns(left, right):
    tokens, rows = left.shape
    width = right.shape[1]
    return pl.pallas_call(
        grad_kernel,
        grid=(width // rows,),
        in_specs=[whole_spec((tokens, rows)), pl.BlockSpec((tokens, rows), lambda u: (0, u))],
        out_specs=pl.BlockSpec((rows, rows), lambda u: (0, u)),
        out_shape=jax.ShapeDtypeStruct((rows, width), BF16),
        compiler_params=params(48),
        cost_estimate=pl.CostEstimate(
            flops=2 * tokens * rows * width, bytes_accessed=2 * rows * width + 4 * tokens * width, transcendentals=0
        ),
    )(left, right)


def grad_rows(left, right):
    tokens, rows = left.shape
    width = right.shape[1]
    return pl.pallas_call(
        grad_kernel,
        grid=(rows // width,),
        in_specs=[pl.BlockSpec((tokens, width), lambda u: (0, u)), whole_spec((tokens, width))],
        out_specs=rows_spec(width, width),
        out_shape=jax.ShapeDtypeStruct((rows, width), BF16),
        compiler_params=params(48),
        cost_estimate=pl.CostEstimate(
            flops=2 * tokens * rows * width, bytes_accessed=2 * rows * width + 4 * tokens * rows, transcendentals=0
        ),
    )(left, right)


def after(*values):
    return lax.optimization_barrier(values)


def own_half(value, index):
    return lax.dynamic_index_in_dim(value, index, 1, keepdims=False)


def body(
    images,
    cotangent,
    counts,
    timesteps,
    labels,
    label_table,
    step_count,
    w_ada,
    w_qkv,
    w_proj,
    w_fc1,
    w_fc2,
    biases,
    first_ada,
    first_qkv,
    first_proj,
    first_fc1,
    first_fc2,
    first_bias,
    second_ada,
    second_qkv,
    second_proj,
    second_fc1,
    second_fc2,
    second_bias,
    outer_ada,
    outer_qkv,
    outer_proj,
    outer_fc1,
    outer_fc2,
    outer_bias,
):
    masters = (w_ada, w_qkv, w_proj, w_fc1, w_fc2, biases)
    firsts = (first_ada, first_qkv, first_proj, first_fc1, first_fc2, first_bias)
    seconds = (second_ada, second_qkv, second_proj, second_fc1, second_fc2, second_bias)
    outers = (outer_ada, outer_qkv, outer_proj, outer_fc1, outer_fc2, outer_bias)
    slots, length, width = images.shape
    tokens = slots * length
    rows = w_qkv.shape[0]
    rows_two = w_fc2.shape[0]
    lines = lax.axis_size("fsdp")
    groups = lax.axis_size("rep")
    rep = lax.axis_index("rep")
    pair = lax.axis_index("dp")
    line = lax.axis_index("fsdp")
    half = rows // 2
    everyone = ("rep", "fsdp", "dp")

    def rows_of(weight):
        return lax.dynamic_slice_in_dim(weight, pair * half, half, axis=0).astype(BF16)

    attention_cut = jnp.concatenate([rows_of(w_qkv), rows_of(w_proj)], axis=1)
    attention_cut = lax.dynamic_slice_in_dim(attention_cut, rep * width, width, axis=1)
    w_attn = lax.all_gather(attention_cut, everyone, axis=0, tiled=True).reshape(4, width, width)
    live = (jnp.arange(slots) < counts[0]).astype(F32)
    condition = time_embed(timesteps, D) + jnp.take(label_table, labels, axis=0).astype(F32)
    style = jax.nn.silu(condition).astype(BF16)
    one_cut = lax.dynamic_slice(w_fc1, (pair * half, rep * width), (half, width)).astype(BF16)
    one_cut, style = after(one_cut, style)
    w_one = lax.all_gather(one_cut, everyone, axis=0, tiled=True).reshape(FF // width, width, width)
    message = jnp.concatenate([style.reshape(-1), biases.astype(BF16)])
    heard = gather_line(message, "fsdp")
    bias_all = heard[:, slots * width :].reshape(-1).astype(F32)
    style_line = heard[:, : slots * width].reshape(lines * slots, width)
    style_cut = lax.dynamic_slice_in_dim(style_line, line * rows, rows, axis=1)
    mod_part = dot(style_cut, w_ada.astype(BF16))
    b_ada = bias_all[: 6 * width]
    modulation = scatter_line(mod_part.reshape(lines, slots, 6 * width), "fsdp") + b_ada
    eighth = rows_two // (2 * groups)
    two_cut = lax.dynamic_slice_in_dim(w_fc2, (rep * 2 + pair) * eighth, eighth, axis=0).astype(BF16)
    two_cut, modulation = after(two_cut, modulation)
    w_two = lax.all_gather(two_cut, ("fsdp", "rep", "dp"), axis=0, tiled=True)
    mod = jnp.concatenate(
        [
            modulation.reshape(slots, 6, width),
            jnp.broadcast_to(live[:, None, None], (slots, 2, width)),
        ],
        axis=1,
    )
    b_rest = bias_all[6 * width : 9 * width].reshape(3, width)
    bias = jnp.zeros((8, width), F32)
    bias = bias.at[0].set(b_rest[0]).at[2].set(b_rest[1]).at[3].set(b_rest[2])
    bias = bias.at[4].set(bias_all[9 * width + FF :])
    b_fc1 = bias_all[9 * width : 9 * width + FF].reshape(1, FF)
    x = images.reshape(tokens, width)
    cot = cotangent.reshape(tokens, width)

    attn_in, packed, attended, log_total, attn_out, middle, mlp_in, d_mlp, mlp_sums = attention_forward(
        x, cot, mod, bias, w_attn, slots, length, width
    )
    activated, slope = hidden_forward(mlp_in, w_one, b_fc1)
    grad_two = grad_rows(activated, d_mlp)

    def halves(gradient):
        return gradient.reshape(lines, 2, gradient.shape[0] // (2 * lines), gradient.shape[1])

    def line_sum(both):
        return lax.psum_scatter(
            both.reshape(-1, both.shape[-1]), "fsdp", scatter_dimension=0, tiled=True
        )

    def pair_sum(gradient, there):
        return (own_half(halves(gradient), pair).astype(F32) + there.astype(F32)).astype(BF16)

    grad_two, d_mlp = after(grad_two, d_mlp)
    two_line = line_sum(grad_two)
    d_hidden, hidden_sums = hidden_back(d_mlp, w_two, slope)
    grad_one = grad_columns(mlp_in, d_hidden)
    give_one = own_half(halves(grad_one), 1 - pair)
    give_one, d_hidden = after(give_one, d_hidden)
    there_one = swap_with(give_one, "dp", 1)
    mlp_out, d_mlp_in = mlp_rest(activated, w_two, d_hidden, w_one)
    result, d_middle, d_attn, d_attended, middle_rows = middle_back(
        mlp_out, bias, d_mlp_in, middle, attn_out, cot, mod, w_attn, slots, length, width
    )
    grad_proj = grad_columns(attended, d_attn)
    grad_proj, d_attended = after(grad_proj, d_attended)
    d_packed, packed_sums = attention_back(packed, d_attended, log_total, slots, length, width)
    grad_qkv = grad_columns(attn_in, d_packed)
    give_attn = jnp.concatenate(
        [own_half(halves(grad_qkv), 1 - pair), own_half(halves(grad_proj), 1 - pair)], axis=2
    )
    give_attn, d_packed = after(give_attn, d_packed)
    in_grad, input_rows = input_back(d_packed, w_attn, x, d_middle, mod, slots, length, width)

    two_line, there_one, give_attn, input_rows = after(two_line, there_one, give_attn, input_rows)
    there_attn = swap_with(give_attn, "dp", 1)
    one_both, input_rows = after(pair_sum(grad_one, there_one), input_rows)
    one_half = line_sum(one_both)
    d_modulation = jnp.concatenate([input_rows[:, :2], middle_rows[:, 2:6]], axis=1).astype(BF16)
    packed_total = jnp.sum(packed_sums, axis=0)
    bias_sums = jnp.concatenate(
        [
            packed_total[0],
            packed_total[2],
            jnp.sum(middle_rows[:, 6], axis=0),
            hidden_sums[0],
            jnp.sum(mlp_sums[:, 0], axis=0),
        ]
    ).astype(BF16)

    report = jnp.concatenate([style.reshape(-1), d_modulation.reshape(-1), bias_sums])
    report = jnp.stack([report, swap_with(report, "dp", 1)])
    reports = gather_line(report, "fsdp").reshape(2 * lines, -1)
    edge = slots * width
    style_group = reports[:, :edge].reshape(2 * lines * slots, width)
    mod_group = reports[:, edge : 7 * edge].reshape(2 * lines * slots, 6 * width)
    style_own = lax.dynamic_slice_in_dim(style_group, line * rows, rows, axis=1)
    grad_ada = dot_tn(style_own, mod_group)
    bias_group = jnp.concatenate(
        [
            jnp.sum(mod_group.astype(F32), axis=0),
            jnp.sum(reports[:, 7 * edge :].astype(F32), axis=0),
        ]
    )
    one_half, there_attn, grad_ada, bias_group = after(one_half, there_attn, grad_ada, bias_group)
    attn_both = jnp.concatenate(
        [own_half(halves(grad_qkv), pair), own_half(halves(grad_proj), pair)], axis=2
    )
    attn_both = (attn_both.astype(F32) + there_attn.astype(F32)).astype(BF16)
    attn_both, two_line, one_half, grad_ada = after(attn_both, two_line, one_half, grad_ada)
    attn_half = line_sum(attn_both)
    two_there = swap_with(two_line, "dp", 1)
    own_bias = biases.shape[0]
    grad_bias = lax.dynamic_slice_in_dim(bias_group, line * own_bias, own_bias, axis=0)

    def two_rows(own, other):
        first = jnp.where(pair == 0, own, other)
        second = jnp.where(pair == 0, other, own)
        return jnp.concatenate([first, second], axis=0)

    def both_halves(piece):
        return two_rows(piece, swap_with(piece, "dp", 1)).astype(F32)

    power = step_count[0].astype(F32)
    fix_one = 1.0 - jnp.power(BETA_ONE, power)
    fix_two = 1.0 - jnp.power(BETA_TWO, power)
    rates = learning_rates(D, FF)
    reduced = [None] * 6
    firsts_out = [None] * 6
    seconds_out = [None] * 6
    deltas_out = [None] * 6
    outers_out = [None] * 6
    weights_out = [None] * 6

    def moments_next(first, second, gradient):
        first_next = BETA_ONE * first + (1.0 - BETA_ONE) * gradient
        second_next = BETA_TWO * second + (1.0 - BETA_TWO) * gradient * gradient
        return first_next, second_next

    def local_delta(master, first, second, gradient, rate):
        first_next, second_next = moments_next(first, second, gradient)
        local = master - rate * (
            first_next / fix_one / (jnp.sqrt(second_next / fix_two) + ADAM_EPS)
            + WEIGHT_DECAY * master
        )
        return (master - local).astype(BF16)

    def sum_groups(mine):
        if mine.ndim == 1:
            total = (mine.astype(F32) + swap_with(mine, "rep", 1).astype(F32)).astype(BF16)
            return total.astype(F32) + swap_with(total, "rep", 2).astype(F32)
        quarter = mine.shape[0] // 2
        columns = mine.shape[1]
        low = rep % 2
        mine = mine.reshape(2, quarter, columns)
        keep = lax.dynamic_index_in_dim(mine, low, 0, keepdims=False)
        give = lax.dynamic_index_in_dim(mine, 1 - low, 0, keepdims=False)
        total = (keep.astype(F32) + swap_with(give, "rep", 1).astype(F32)).astype(BF16)
        total = (total.astype(F32) + swap_with(total, "rep", 2).astype(F32)).astype(BF16)
        twin = two_rows(total[None], swap_with(total, "dp", 1)[None])
        other = swap_with(twin, "rep", 1)
        first = jnp.where(low == 0, twin, other)
        second = jnp.where(low == 0, other, twin)
        return jnp.stack([first, second], axis=1).reshape(4 * quarter, columns).astype(F32)

    def own_rows(value):
        count = value.shape[0] // 2
        return lax.dynamic_slice_in_dim(value, pair * count, count, axis=0)

    def own_delta(index, own_gradient):
        master, first, second = masters[index], firsts[index][0], seconds[index][0]
        return local_delta(
            own_rows(master), own_rows(first), own_rows(second), own_gradient.astype(F32), rates[index]
        )

    def finish(index, gradient, summed):
        reduced[index] = gradient
        first_next, second_next = moments_next(firsts[index][0], seconds[index][0], gradient)
        firsts_out[index] = first_next[None]
        seconds_out[index] = second_next[None]
        delta = summed / groups
        outer_next = OUTER_MOMENTUM * outers[index] + delta
        deltas_out[index] = delta
        outers_out[index] = outer_next
        weights_out[index] = masters[index] - OUTER_RATE * (delta + OUTER_MOMENTUM * outer_next)

    finish(0, grad_ada, sum_groups(own_delta(0, own_rows(grad_ada))))
    bias_delta = local_delta(biases, first_bias[0], second_bias[0], grad_bias, rates[5])
    finish(5, grad_bias, sum_groups(bias_delta))
    finish(3, both_halves(one_half), sum_groups(own_delta(3, one_half)))
    grad_two_sum = two_line.astype(F32) + two_there.astype(F32)
    finish(4, grad_two_sum, sum_groups(own_delta(4, own_rows(grad_two_sum))))
    attn_half, weights_out[4], weights_out[3], weights_out[0] = after(
        attn_half, weights_out[4], weights_out[3], weights_out[0]
    )
    edge = 3 * width
    summed = sum_groups(
        jnp.concatenate([own_delta(1, attn_half[:, :edge]), own_delta(2, attn_half[:, edge:])], axis=1)
    )
    attn_full = both_halves(attn_half)
    finish(1, attn_full[:, :edge], summed[:, :edge])
    finish(2, attn_full[:, edge:], summed[:, edge:])
    grads_out = tuple((gradient[None] for gradient in reduced))
    return (
        (result.reshape(images.shape), in_grad.reshape(images.shape))
        + grads_out
        + tuple(firsts_out)
        + tuple(seconds_out)
        + tuple(deltas_out)
        + tuple(outers_out)
        + tuple(weights_out)
    )


def solution(mesh):
    in_specs = (
        P(("rep", "dp", "fsdp"), None, None),
        P(("rep", "dp", "fsdp"), None, None),
        P(("rep", "dp", "fsdp")),
        P(("rep", "dp", "fsdp")),
        P(("rep", "dp", "fsdp")),
        P(),
        P(),
        P("fsdp", None),
        P("fsdp", None),
        P("fsdp", None),
        P("fsdp", None),
        P("fsdp", None),
        P("fsdp"),
        P("rep", "fsdp", None),
        P("rep", "fsdp", None),
        P("rep", "fsdp", None),
        P("rep", "fsdp", None),
        P("rep", "fsdp", None),
        P("rep", "fsdp"),
        P("rep", "fsdp", None),
        P("rep", "fsdp", None),
        P("rep", "fsdp", None),
        P("rep", "fsdp", None),
        P("rep", "fsdp", None),
        P("rep", "fsdp"),
        P("fsdp", None),
        P("fsdp", None),
        P("fsdp", None),
        P("fsdp", None),
        P("fsdp", None),
        P("fsdp"),
    )
    out_specs = (
        P(("rep", "dp", "fsdp"), None, None),
        P(("rep", "dp", "fsdp"), None, None),
        P("rep", "fsdp", None),
        P("rep", "fsdp", None),
        P("rep", "fsdp", None),
        P("rep", "fsdp", None),
        P("rep", "fsdp", None),
        P("rep", "fsdp"),
        P("rep", "fsdp", None),
        P("rep", "fsdp", None),
        P("rep", "fsdp", None),
        P("rep", "fsdp", None),
        P("rep", "fsdp", None),
        P("rep", "fsdp"),
        P("rep", "fsdp", None),
        P("rep", "fsdp", None),
        P("rep", "fsdp", None),
        P("rep", "fsdp", None),
        P("rep", "fsdp", None),
        P("rep", "fsdp"),
        P("fsdp", None),
        P("fsdp", None),
        P("fsdp", None),
        P("fsdp", None),
        P("fsdp", None),
        P("fsdp"),
        P("fsdp", None),
        P("fsdp", None),
        P("fsdp", None),
        P("fsdp", None),
        P("fsdp", None),
        P("fsdp"),
        P("fsdp", None),
        P("fsdp", None),
        P("fsdp", None),
        P("fsdp", None),
        P("fsdp", None),
        P("fsdp"),
    )
    return jax.shard_map(body, mesh=mesh, in_specs=in_specs, out_specs=out_specs, check_vma=False)
```

```python
import math

import jax
import jax.numpy as jnp
from jax import lax
from jax.experimental import pallas as pl
from jax.experimental.pallas import tpu as pltpu
from jax.sharding import PartitionSpec as P

D = 1152
HEADS = 16
FF = 4608


NORM_EPS = 1e-06
BETA_ONE = 0.9
BETA_TWO = 0.95
ADAM_EPS = 1e-08
WEIGHT_DECAY = 0.1
OUTER_RATE = 0.7
OUTER_MOMENTUM = 0.9
FEW = 8

F32 = jnp.float32
BF16 = jnp.bfloat16


def dot(left, right):
    return jnp.dot(left, right, preferred_element_type=F32)


def dot_nt(left, right):
    return lax.dot_general(left, right, (((1,), (1,)), ((), ())), preferred_element_type=F32)


def dot_tn(left, right):
    return lax.dot_general(left, right, (((0,), (0,)), ((), ())), preferred_element_type=F32)


def time_embed(steps, width):
    half = width // 2
    frequency = jnp.exp(-math.log(10000.0) * jnp.arange(half).astype(F32) / half)
    angles = steps.astype(F32)[:, None] * frequency[None, :]
    return jnp.concatenate([jnp.cos(angles), jnp.sin(angles)], axis=1)


def learning_rates(width, hidden):
    return (
        2.0 / math.sqrt(width),
        2.0 / math.sqrt(width),
        2.0 / math.sqrt(width // 32),
        2.0 / math.sqrt(width),
        2.0 / math.sqrt(hidden),
        0.3,
    )


def shift_by(value, axis, step):
    size = lax.axis_size(axis)
    return lax.ppermute(value, axis, [(i, (i + step) % size) for i in range(size)])


def swap_with(value, axis, bit):
    size = lax.axis_size(axis)
    return lax.ppermute(value, axis, [(i, i ^ bit) for i in range(size)])


def gather_line(value, axis):
    size = lax.axis_size(axis)
    if size > FEW:
        return lax.all_gather(value, axis, axis=0)
    place = lax.axis_index(axis)
    result = jnp.zeros((size,) + value.shape, value.dtype)
    for step in range(size):
        piece = value if step == 0 else shift_by(value, axis, step)
        result = lax.dynamic_update_index_in_dim(result, piece, (place - step) % size, 0)
    return result


def scatter_line(value, axis):
    size = lax.axis_size(axis)
    if size > FEW:
        return lax.psum_scatter(value, axis, scatter_dimension=0, tiled=False)
    place = lax.axis_index(axis)
    total = lax.dynamic_index_in_dim(value, place, 0, keepdims=False)
    for step in range(1, size):
        piece = lax.dynamic_index_in_dim(value, (place + step) % size, 0, keepdims=False)
        total = total + shift_by(piece, axis, step)
    return total


def moments(values):
    center = values - jnp.mean(values, axis=-1, keepdims=True)
    inverse = lax.rsqrt(jnp.mean(center * center, axis=-1, keepdims=True) + NORM_EPS)
    return center * inverse, inverse


def norm_back(normed, inverse, upstream):
    first = jnp.mean(upstream, axis=-1, keepdims=True)
    second = jnp.mean(upstream * normed, axis=-1, keepdims=True)
    return (upstream - first - normed * second) * inverse


def gelu_pair(h):
    c = math.sqrt(2.0 / math.pi)
    inner = c * (h + 0.044715 * h * h * h)
    t = jnp.tanh(inner)
    value = 0.5 * h * (1.0 + t)
    slope = 0.5 * (1.0 + t) + 0.5 * h * (1.0 - t * t) * c * (1.0 + 3.0 * 0.044715 * h * h)
    return value, slope


def head_window(head, head_dim):
    low = head * head_dim
    start = low // 128 * 128
    stop = -(-(low + head_dim) // 128) * 128
    return start, stop, low - start


def head_mask(shape, offset, head_dim):
    lane = lax.broadcasted_iota(jnp.int32, shape, 1)
    return (lane >= offset) & (lane < offset + head_dim)


def attention_forward_kernel(
    x_ref, cot_ref, mod_ref, bias_ref, weight_ref,
    attn_in_ref, packed_ref, attended_ref, log_ref, attn_ref, x1_ref, mlp_in_ref, d_mlp_ref, sums_ref,
    gather_ref,
):
    length, width = x_ref.shape
    head_dim = width // HEADS
    factor = 1.0 / math.sqrt(head_dim)
    residual = x_ref[...].astype(F32)
    normed, _ = moments(residual)
    attn_in_ref[...] = (normed * (1.0 + mod_ref[0, 1:2]) + mod_ref[0, 0:1]).astype(BF16)
    for unit in range(3):
        piece = dot(attn_in_ref[...], weight_ref[unit]) + bias_ref[unit : unit + 1]
        packed_ref[:, unit * width : (unit + 1) * width] = piece.astype(BF16)
    for head in range(HEADS):
        start, stop, offset = head_window(head, head_dim)
        mask = head_mask((length, stop - start), offset, head_dim)
        query = packed_ref[:, start:stop]
        query = jnp.where(mask, query, jnp.zeros_like(query))
        keys = packed_ref[:, width + start : width + stop]
        values = packed_ref[:, 2 * width + start : 2 * width + stop]
        scores = dot_nt(query, keys) * factor
        top = jnp.max(scores, axis=-1, keepdims=True)
        raised = jnp.exp(scores - top)
        summed = jnp.sum(raised, axis=-1, keepdims=True)
        probs = (raised * (1.0 / summed)).astype(BF16)
        log_ref[:, head : head + 1] = top + jnp.log(summed)
        out = dot(probs, values)
        if offset == 0:
            gather_ref[:, start:stop] = out
        else:
            gather_ref[:, start:stop] = jnp.where(mask, out, gather_ref[:, start:stop])
    attended_ref[...] = gather_ref[...].astype(BF16)
    attn = dot(attended_ref[...], weight_ref[3]) + bias_ref[3:4]
    attn_ref[...] = attn
    middle = residual + mod_ref[0, 2:3] * attn
    x1_ref[...] = middle
    normed_two, _ = moments(middle)
    mlp_in_ref[...] = (normed_two * (1.0 + mod_ref[0, 4:5]) + mod_ref[0, 3:4]).astype(BF16)
    d_mlp = (mod_ref[0, 5:6] * (cot_ref[...].astype(F32) * mod_ref[0, 6:7])).astype(BF16)
    d_mlp_ref[...] = d_mlp
    sums_ref[0, 0:1] = jnp.sum(d_mlp.astype(F32), axis=0, keepdims=True)


def rows_spec(length, width):
    return pl.BlockSpec((length, width), lambda i: (i, 0))


def whole_spec(shape):
    return pl.BlockSpec(shape, lambda i: (0,) * len(shape), pipeline_mode=pl.Buffered(1))


def lead_spec(rows, width):
    return pl.BlockSpec((1, rows, width), lambda i: (i, 0, 0))


def params(megabytes):
    return pltpu.CompilerParams(vmem_limit_bytes=megabytes << 20)


def attention_forward(x, cot, mod, bias, weights, slots, length, width):
    tokens = slots * length
    row = rows_spec(length, width)
    return pl.pallas_call(
        attention_forward_kernel,
        grid=(slots,),
        in_specs=[row, row, lead_spec(8, width), whole_spec((8, width)), whole_spec((4, width, width))],
        out_specs=[
            row, rows_spec(length, 3 * width), row, rows_spec(length, 128), row, row, row, row,
            lead_spec(8, width),
        ],
        out_shape=[
            jax.ShapeDtypeStruct((tokens, width), BF16),
            jax.ShapeDtypeStruct((tokens, 3 * width), BF16),
            jax.ShapeDtypeStruct((tokens, width), BF16),
            jax.ShapeDtypeStruct((tokens, 128), F32),
            jax.ShapeDtypeStruct((tokens, width), F32),
            jax.ShapeDtypeStruct((tokens, width), F32),
            jax.ShapeDtypeStruct((tokens, width), BF16),
            jax.ShapeDtypeStruct((tokens, width), BF16),
            jax.ShapeDtypeStruct((slots, 8, width), F32),
        ],
        scratch_shapes=[pltpu.VMEM((length, width), F32)],
        compiler_params=params(48),
        cost_estimate=pl.CostEstimate(
            flops=2 * tokens * width * width * 4, bytes_accessed=40 << 20, transcendentals=0
        ),
    )(x, cot, mod, bias, weights)


def hidden_kernel(mlp_in_ref, weight_ref, bias_ref, act_ref, slope_ref):
    step = 256

    def chunk(index, carry):
        here = pl.ds(pl.multiple_of(index * step, step), step)
        hidden = dot(mlp_in_ref[here, :], weight_ref[0]) + bias_ref[0:1]
        value, slope = gelu_pair(hidden)
        act_ref[here, :] = value.astype(BF16)
        slope_ref[here, :] = slope.astype(BF16)
        return carry

    lax.fori_loop(0, mlp_in_ref.shape[0] // step, chunk, 0)


def hidden_forward(mlp_in, weights, bias):
    tokens, width = mlp_in.shape
    units = weights.shape[0]
    column = pl.BlockSpec((tokens, width), lambda u: (0, u))
    return pl.pallas_call(
        hidden_kernel,
        grid=(units,),
        in_specs=[whole_spec((tokens, width)), lead_spec(width, width), pl.BlockSpec((1, width), lambda u: (0, u))],
        out_specs=[column, column],
        out_shape=[jax.ShapeDtypeStruct((tokens, units * width), BF16)] * 2,
        compiler_params=params(48),
        cost_estimate=pl.CostEstimate(
            flops=2 * tokens * width * width * units, bytes_accessed=26 << 20, transcendentals=0
        ),
    )(mlp_in, weights, bias)


def hidden_back_kernel(d_mlp_ref, weight_ref, slope_ref, d_hidden_ref, sums_ref):
    step = 256

    def chunk(index, carry):
        here = pl.ds(pl.multiple_of(index * step, step), step)
        d_hidden = dot_nt(d_mlp_ref[here, :], weight_ref[...]) * slope_ref[here, :].astype(F32)
        d_hidden = d_hidden.astype(BF16)
        d_hidden_ref[here, :] = d_hidden
        return carry + jnp.sum(d_hidden.astype(F32), axis=0, keepdims=True)

    zero = jnp.zeros((1, weight_ref.shape[0]), F32)
    sums_ref[0:1] = lax.fori_loop(0, d_mlp_ref.shape[0] // step, chunk, zero)


def hidden_back(d_mlp, weights, slope):
    tokens, width = d_mlp.shape
    units = weights.shape[0] // width
    column = pl.BlockSpec((tokens, width), lambda u: (0, u))
    return pl.pallas_call(
        hidden_back_kernel,
        grid=(units,),
        in_specs=[whole_spec((tokens, width)), rows_spec(width, width), column],
        out_specs=[column, pl.BlockSpec((8, width), lambda u: (0, u))],
        out_shape=[
            jax.ShapeDtypeStruct((tokens, units * width), BF16),
            jax.ShapeDtypeStruct((8, units * width), F32),
        ],
        compiler_params=params(48),
        cost_estimate=pl.CostEstimate(
            flops=2 * tokens * width * width * units, bytes_accessed=26 << 20, transcendentals=0
        ),
    )(d_mlp, weights, slope)


def mlp_rest_kernel(act_ref, two_ref, d_hidden_ref, one_ref, mlp_ref, d_in_ref):
    step = 256

    @pl.when(pl.program_id(0) == 0)
    def _():
        mlp_ref[...] = jnp.zeros_like(mlp_ref)
        d_in_ref[...] = jnp.zeros_like(d_in_ref)

    def chunk(index, carry):
        here = pl.ds(pl.multiple_of(index * step, step), step)
        mlp_ref[here, :] += dot(act_ref[here, :], two_ref[...])
        d_in_ref[here, :] += dot_nt(d_hidden_ref[here, :], one_ref[0])
        return carry

    lax.fori_loop(0, act_ref.shape[0] // step, chunk, 0)


def mlp_rest(act, two, d_hidden, one):
    tokens = act.shape[0]
    units, width = one.shape[:2]
    column = pl.BlockSpec((tokens, width), lambda u: (0, u))
    total = pl.BlockSpec((tokens, width), lambda u: (0, 0))
    return pl.pallas_call(
        mlp_rest_kernel,
        grid=(units,),
        in_specs=[column, rows_spec(width, width), column, lead_spec(width, width)],
        out_specs=[total, total],
        out_shape=[jax.ShapeDtypeStruct((tokens, width), F32)] * 2,
        compiler_params=params(48),
        cost_estimate=pl.CostEstimate(
            flops=4 * tokens * width * width * units, bytes_accessed=42 << 20, transcendentals=0
        ),
    )(act, two, d_hidden, one)


def middle_back_kernel(
    mlp_ref, bias_ref, d_in_ref, x1_ref, attn_ref, cot_ref, mod_ref, weight_ref,
    out_ref, d_mid_ref, d_attn_ref, d_att_ref, rows_ref,
):
    live = mod_ref[0, 6:7]
    gate_two = mod_ref[0, 5:6]
    upstream = cot_ref[...].astype(F32) * live
    middle = x1_ref[...]
    mlp = mlp_ref[...] + bias_ref[4:5]
    out_ref[...] = ((middle + gate_two * mlp) * live).astype(BF16)
    rows_ref[0, 5:6] = jnp.sum(upstream * mlp, axis=0, keepdims=True)
    normed, inverse = moments(middle)
    d_in = d_in_ref[...]
    rows_ref[0, 3:4] = jnp.sum(d_in, axis=0, keepdims=True)
    rows_ref[0, 4:5] = jnp.sum(d_in * normed, axis=0, keepdims=True)
    d_mid = upstream + norm_back(normed, inverse, d_in * (1.0 + mod_ref[0, 4:5]))
    d_mid_ref[...] = d_mid
    rows_ref[0, 2:3] = jnp.sum(d_mid * attn_ref[...], axis=0, keepdims=True)
    d_attn = (mod_ref[0, 2:3] * d_mid).astype(BF16)
    d_attn_ref[...] = d_attn
    rows_ref[0, 6:7] = jnp.sum(d_attn.astype(F32), axis=0, keepdims=True)
    d_att_ref[...] = dot_nt(d_attn_ref[...], weight_ref[0]).astype(BF16)


def middle_back(mlp, bias, d_in, x1, attn, cot, mod, weights, slots, length, width):
    tokens = slots * length
    row = rows_spec(length, width)
    proj = pl.BlockSpec((1, width, width), lambda i: (3, 0, 0), pipeline_mode=pl.Buffered(1))
    return pl.pallas_call(
        middle_back_kernel,
        grid=(slots,),
        in_specs=[row, whole_spec((8, width)), row, row, row, row, lead_spec(8, width), proj],
        out_specs=[row, row, row, row, lead_spec(8, width)],
        out_shape=[
            jax.ShapeDtypeStruct((tokens, width), BF16),
            jax.ShapeDtypeStruct((tokens, width), F32),
            jax.ShapeDtypeStruct((tokens, width), BF16),
            jax.ShapeDtypeStruct((tokens, width), BF16),
            jax.ShapeDtypeStruct((slots, 8, width), F32),
        ],
        compiler_params=params(48),
        cost_estimate=pl.CostEstimate(
            flops=2 * tokens * width * width, bytes_accessed=30 << 20, transcendentals=0
        ),
    )(mlp, bias, d_in, x1, attn, cot, mod, weights)


def attention_back_kernel(packed_ref, d_att_ref, log_ref, d_packed_ref, sums_ref, q_ref, k_ref, v_ref):
    length, width = d_att_ref.shape
    head_dim = width // HEADS
    factor = 1.0 / math.sqrt(head_dim)
    for head in range(HEADS):
        start, stop, offset = head_window(head, head_dim)
        mask = head_mask((length, stop - start), offset, head_dim)
        query = packed_ref[:, start:stop]
        query_one = jnp.where(mask, query, jnp.zeros_like(query))
        keys = packed_ref[:, width + start : width + stop]
        values = packed_ref[:, 2 * width + start : 2 * width + stop]
        d_att = d_att_ref[:, start:stop]
        d_att = jnp.where(mask, d_att, jnp.zeros_like(d_att))
        weights = jnp.exp(dot_nt(query_one, keys) * factor - log_ref[:, head : head + 1])
        d_probs = dot_nt(d_att, values)
        inner = jnp.sum(weights * d_probs, axis=-1, keepdims=True)
        d_scores = (weights * (d_probs - inner)).astype(BF16)
        probs = weights.astype(BF16)
        pieces = (
            (q_ref, dot(d_scores, keys) * factor),
            (k_ref, dot_tn(d_scores, query) * factor),
            (v_ref, dot_tn(probs, d_att)),
        )
        for ref, piece in pieces:
            if offset == 0:
                ref[:, start:stop] = piece
            else:
                ref[:, start:stop] = jnp.where(mask, piece, ref[:, start:stop])
    for unit, ref in enumerate((q_ref, k_ref, v_ref)):
        piece = ref[...].astype(BF16)
        d_packed_ref[:, unit * width : (unit + 1) * width] = piece
        sums_ref[0, unit : unit + 1] = jnp.sum(piece.astype(F32), axis=0, keepdims=True)


def attention_back(packed, d_att, log, slots, length, width):
    tokens = slots * length
    return pl.pallas_call(
        attention_back_kernel,
        grid=(slots,),
        in_specs=[rows_spec(length, 3 * width), rows_spec(length, width), rows_spec(length, 128)],
        out_specs=[rows_spec(length, 3 * width), lead_spec(8, width)],
        out_shape=[
            jax.ShapeDtypeStruct((tokens, 3 * width), BF16),
            jax.ShapeDtypeStruct((slots, 8, width), F32),
        ],
        scratch_shapes=[pltpu.VMEM((length, width), F32)] * 3,
        compiler_params=params(48),
        cost_estimate=pl.CostEstimate(
            flops=10 * tokens * length * 256 * HEADS, bytes_accessed=14 << 20, transcendentals=0
        ),
    )(packed, d_att, log)


def input_back_kernel(d_packed_ref, weight_ref, x_ref, d_mid_ref, mod_ref, grad_ref, rows_ref):
    width = x_ref.shape[1]
    d_in = dot_nt(d_packed_ref[:, :width], weight_ref[0])
    for unit in (1, 2):
        d_in = d_in + dot_nt(d_packed_ref[:, unit * width : (unit + 1) * width], weight_ref[unit])
    normed, inverse = moments(x_ref[...].astype(F32))
    rows_ref[0, 0:1] = jnp.sum(d_in, axis=0, keepdims=True)
    rows_ref[0, 1:2] = jnp.sum(d_in * normed, axis=0, keepdims=True)
    back = norm_back(normed, inverse, d_in * (1.0 + mod_ref[0, 1:2]))
    grad_ref[...] = (d_mid_ref[...] + back).astype(BF16)


def input_back(d_packed, weights, x, d_mid, mod, slots, length, width):
    tokens = slots * length
    row = rows_spec(length, width)
    return pl.pallas_call(
        input_back_kernel,
        grid=(slots,),
        in_specs=[
            rows_spec(length, 3 * width), whole_spec((3, width, width)), row, row, lead_spec(8, width),
        ],
        out_specs=[row, lead_spec(8, width)],
        out_shape=[
            jax.ShapeDtypeStruct((tokens, width), BF16),
            jax.ShapeDtypeStruct((slots, 8, width), F32),
        ],
        compiler_params=params(48),
        cost_estimate=pl.CostEstimate(
            flops=6 * tokens * width * width, bytes_accessed=20 << 20, transcendentals=0
        ),
    )(d_packed, weights, x, d_mid, mod)


def grad_kernel(left_ref, right_ref, grad_ref):
    step = grad_ref.shape[0] // 3

    def chunk(index, carry):
        here = pl.ds(pl.multiple_of(index * step, step), step)
        grad_ref[here, :] = dot_tn(left_ref[:, here], right_ref[...]).astype(BF16)
        return carry

    lax.fori_loop(0, 3, chunk, 0)


def grad_columns(left, right):
    tokens, rows = left.shape
    width = right.shape[1]
    return pl.pallas_call(
        grad_kernel,
        grid=(width // rows,),
        in_specs=[whole_spec((tokens, rows)), pl.BlockSpec((tokens, rows), lambda u: (0, u))],
        out_specs=pl.BlockSpec((rows, rows), lambda u: (0, u)),
        out_shape=jax.ShapeDtypeStruct((rows, width), BF16),
        compiler_params=params(48),
        cost_estimate=pl.CostEstimate(
            flops=2 * tokens * rows * width, bytes_accessed=2 * rows * width + 4 * tokens * width, transcendentals=0
        ),
    )(left, right)


def grad_rows(left, right):
    tokens, rows = left.shape
    width = right.shape[1]
    return pl.pallas_call(
        grad_kernel,
        grid=(rows // width,),
        in_specs=[pl.BlockSpec((tokens, width), lambda u: (0, u)), whole_spec((tokens, width))],
        out_specs=rows_spec(width, width),
        out_shape=jax.ShapeDtypeStruct((rows, width), BF16),
        compiler_params=params(48),
        cost_estimate=pl.CostEstimate(
            flops=2 * tokens * rows * width, bytes_accessed=2 * rows * width + 4 * tokens * rows, transcendentals=0
        ),
    )(left, right)


def after(*values):
    return lax.optimization_barrier(values)


def place_kernel(order_ref, *refs):
    sources, target, held, came, left = refs[:-4], refs[-4], refs[-3], refs[-2], refs[-1]
    inward, outward = [], []
    for which, source in enumerate(sources):
        for block in range(source.shape[0]):
            index = which * source.shape[0] + block
            inward.append(pltpu.make_async_copy(source.at[block], held.at[index], came.at[index]))
            outward.append(
                pltpu.make_async_copy(held.at[index], target.at[order_ref[index]], left.at[index])
            )
    for copy in inward:
        copy.start()
    for first, second in zip(inward, outward):
        first.wait()
        second.start()
    for copy in outward:
        copy.wait()


def place_blocks(order, sources):
    blocks = sum(source.shape[0] for source in sources)
    shape = (blocks,) + sources[0].shape[1:]
    return pl.pallas_call(
        place_kernel,
        grid_spec=pltpu.PrefetchScalarGridSpec(
            num_scalar_prefetch=1,
            grid=(1,),
            in_specs=[pl.BlockSpec(memory_space=pl.ANY)] * len(sources),
            out_specs=pl.BlockSpec(memory_space=pl.ANY),
            scratch_shapes=[
                pltpu.VMEM(shape, sources[0].dtype),
                pltpu.SemaphoreType.DMA((blocks,)),
                pltpu.SemaphoreType.DMA((blocks,)),
            ],
        ),
        out_shape=jax.ShapeDtypeStruct(shape, sources[0].dtype),
        compiler_params=params(48),
        cost_estimate=pl.CostEstimate(
            flops=0, bytes_accessed=4 * blocks * shape[1] * shape[2], transcendentals=0
        ),
    )(order, *sources)


def hops_line(piece):
    near = jnp.stack([piece, shift_by(piece, "fsdp", 1)])
    far = jnp.stack([shift_by(piece, "fsdp", 2), shift_by(piece, "fsdp", 3)])
    return near, far


def hops_side(near, far):
    near = jnp.concatenate([near, swap_with(near, "rep", 2)])
    far = jnp.concatenate([far, swap_with(far, "dp", 1)])
    return near, far


def hops_other(near, far):
    return near, far, swap_with(near, "dp", 1), swap_with(far, "rep", 2)


def hops_core(sources):
    return tuple(sources) + tuple(swap_with(source, "rep", 1) for source in sources)


def hops_place(sources, weigh):
    size = lax.axis_size("fsdp")
    rep, pair, line = lax.axis_index("rep"), lax.axis_index("dp"), lax.axis_index("fsdp")
    order = []
    for core in (0, 1):
        for kind in range(4):
            for block in range(4):
                hop, step = block // 2, block % 2
                if kind in (0, 2):
                    flip_rep, flip_pair, back = hop, kind // 2, step
                else:
                    flip_rep, flip_pair, back = kind // 2, hop, 2 + step
                place = lax.rem(line - back + size, size) * weigh[0]
                place = place + (rep ^ (2 * flip_rep + core)) * weigh[1] + (pair ^ flip_pair) * weigh[2]
                order.append(place)
    return place_blocks(jnp.stack(order).astype(jnp.int32), sources)


def own_half(value, index):
    return lax.dynamic_index_in_dim(value, index, 1, keepdims=False)


def body(
    images,
    cotangent,
    counts,
    timesteps,
    labels,
    label_table,
    step_count,
    w_ada,
    w_qkv,
    w_proj,
    w_fc1,
    w_fc2,
    biases,
    first_ada,
    first_qkv,
    first_proj,
    first_fc1,
    first_fc2,
    first_bias,
    second_ada,
    second_qkv,
    second_proj,
    second_fc1,
    second_fc2,
    second_bias,
    outer_ada,
    outer_qkv,
    outer_proj,
    outer_fc1,
    outer_fc2,
    outer_bias,
):
    masters = (w_ada, w_qkv, w_proj, w_fc1, w_fc2, biases)
    firsts = (first_ada, first_qkv, first_proj, first_fc1, first_fc2, first_bias)
    seconds = (second_ada, second_qkv, second_proj, second_fc1, second_fc2, second_bias)
    outers = (outer_ada, outer_qkv, outer_proj, outer_fc1, outer_fc2, outer_bias)
    slots, length, width = images.shape
    tokens = slots * length
    rows = w_qkv.shape[0]
    rows_two = w_fc2.shape[0]
    lines = lax.axis_size("fsdp")
    groups = lax.axis_size("rep")
    rep = lax.axis_index("rep")
    pair = lax.axis_index("dp")
    line = lax.axis_index("fsdp")
    half = rows // 2
    everyone = ("rep", "fsdp", "dp")

    def rows_of(weight):
        return lax.dynamic_slice_in_dim(weight, pair * half, half, axis=0).astype(BF16)

    attention_cut = jnp.concatenate([rows_of(w_qkv), rows_of(w_proj)], axis=1)
    attention_cut = lax.dynamic_slice_in_dim(attention_cut, rep * width, width, axis=1)
    w_attn = lax.all_gather(attention_cut, everyone, axis=0, tiled=True).reshape(4, width, width)
    live = (jnp.arange(slots) < counts[0]).astype(F32)
    condition = time_embed(timesteps, D) + jnp.take(label_table, labels, axis=0).astype(F32)
    style = jax.nn.silu(condition).astype(BF16)
    one_cut = lax.dynamic_slice(w_fc1, (pair * half, rep * width), (half, width)).astype(BF16)
    one_cut, style = after(one_cut, style)
    hops = lines == 4 and groups == 4
    if hops:
        w_one = hops_place(hops_core(hops_other(*hops_side(*hops_line(one_cut)))), (2, 8, 1))
    else:
        w_one = lax.all_gather(one_cut, everyone, axis=0, tiled=True)
    w_one = w_one.reshape(FF // width, width, width)
    message = jnp.concatenate([style.reshape(-1), biases.astype(BF16)])
    heard = gather_line(message, "fsdp")
    bias_all = heard[:, slots * width :].reshape(-1).astype(F32)
    style_line = heard[:, : slots * width].reshape(lines * slots, width)
    style_cut = lax.dynamic_slice_in_dim(style_line, line * rows, rows, axis=1)
    mod_part = dot(style_cut, w_ada.astype(BF16))
    b_ada = bias_all[: 6 * width]
    modulation = scatter_line(mod_part.reshape(lines, slots, 6 * width), "fsdp") + b_ada
    eighth = rows_two // (2 * groups)
    two_cut = lax.dynamic_slice_in_dim(w_fc2, (rep * 2 + pair) * eighth, eighth, axis=0).astype(BF16)
    two_cut, modulation = after(two_cut, modulation)
    if hops:
        parts = hops_line(two_cut)
    else:
        w_two = lax.all_gather(two_cut, ("fsdp", "rep", "dp"), axis=0, tiled=True)
    mod = jnp.concatenate(
        [
            modulation.reshape(slots, 6, width),
            jnp.broadcast_to(live[:, None, None], (slots, 2, width)),
        ],
        axis=1,
    )
    b_rest = bias_all[6 * width : 9 * width].reshape(3, width)
    bias = jnp.zeros((8, width), F32)
    bias = bias.at[0].set(b_rest[0]).at[2].set(b_rest[1]).at[3].set(b_rest[2])
    bias = bias.at[4].set(bias_all[9 * width + FF :])
    b_fc1 = bias_all[9 * width : 9 * width + FF].reshape(1, FF)
    x = images.reshape(tokens, width)
    cot = cotangent.reshape(tokens, width)

    if hops:
        *parts, mod = after(*parts, mod)
        parts = hops_side(*parts)
    attn_in, packed, attended, log_total, attn_out, middle, mlp_in, d_mlp, mlp_sums = attention_forward(
        x, cot, mod, bias, w_attn, slots, length, width
    )
    if hops:
        *parts, mlp_in = after(*parts, mlp_in)
        parts = hops_other(*parts)
    activated, slope = hidden_forward(mlp_in, w_one, b_fc1)
    if hops:
        *parts, activated = after(*parts, activated)
        parts = hops_core(parts)
    grad_two = grad_rows(activated, d_mlp)

    def halves(gradient):
        return gradient.reshape(lines, 2, gradient.shape[0] // (2 * lines), gradient.shape[1])

    def line_sum(both):
        return lax.psum_scatter(
            both.reshape(-1, both.shape[-1]), "fsdp", scatter_dimension=0, tiled=True
        )

    def pair_sum(gradient, there):
        return (own_half(halves(gradient), pair).astype(F32) + there.astype(F32)).astype(BF16)

    if hops:
        w_two = hops_place(parts, (8, 2, 1)).reshape(FF, width)
    grad_two, d_mlp = after(grad_two, d_mlp)
    two_half = lax.psum_scatter(grad_two, ("fsdp", "dp"), scatter_dimension=0, tiled=True)
    d_hidden, hidden_sums = hidden_back(d_mlp, w_two, slope)
    grad_one = grad_columns(mlp_in, d_hidden)
    give_one = own_half(halves(grad_one), 1 - pair)
    give_one, d_hidden = after(give_one, d_hidden)
    there_one = swap_with(give_one, "dp", 1)
    mlp_out, d_mlp_in = mlp_rest(activated, w_two, d_hidden, w_one)
    result, d_middle, d_attn, d_attended, middle_rows = middle_back(
        mlp_out, bias, d_mlp_in, middle, attn_out, cot, mod, w_attn, slots, length, width
    )
    grad_proj = grad_columns(attended, d_attn)
    grad_proj, d_attended = after(grad_proj, d_attended)
    d_packed, packed_sums = attention_back(packed, d_attended, log_total, slots, length, width)
    grad_qkv = grad_columns(attn_in, d_packed)
    give_attn = jnp.concatenate(
        [own_half(halves(grad_qkv), 1 - pair), own_half(halves(grad_proj), 1 - pair)], axis=2
    )
    give_attn, d_packed = after(give_attn, d_packed)
    in_grad, input_rows = input_back(d_packed, w_attn, x, d_middle, mod, slots, length, width)

    two_half, there_one, give_attn, input_rows = after(two_half, there_one, give_attn, input_rows)
    there_attn = swap_with(give_attn, "dp", 1)
    one_both, input_rows = after(pair_sum(grad_one, there_one), input_rows)
    one_half = line_sum(one_both)
    d_modulation = jnp.concatenate([input_rows[:, :2], middle_rows[:, 2:6]], axis=1).astype(BF16)
    packed_total = jnp.sum(packed_sums, axis=0)
    bias_sums = jnp.concatenate(
        [
            packed_total[0],
            packed_total[2],
            jnp.sum(middle_rows[:, 6], axis=0),
            hidden_sums[0],
            jnp.sum(mlp_sums[:, 0], axis=0),
        ]
    ).astype(BF16)

    report = jnp.concatenate([style.reshape(-1), d_modulation.reshape(-1), bias_sums])
    report = jnp.stack([report, swap_with(report, "dp", 1)])
    reports = gather_line(report, "fsdp").reshape(2 * lines, -1)
    edge = slots * width
    style_group = reports[:, :edge].reshape(2 * lines * slots, width)
    mod_group = reports[:, edge : 7 * edge].reshape(2 * lines * slots, 6 * width)
    style_own = lax.dynamic_slice_in_dim(style_group, line * rows, rows, axis=1)
    grad_ada = dot_tn(style_own, mod_group)
    bias_group = jnp.concatenate(
        [
            jnp.sum(mod_group.astype(F32), axis=0),
            jnp.sum(reports[:, 7 * edge :].astype(F32), axis=0),
        ]
    )
    own_bias = biases.shape[0]
    grad_bias = lax.dynamic_slice_in_dim(bias_group, line * own_bias, own_bias, axis=0)

    def two_rows(own, other):
        first = jnp.where(pair == 0, own, other)
        second = jnp.where(pair == 0, other, own)
        return jnp.concatenate([first, second], axis=0)

    def both_halves(piece):
        return two_rows(piece, swap_with(piece, "dp", 1)).astype(F32)

    power = step_count[0].astype(F32)
    fix_one = 1.0 - jnp.power(BETA_ONE, power)
    fix_two = 1.0 - jnp.power(BETA_TWO, power)
    rates = learning_rates(D, FF)
    reduced = [None] * 6
    firsts_out = [None] * 6
    seconds_out = [None] * 6
    deltas_out = [None] * 6
    outers_out = [None] * 6
    weights_out = [None] * 6

    def moments_next(first, second, gradient):
        first_next = BETA_ONE * first + (1.0 - BETA_ONE) * gradient
        second_next = BETA_TWO * second + (1.0 - BETA_TWO) * gradient * gradient
        return first_next, second_next

    def local_delta(master, first, second, gradient, rate):
        first_next, second_next = moments_next(first, second, gradient)
        local = master - rate * (
            first_next / fix_one / (jnp.sqrt(second_next / fix_two) + ADAM_EPS)
            + WEIGHT_DECAY * master
        )
        return (master - local).astype(BF16)

    low = rep % 2

    def sum_rep(mine):
        if mine.ndim == 1:
            total = (mine.astype(F32) + swap_with(mine, "rep", 1).astype(F32)).astype(BF16)
            return total.astype(F32) + swap_with(total, "rep", 2).astype(F32)
        mine = mine.reshape(2, mine.shape[0] // 2, mine.shape[1])
        keep = lax.dynamic_index_in_dim(mine, low, 0, keepdims=False)
        give = lax.dynamic_index_in_dim(mine, 1 - low, 0, keepdims=False)
        total = (keep.astype(F32) + swap_with(give, "rep", 1).astype(F32)).astype(BF16)
        return (total.astype(F32) + swap_with(total, "rep", 2).astype(F32)).astype(BF16)

    def join_cores(total):
        other = swap_with(total, "rep", 1)
        first = jnp.where(low == 0, total, other)
        second = jnp.where(low == 0, other, total)
        return jnp.stack([first, second], axis=1).reshape(-1, total.shape[2]).astype(F32)

    def join_pair(total):
        return join_cores(two_rows(total[None], swap_with(total, "dp", 1)[None]))

    def own_rows(value):
        count = value.shape[0] // 2
        return lax.dynamic_slice_in_dim(value, pair * count, count, axis=0)

    def own_delta(index, own_gradient):
        master, first, second = masters[index], firsts[index][0], seconds[index][0]
        return local_delta(
            own_rows(master), own_rows(first), own_rows(second), own_gradient.astype(F32), rates[index]
        )

    def finish(index, gradient, summed):
        reduced[index] = gradient
        first_next, second_next = moments_next(firsts[index][0], seconds[index][0], gradient)
        firsts_out[index] = first_next[None]
        seconds_out[index] = second_next[None]
        delta = summed / groups
        outer_next = OUTER_MOMENTUM * outers[index] + delta
        deltas_out[index] = delta
        outers_out[index] = outer_next
        weights_out[index] = masters[index] - OUTER_RATE * (delta + OUTER_MOMENTUM * outer_next)

    ada_delta = local_delta(w_ada, first_ada[0], second_ada[0], grad_ada, rates[0])
    one_half, there_attn, two_half, ada_delta = after(one_half, there_attn, two_half, ada_delta)
    attn_both = jnp.concatenate(
        [own_half(halves(grad_qkv), pair), own_half(halves(grad_proj), pair)], axis=2
    )
    attn_both = (attn_both.astype(F32) + there_attn.astype(F32)).astype(BF16)
    attn_both, two_half, one_half, ada_delta = after(attn_both, two_half, one_half, ada_delta)
    attn_half = line_sum(attn_both)
    finish(0, grad_ada, join_cores(sum_rep(ada_delta)[None]))
    bias_delta = local_delta(biases, first_bias[0], second_bias[0], grad_bias, rates[5])
    finish(5, grad_bias, sum_rep(bias_delta))
    two_total = sum_rep(own_delta(4, two_half))
    finish(4, both_halves(two_half), join_pair(two_total))
    one_total = sum_rep(own_delta(3, one_half))
    finish(3, both_halves(one_half), join_pair(one_total))
    attn_half, one_total = after(attn_half, one_total)
    edge = 3 * width
    summed = join_pair(
        sum_rep(
            jnp.concatenate(
                [own_delta(1, attn_half[:, :edge]), own_delta(2, attn_half[:, edge:])], axis=1
            )
        )
    )
    attn_full = both_halves(attn_half)
    finish(1, attn_full[:, :edge], summed[:, :edge])
    finish(2, attn_full[:, edge:], summed[:, edge:])
    grads_out = tuple((gradient[None] for gradient in reduced))
    return (
        (result.reshape(images.shape), in_grad.reshape(images.shape))
        + grads_out
        + tuple(firsts_out)
        + tuple(seconds_out)
        + tuple(deltas_out)
        + tuple(outers_out)
        + tuple(weights_out)
    )


def solution(mesh):
    in_specs = (
        P(("rep", "dp", "fsdp"), None, None),
        P(("rep", "dp", "fsdp"), None, None),
        P(("rep", "dp", "fsdp")),
        P(("rep", "dp", "fsdp")),
        P(("rep", "dp", "fsdp")),
        P(),
        P(),
        P("fsdp", None),
        P("fsdp", None),
        P("fsdp", None),
        P("fsdp", None),
        P("fsdp", None),
        P("fsdp"),
        P("rep", "fsdp", None),
        P("rep", "fsdp", None),
        P("rep", "fsdp", None),
        P("rep", "fsdp", None),
        P("rep", "fsdp", None),
        P("rep", "fsdp"),
        P("rep", "fsdp", None),
        P("rep", "fsdp", None),
        P("rep", "fsdp", None),
        P("rep", "fsdp", None),
        P("rep", "fsdp", None),
        P("rep", "fsdp"),
        P("fsdp", None),
        P("fsdp", None),
        P("fsdp", None),
        P("fsdp", None),
        P("fsdp", None),
        P("fsdp"),
    )
    out_specs = (
        P(("rep", "dp", "fsdp"), None, None),
        P(("rep", "dp", "fsdp"), None, None),
        P("rep", "fsdp", None),
        P("rep", "fsdp", None),
        P("rep", "fsdp", None),
        P("rep", "fsdp", None),
        P("rep", "fsdp", None),
        P("rep", "fsdp"),
        P("rep", "fsdp", None),
        P("rep", "fsdp", None),
        P("rep", "fsdp", None),
        P("rep", "fsdp", None),
        P("rep", "fsdp", None),
        P("rep", "fsdp"),
        P("rep", "fsdp", None),
        P("rep", "fsdp", None),
        P("rep", "fsdp", None),
        P("rep", "fsdp", None),
        P("rep", "fsdp", None),
        P("rep", "fsdp"),
        P("fsdp", None),
        P("fsdp", None),
        P("fsdp", None),
        P("fsdp", None),
        P("fsdp", None),
        P("fsdp"),
        P("fsdp", None),
        P("fsdp", None),
        P("fsdp", None),
        P("fsdp", None),
        P("fsdp", None),
        P("fsdp"),
        P("fsdp", None),
        P("fsdp", None),
        P("fsdp", None),
        P("fsdp", None),
        P("fsdp", None),
        P("fsdp"),
    )
    return jax.shard_map(body, mesh=mesh, in_specs=in_specs, out_specs=out_specs, check_vma=False)
```

```python
import math

import jax
import jax.numpy as jnp
from jax import lax
from jax.experimental import pallas as pl
from jax.experimental.pallas import tpu as pltpu
from jax.sharding import PartitionSpec as P

D = 1152
HEADS = 16
FF = 4608


NORM_EPS = 1e-06
BETA_ONE = 0.9
BETA_TWO = 0.95
ADAM_EPS = 1e-08
WEIGHT_DECAY = 0.1
OUTER_RATE = 0.7
OUTER_MOMENTUM = 0.9
FEW = 8

F32 = jnp.float32
BF16 = jnp.bfloat16


def dot(left, right):
    return jnp.dot(left, right, preferred_element_type=F32)


def dot_nt(left, right):
    return lax.dot_general(left, right, (((1,), (1,)), ((), ())), preferred_element_type=F32)


def dot_tn(left, right):
    return lax.dot_general(left, right, (((0,), (0,)), ((), ())), preferred_element_type=F32)


def time_embed(steps, width):
    half = width // 2
    frequency = jnp.exp(-math.log(10000.0) * jnp.arange(half).astype(F32) / half)
    angles = steps.astype(F32)[:, None] * frequency[None, :]
    return jnp.concatenate([jnp.cos(angles), jnp.sin(angles)], axis=1)


def learning_rates(width, hidden):
    return (
        2.0 / math.sqrt(width),
        2.0 / math.sqrt(width),
        2.0 / math.sqrt(width // 32),
        2.0 / math.sqrt(width),
        2.0 / math.sqrt(hidden),
        0.3,
    )


def shift_by(value, axis, step):
    size = lax.axis_size(axis)
    return lax.ppermute(value, axis, [(i, (i + step) % size) for i in range(size)])


def swap_with(value, axis, bit):
    size = lax.axis_size(axis)
    return lax.ppermute(value, axis, [(i, i ^ bit) for i in range(size)])


def gather_line(value, axis):
    size = lax.axis_size(axis)
    if size > FEW:
        return lax.all_gather(value, axis, axis=0)
    place = lax.axis_index(axis)
    result = jnp.zeros((size,) + value.shape, value.dtype)
    for step in range(size):
        piece = value if step == 0 else shift_by(value, axis, step)
        result = lax.dynamic_update_index_in_dim(result, piece, (place - step) % size, 0)
    return result


def scatter_line(value, axis):
    size = lax.axis_size(axis)
    if size > FEW:
        return lax.psum_scatter(value, axis, scatter_dimension=0, tiled=False)
    place = lax.axis_index(axis)
    total = lax.dynamic_index_in_dim(value, place, 0, keepdims=False)
    for step in range(1, size):
        piece = lax.dynamic_index_in_dim(value, (place + step) % size, 0, keepdims=False)
        total = total + shift_by(piece, axis, step)
    return total


def moments(values):
    center = values - jnp.mean(values, axis=-1, keepdims=True)
    inverse = lax.rsqrt(jnp.mean(center * center, axis=-1, keepdims=True) + NORM_EPS)
    return center * inverse, inverse


def norm_back(normed, inverse, upstream):
    first = jnp.mean(upstream, axis=-1, keepdims=True)
    second = jnp.mean(upstream * normed, axis=-1, keepdims=True)
    return (upstream - first - normed * second) * inverse


def gelu_pair(h):
    c = math.sqrt(2.0 / math.pi)
    inner = c * (h + 0.044715 * h * h * h)
    t = jnp.tanh(inner)
    value = 0.5 * h * (1.0 + t)
    slope = 0.5 * (1.0 + t) + 0.5 * h * (1.0 - t * t) * c * (1.0 + 3.0 * 0.044715 * h * h)
    return value, slope


def head_window(head, head_dim):
    low = head * head_dim
    start = low // 128 * 128
    stop = -(-(low + head_dim) // 128) * 128
    return start, stop, low - start


def head_mask(shape, offset, head_dim):
    lane = lax.broadcasted_iota(jnp.int32, shape, 1)
    return (lane >= offset) & (lane < offset + head_dim)


def attention_forward_kernel(
    x_ref, cot_ref, mod_ref, bias_ref, weight_ref,
    attn_in_ref, packed_ref, attended_ref, log_ref, attn_ref, x1_ref, mlp_in_ref, d_mlp_ref, sums_ref,
    gather_ref,
):
    length, width = x_ref.shape
    head_dim = width // HEADS
    factor = 1.0 / math.sqrt(head_dim)
    residual = x_ref[...].astype(F32)
    normed, _ = moments(residual)
    attn_in_ref[...] = (normed * (1.0 + mod_ref[0, 1:2]) + mod_ref[0, 0:1]).astype(BF16)
    for unit in range(3):
        piece = dot(attn_in_ref[...], weight_ref[unit]) + bias_ref[unit : unit + 1]
        packed_ref[:, unit * width : (unit + 1) * width] = piece.astype(BF16)
    for head in range(HEADS):
        start, stop, offset = head_window(head, head_dim)
        mask = head_mask((length, stop - start), offset, head_dim)
        query = packed_ref[:, start:stop]
        query = jnp.where(mask, query, jnp.zeros_like(query))
        keys = packed_ref[:, width + start : width + stop]
        values = packed_ref[:, 2 * width + start : 2 * width + stop]
        scores = dot_nt(query, keys) * factor
        top = jnp.max(scores, axis=-1, keepdims=True)
        raised = jnp.exp(scores - top)
        summed = jnp.sum(raised, axis=-1, keepdims=True)
        probs = (raised * (1.0 / summed)).astype(BF16)
        log_ref[:, head : head + 1] = top + jnp.log(summed)
        out = dot(probs, values)
        if offset == 0:
            gather_ref[:, start:stop] = out
        else:
            gather_ref[:, start:stop] = jnp.where(mask, out, gather_ref[:, start:stop])
    attended_ref[...] = gather_ref[...].astype(BF16)
    attn = dot(attended_ref[...], weight_ref[3]) + bias_ref[3:4]
    attn_ref[...] = attn
    middle = residual + mod_ref[0, 2:3] * attn
    x1_ref[...] = middle
    normed_two, _ = moments(middle)
    mlp_in_ref[...] = (normed_two * (1.0 + mod_ref[0, 4:5]) + mod_ref[0, 3:4]).astype(BF16)
    d_mlp = (mod_ref[0, 5:6] * (cot_ref[...].astype(F32) * mod_ref[0, 6:7])).astype(BF16)
    d_mlp_ref[...] = d_mlp
    sums_ref[0, 0:1] = jnp.sum(d_mlp.astype(F32), axis=0, keepdims=True)


def rows_spec(length, width):
    return pl.BlockSpec((length, width), lambda i: (i, 0))


def whole_spec(shape):
    return pl.BlockSpec(shape, lambda i: (0,) * len(shape), pipeline_mode=pl.Buffered(1))


def lead_spec(rows, width):
    return pl.BlockSpec((1, rows, width), lambda i: (i, 0, 0))


def params(megabytes):
    return pltpu.CompilerParams(vmem_limit_bytes=megabytes << 20)


def attention_forward(x, cot, mod, bias, weights, slots, length, width):
    tokens = slots * length
    row = rows_spec(length, width)
    return pl.pallas_call(
        attention_forward_kernel,
        grid=(slots,),
        in_specs=[row, row, lead_spec(8, width), whole_spec((8, width)), whole_spec((4, width, width))],
        out_specs=[
            row, rows_spec(length, 3 * width), row, rows_spec(length, 128), row, row, row, row,
            lead_spec(8, width),
        ],
        out_shape=[
            jax.ShapeDtypeStruct((tokens, width), BF16),
            jax.ShapeDtypeStruct((tokens, 3 * width), BF16),
            jax.ShapeDtypeStruct((tokens, width), BF16),
            jax.ShapeDtypeStruct((tokens, 128), F32),
            jax.ShapeDtypeStruct((tokens, width), F32),
            jax.ShapeDtypeStruct((tokens, width), F32),
            jax.ShapeDtypeStruct((tokens, width), BF16),
            jax.ShapeDtypeStruct((tokens, width), BF16),
            jax.ShapeDtypeStruct((slots, 8, width), F32),
        ],
        scratch_shapes=[pltpu.VMEM((length, width), F32)],
        compiler_params=params(48),
        cost_estimate=pl.CostEstimate(
            flops=2 * tokens * width * width * 4, bytes_accessed=40 << 20, transcendentals=0
        ),
    )(x, cot, mod, bias, weights)


def one_spec(joint):
    lines, rows, width = joint.shape[1], joint.shape[4], joint.shape[5]
    return pl.BlockSpec((1, lines, 2, 1, rows, width), lambda u: (u, 0, 0, 0, 0, 0))


def two_spec(joint):
    groups, lines, _, _, rows, width = joint.shape
    return pl.BlockSpec((groups, lines // groups, 2, 1, rows, width), lambda u: (0, u, 0, 1, 0, 0))


def one_of(ref):
    return ref[...].reshape(ref.shape[-1], ref.shape[-1])


def two_of(ref):
    value = ref[...]
    if value.shape[1] > 1:
        value = jnp.swapaxes(value, 0, 1)
    return value.reshape(ref.shape[-1], ref.shape[-1])


def hidden_kernel(mlp_in_ref, weight_ref, bias_ref, act_ref, slope_ref):
    step = 256

    def chunk(index, carry):
        here = pl.ds(pl.multiple_of(index * step, step), step)
        hidden = dot(mlp_in_ref[here, :], one_of(weight_ref)) + bias_ref[0:1]
        value, slope = gelu_pair(hidden)
        act_ref[here, :] = value.astype(BF16)
        slope_ref[here, :] = slope.astype(BF16)
        return carry

    lax.fori_loop(0, mlp_in_ref.shape[0] // step, chunk, 0)


def hidden_forward(mlp_in, weights, bias):
    tokens, width = mlp_in.shape
    units = weights.shape[0]
    column = pl.BlockSpec((tokens, width), lambda u: (0, u))
    return pl.pallas_call(
        hidden_kernel,
        grid=(units,),
        in_specs=[whole_spec((tokens, width)), one_spec(weights), pl.BlockSpec((1, width), lambda u: (0, u))],
        out_specs=[column, column],
        out_shape=[jax.ShapeDtypeStruct((tokens, units * width), BF16)] * 2,
        compiler_params=params(48),
        cost_estimate=pl.CostEstimate(
            flops=2 * tokens * width * width * units, bytes_accessed=26 << 20, transcendentals=0
        ),
    )(mlp_in, weights, bias)


def hidden_back_kernel(d_mlp_ref, weight_ref, slope_ref, d_hidden_ref, sums_ref):
    step = 256

    def chunk(index, carry):
        here = pl.ds(pl.multiple_of(index * step, step), step)
        d_hidden = dot_nt(d_mlp_ref[here, :], two_of(weight_ref)) * slope_ref[here, :].astype(F32)
        d_hidden = d_hidden.astype(BF16)
        d_hidden_ref[here, :] = d_hidden
        return carry + jnp.sum(d_hidden.astype(F32), axis=0, keepdims=True)

    zero = jnp.zeros((1, slope_ref.shape[1]), F32)
    sums_ref[0:1] = lax.fori_loop(0, d_mlp_ref.shape[0] // step, chunk, zero)


def hidden_back(d_mlp, weights, slope):
    tokens, width = d_mlp.shape
    units = weights.shape[0]
    column = pl.BlockSpec((tokens, width), lambda u: (0, u))
    return pl.pallas_call(
        hidden_back_kernel,
        grid=(units,),
        in_specs=[whole_spec((tokens, width)), two_spec(weights), column],
        out_specs=[column, pl.BlockSpec((8, width), lambda u: (0, u))],
        out_shape=[
            jax.ShapeDtypeStruct((tokens, units * width), BF16),
            jax.ShapeDtypeStruct((8, units * width), F32),
        ],
        compiler_params=params(48),
        cost_estimate=pl.CostEstimate(
            flops=2 * tokens * width * width * units, bytes_accessed=26 << 20, transcendentals=0
        ),
    )(d_mlp, weights, slope)


def mlp_rest_kernel(act_ref, d_hidden_ref, two_ref, one_ref, mlp_ref, d_in_ref):
    step = 256

    @pl.when(pl.program_id(0) == 0)
    def _():
        mlp_ref[...] = jnp.zeros_like(mlp_ref)
        d_in_ref[...] = jnp.zeros_like(d_in_ref)

    def chunk(index, carry):
        here = pl.ds(pl.multiple_of(index * step, step), step)
        mlp_ref[here, :] += dot(act_ref[here, :], two_of(two_ref))
        d_in_ref[here, :] += dot_nt(d_hidden_ref[here, :], one_of(one_ref))
        return carry

    lax.fori_loop(0, act_ref.shape[0] // step, chunk, 0)


def mlp_rest(act, d_hidden, weights):
    tokens = act.shape[0]
    units, width = weights.shape[0], weights.shape[-1]
    column = pl.BlockSpec((tokens, width), lambda u: (0, u))
    total = pl.BlockSpec((tokens, width), lambda u: (0, 0))
    return pl.pallas_call(
        mlp_rest_kernel,
        grid=(units,),
        in_specs=[column, column, two_spec(weights), one_spec(weights)],
        out_specs=[total, total],
        out_shape=[jax.ShapeDtypeStruct((tokens, width), F32)] * 2,
        compiler_params=params(48),
        cost_estimate=pl.CostEstimate(
            flops=4 * tokens * width * width * units, bytes_accessed=42 << 20, transcendentals=0
        ),
    )(act, d_hidden, weights, weights)


def middle_back_kernel(
    mlp_ref, bias_ref, d_in_ref, x1_ref, attn_ref, cot_ref, mod_ref, weight_ref,
    out_ref, d_mid_ref, d_attn_ref, d_att_ref, rows_ref,
):
    live = mod_ref[0, 6:7]
    gate_two = mod_ref[0, 5:6]
    upstream = cot_ref[...].astype(F32) * live
    middle = x1_ref[...]
    mlp = mlp_ref[...] + bias_ref[4:5]
    out_ref[...] = ((middle + gate_two * mlp) * live).astype(BF16)
    rows_ref[0, 5:6] = jnp.sum(upstream * mlp, axis=0, keepdims=True)
    normed, inverse = moments(middle)
    d_in = d_in_ref[...]
    rows_ref[0, 3:4] = jnp.sum(d_in, axis=0, keepdims=True)
    rows_ref[0, 4:5] = jnp.sum(d_in * normed, axis=0, keepdims=True)
    d_mid = upstream + norm_back(normed, inverse, d_in * (1.0 + mod_ref[0, 4:5]))
    d_mid_ref[...] = d_mid
    rows_ref[0, 2:3] = jnp.sum(d_mid * attn_ref[...], axis=0, keepdims=True)
    d_attn = (mod_ref[0, 2:3] * d_mid).astype(BF16)
    d_attn_ref[...] = d_attn
    rows_ref[0, 6:7] = jnp.sum(d_attn.astype(F32), axis=0, keepdims=True)
    d_att_ref[...] = dot_nt(d_attn_ref[...], weight_ref[0]).astype(BF16)


def middle_back(mlp, bias, d_in, x1, attn, cot, mod, weights, slots, length, width):
    tokens = slots * length
    row = rows_spec(length, width)
    proj = pl.BlockSpec((1, width, width), lambda i: (3, 0, 0), pipeline_mode=pl.Buffered(1))
    return pl.pallas_call(
        middle_back_kernel,
        grid=(slots,),
        in_specs=[row, whole_spec((8, width)), row, row, row, row, lead_spec(8, width), proj],
        out_specs=[row, row, row, row, lead_spec(8, width)],
        out_shape=[
            jax.ShapeDtypeStruct((tokens, width), BF16),
            jax.ShapeDtypeStruct((tokens, width), F32),
            jax.ShapeDtypeStruct((tokens, width), BF16),
            jax.ShapeDtypeStruct((tokens, width), BF16),
            jax.ShapeDtypeStruct((slots, 8, width), F32),
        ],
        compiler_params=params(48),
        cost_estimate=pl.CostEstimate(
            flops=2 * tokens * width * width, bytes_accessed=30 << 20, transcendentals=0
        ),
    )(mlp, bias, d_in, x1, attn, cot, mod, weights)


def attention_back_kernel(packed_ref, d_att_ref, log_ref, d_packed_ref, sums_ref, q_ref, k_ref, v_ref):
    length, width = d_att_ref.shape
    head_dim = width // HEADS
    factor = 1.0 / math.sqrt(head_dim)
    for head in range(HEADS):
        start, stop, offset = head_window(head, head_dim)
        mask = head_mask((length, stop - start), offset, head_dim)
        query = packed_ref[:, start:stop]
        query_one = jnp.where(mask, query, jnp.zeros_like(query))
        keys = packed_ref[:, width + start : width + stop]
        values = packed_ref[:, 2 * width + start : 2 * width + stop]
        d_att = d_att_ref[:, start:stop]
        d_att = jnp.where(mask, d_att, jnp.zeros_like(d_att))
        weights = jnp.exp(dot_nt(query_one, keys) * factor - log_ref[:, head : head + 1])
        d_probs = dot_nt(d_att, values)
        inner = jnp.sum(weights * d_probs, axis=-1, keepdims=True)
        d_scores = (weights * (d_probs - inner)).astype(BF16)
        probs = weights.astype(BF16)
        pieces = (
            (q_ref, dot(d_scores, keys) * factor),
            (k_ref, dot_tn(d_scores, query) * factor),
            (v_ref, dot_tn(probs, d_att)),
        )
        for ref, piece in pieces:
            if offset == 0:
                ref[:, start:stop] = piece
            else:
                ref[:, start:stop] = jnp.where(mask, piece, ref[:, start:stop])
    for unit, ref in enumerate((q_ref, k_ref, v_ref)):
        piece = ref[...].astype(BF16)
        d_packed_ref[:, unit * width : (unit + 1) * width] = piece
        sums_ref[0, unit : unit + 1] = jnp.sum(piece.astype(F32), axis=0, keepdims=True)


def attention_back(packed, d_att, log, slots, length, width):
    tokens = slots * length
    return pl.pallas_call(
        attention_back_kernel,
        grid=(slots,),
        in_specs=[rows_spec(length, 3 * width), rows_spec(length, width), rows_spec(length, 128)],
        out_specs=[rows_spec(length, 3 * width), lead_spec(8, width)],
        out_shape=[
            jax.ShapeDtypeStruct((tokens, 3 * width), BF16),
            jax.ShapeDtypeStruct((slots, 8, width), F32),
        ],
        scratch_shapes=[pltpu.VMEM((length, width), F32)] * 3,
        compiler_params=params(48),
        cost_estimate=pl.CostEstimate(
            flops=10 * tokens * length * 256 * HEADS, bytes_accessed=14 << 20, transcendentals=0
        ),
    )(packed, d_att, log)


def input_back_kernel(d_packed_ref, weight_ref, x_ref, d_mid_ref, mod_ref, grad_ref, rows_ref):
    width = x_ref.shape[1]
    d_in = dot_nt(d_packed_ref[:, :width], weight_ref[0])
    for unit in (1, 2):
        d_in = d_in + dot_nt(d_packed_ref[:, unit * width : (unit + 1) * width], weight_ref[unit])
    normed, inverse = moments(x_ref[...].astype(F32))
    rows_ref[0, 0:1] = jnp.sum(d_in, axis=0, keepdims=True)
    rows_ref[0, 1:2] = jnp.sum(d_in * normed, axis=0, keepdims=True)
    back = norm_back(normed, inverse, d_in * (1.0 + mod_ref[0, 1:2]))
    grad_ref[...] = (d_mid_ref[...] + back).astype(BF16)


def input_back(d_packed, weights, x, d_mid, mod, slots, length, width):
    tokens = slots * length
    row = rows_spec(length, width)
    return pl.pallas_call(
        input_back_kernel,
        grid=(slots,),
        in_specs=[
            rows_spec(length, 3 * width), whole_spec((3, width, width)), row, row, lead_spec(8, width),
        ],
        out_specs=[row, lead_spec(8, width)],
        out_shape=[
            jax.ShapeDtypeStruct((tokens, width), BF16),
            jax.ShapeDtypeStruct((slots, 8, width), F32),
        ],
        compiler_params=params(48),
        cost_estimate=pl.CostEstimate(
            flops=6 * tokens * width * width, bytes_accessed=20 << 20, transcendentals=0
        ),
    )(d_packed, weights, x, d_mid, mod)


def grad_kernel(left_ref, right_ref, grad_ref):
    step = grad_ref.shape[0] // 3

    def chunk(index, carry):
        here = pl.ds(pl.multiple_of(index * step, step), step)
        grad_ref[here, :] = dot_tn(left_ref[:, here], right_ref[...]).astype(BF16)
        return carry

    lax.fori_loop(0, 3, chunk, 0)


def grad_columns(left, right):
    tokens, rows = left.shape
    width = right.shape[1]
    return pl.pallas_call(
        grad_kernel,
        grid=(width // rows,),
        in_specs=[whole_spec((tokens, rows)), pl.BlockSpec((tokens, rows), lambda u: (0, u))],
        out_specs=pl.BlockSpec((rows, rows), lambda u: (0, u)),
        out_shape=jax.ShapeDtypeStruct((rows, width), BF16),
        compiler_params=params(48),
        cost_estimate=pl.CostEstimate(
            flops=2 * tokens * rows * width, bytes_accessed=2 * rows * width + 4 * tokens * width, transcendentals=0
        ),
    )(left, right)


def grad_rows(left, right):
    tokens, rows = left.shape
    width = right.shape[1]
    return pl.pallas_call(
        grad_kernel,
        grid=(rows // width,),
        in_specs=[pl.BlockSpec((tokens, width), lambda u: (0, u)), whole_spec((tokens, width))],
        out_specs=rows_spec(width, width),
        out_shape=jax.ShapeDtypeStruct((rows, width), BF16),
        compiler_params=params(48),
        cost_estimate=pl.CostEstimate(
            flops=2 * tokens * rows * width, bytes_accessed=2 * rows * width + 4 * tokens * rows, transcendentals=0
        ),
    )(left, right)


def after(*values):
    return lax.optimization_barrier(values)


def place_kernel(order_ref, *refs):
    sources, target, held, came, left = refs[:-4], refs[-4], refs[-3], refs[-2], refs[-1]
    inward, outward = [], []
    for which, source in enumerate(sources):
        for block in range(source.shape[0]):
            index = which * source.shape[0] + block
            inward.append(pltpu.make_async_copy(source.at[block], held.at[index], came.at[index]))
            outward.append(
                pltpu.make_async_copy(held.at[index], target.at[order_ref[index]], left.at[index])
            )
    for copy in inward:
        copy.start()
    for first, second in zip(inward, outward):
        first.wait()
        second.start()
    for copy in outward:
        copy.wait()


def place_blocks(order, sources):
    blocks = sum(source.shape[0] for source in sources)
    shape = (blocks,) + sources[0].shape[1:]
    return pl.pallas_call(
        place_kernel,
        grid_spec=pltpu.PrefetchScalarGridSpec(
            num_scalar_prefetch=1,
            grid=(1,),
            in_specs=[pl.BlockSpec(memory_space=pl.ANY)] * len(sources),
            out_specs=pl.BlockSpec(memory_space=pl.ANY),
            scratch_shapes=[
                pltpu.VMEM(shape, sources[0].dtype),
                pltpu.SemaphoreType.DMA((blocks,)),
                pltpu.SemaphoreType.DMA((blocks,)),
            ],
        ),
        out_shape=jax.ShapeDtypeStruct(shape, sources[0].dtype),
        compiler_params=params(48),
        cost_estimate=pl.CostEstimate(
            flops=0, bytes_accessed=4 * blocks * shape[1] * shape[2], transcendentals=0
        ),
    )(order, *sources)


def hops_line(piece):
    near = jnp.stack([piece, shift_by(piece, "fsdp", 1)])
    far = jnp.stack([shift_by(piece, "fsdp", 2), shift_by(piece, "fsdp", 3)])
    return near, far


def hops_side(near, far):
    near = jnp.concatenate([near, swap_with(near, "rep", 2)])
    far = jnp.concatenate([far, swap_with(far, "dp", 1)])
    return near, far


def hops_other(near, far):
    return near, far, swap_with(near, "dp", 1), swap_with(far, "rep", 2)


def hops_core(sources):
    return tuple(sources) + tuple(swap_with(source, "rep", 1) for source in sources)


def hops_place(sources, weigh):
    size = lax.axis_size("fsdp")
    rep, pair, line = lax.axis_index("rep"), lax.axis_index("dp"), lax.axis_index("fsdp")
    order = []
    for core in (0, 1):
        for kind in range(4):
            for block in range(4):
                hop, step = block // 2, block % 2
                if kind in (0, 2):
                    flip_rep, flip_pair, back = hop, kind // 2, step
                else:
                    flip_rep, flip_pair, back = kind // 2, hop, 2 + step
                place = lax.rem(line - back + size, size) * weigh[0]
                place = place + (rep ^ (2 * flip_rep + core)) * weigh[1] + (pair ^ flip_pair) * weigh[2]
                order.append(place)
    return place_blocks(jnp.stack(order).astype(jnp.int32), sources)


def own_half(value, index):
    return lax.dynamic_index_in_dim(value, index, 1, keepdims=False)


def body(
    images,
    cotangent,
    counts,
    timesteps,
    labels,
    label_table,
    step_count,
    w_ada,
    w_qkv,
    w_proj,
    w_fc1,
    w_fc2,
    biases,
    first_ada,
    first_qkv,
    first_proj,
    first_fc1,
    first_fc2,
    first_bias,
    second_ada,
    second_qkv,
    second_proj,
    second_fc1,
    second_fc2,
    second_bias,
    outer_ada,
    outer_qkv,
    outer_proj,
    outer_fc1,
    outer_fc2,
    outer_bias,
):
    masters = (w_ada, w_qkv, w_proj, w_fc1, w_fc2, biases)
    firsts = (first_ada, first_qkv, first_proj, first_fc1, first_fc2, first_bias)
    seconds = (second_ada, second_qkv, second_proj, second_fc1, second_fc2, second_bias)
    outers = (outer_ada, outer_qkv, outer_proj, outer_fc1, outer_fc2, outer_bias)
    slots, length, width = images.shape
    tokens = slots * length
    rows = w_qkv.shape[0]
    rows_two = w_fc2.shape[0]
    lines = lax.axis_size("fsdp")
    groups = lax.axis_size("rep")
    rep = lax.axis_index("rep")
    pair = lax.axis_index("dp")
    line = lax.axis_index("fsdp")
    half = rows // 2
    everyone = ("rep", "fsdp", "dp")

    def rows_of(weight):
        return lax.dynamic_slice_in_dim(weight, pair * half, half, axis=0).astype(BF16)

    attention_cut = jnp.concatenate([rows_of(w_qkv), rows_of(w_proj)], axis=1)
    attention_cut = lax.dynamic_slice_in_dim(attention_cut, rep * width, width, axis=1)
    hops = lines == 4 and groups == 4
    one_cut = lax.dynamic_slice(w_fc1, (pair * half, rep * width), (half, width))
    eighth = rows_two // (2 * groups)
    two_cut = lax.dynamic_slice_in_dim(w_fc2, (rep * 2 + pair) * eighth, eighth, axis=0)
    mlp_cut = jnp.concatenate([one_cut, two_cut]).astype(BF16)
    w_mlp = lax.all_gather(mlp_cut, everyone, axis=0, tiled=True)
    w_mlp = w_mlp.reshape(groups, lines, 2, 2, half, width)
    live = (jnp.arange(slots) < counts[0]).astype(F32)
    condition = time_embed(timesteps, D) + jnp.take(label_table, labels, axis=0).astype(F32)
    style = jax.nn.silu(condition).astype(BF16)
    message = jnp.concatenate([style.reshape(-1), biases.astype(BF16)])
    heard = gather_line(message, "fsdp")
    if hops:
        attention_cut, message = after(attention_cut, message)
        attention_parts = hops_line(attention_cut)
        heard = after(heard, *attention_parts)[0]
        attention_parts = hops_side(*attention_parts)
    else:
        w_attn = lax.all_gather(attention_cut, everyone, axis=0, tiled=True)
    bias_all = heard[:, slots * width :].reshape(-1).astype(F32)
    style_line = heard[:, : slots * width].reshape(lines * slots, width)
    style_cut = lax.dynamic_slice_in_dim(style_line, line * rows, rows, axis=1)
    mod_part = dot(style_cut, w_ada.astype(BF16))
    if hops:
        attention_parts = hops_other(*attention_parts)
        attention_parts = after(*attention_parts, mod_part)[:-1]
        w_attn = hops_place(hops_core(attention_parts), (2, 8, 1))
    w_attn = w_attn.reshape(4, width, width)
    b_ada = bias_all[: 6 * width]
    modulation = scatter_line(mod_part.reshape(lines, slots, 6 * width), "fsdp") + b_ada
    mod = jnp.concatenate(
        [
            modulation.reshape(slots, 6, width),
            jnp.broadcast_to(live[:, None, None], (slots, 2, width)),
        ],
        axis=1,
    )
    b_rest = bias_all[6 * width : 9 * width].reshape(3, width)
    bias = jnp.zeros((8, width), F32)
    bias = bias.at[0].set(b_rest[0]).at[2].set(b_rest[1]).at[3].set(b_rest[2])
    bias = bias.at[4].set(bias_all[9 * width + FF :])
    b_fc1 = bias_all[9 * width : 9 * width + FF].reshape(1, FF)
    x = images.reshape(tokens, width)
    cot = cotangent.reshape(tokens, width)

    attn_in, packed, attended, log_total, attn_out, middle, mlp_in, d_mlp, mlp_sums = attention_forward(
        x, cot, mod, bias, w_attn, slots, length, width
    )
    activated, slope = hidden_forward(mlp_in, w_mlp, b_fc1)
    grad_two = grad_rows(activated, d_mlp)

    def halves(gradient):
        return gradient.reshape(lines, 2, gradient.shape[0] // (2 * lines), gradient.shape[1])

    def line_sum(both):
        return lax.psum_scatter(
            both.reshape(-1, both.shape[-1]), "fsdp", scatter_dimension=0, tiled=True
        )

    def pair_sum(gradient, there):
        return (own_half(halves(gradient), pair).astype(F32) + there.astype(F32)).astype(BF16)

    grad_two, d_mlp = after(grad_two, d_mlp)
    two_line = line_sum(grad_two)
    d_hidden, hidden_sums = hidden_back(d_mlp, w_mlp, slope)
    grad_one = grad_columns(mlp_in, d_hidden)
    give_one = own_half(halves(grad_one), 1 - pair)
    give_one, d_hidden = after(give_one, d_hidden)
    there_one = swap_with(give_one, "dp", 1)
    mlp_out, d_mlp_in = mlp_rest(activated, d_hidden, w_mlp)
    result, d_middle, d_attn, d_attended, middle_rows = middle_back(
        mlp_out, bias, d_mlp_in, middle, attn_out, cot, mod, w_attn, slots, length, width
    )
    grad_proj = grad_columns(attended, d_attn)
    grad_proj, d_attended = after(grad_proj, d_attended)
    d_packed, packed_sums = attention_back(packed, d_attended, log_total, slots, length, width)
    grad_qkv = grad_columns(attn_in, d_packed)
    give_attn = own_half(halves(grad_qkv), 1 - pair)
    give_proj = own_half(halves(grad_proj), 1 - pair)
    give_attn, give_proj, d_packed = after(give_attn, give_proj, d_packed)
    there_proj = swap_with(give_proj, "dp", 1)
    in_grad, input_rows = input_back(d_packed, w_attn, x, d_middle, mod, slots, length, width)

    there_one, give_attn, in_grad, input_rows = after(there_one, give_attn, in_grad, input_rows)
    there_attn = swap_with(give_attn, "dp", 1)
    one_both = pair_sum(grad_one, there_one)
    one_half = line_sum(one_both)
    two_line, one_both, there_proj, input_rows = after(two_line, one_both, there_proj, input_rows)

    d_modulation = jnp.concatenate([input_rows[:, :2], middle_rows[:, 2:6]], axis=1).astype(BF16)
    packed_total = jnp.sum(packed_sums, axis=0)
    bias_sums = jnp.concatenate(
        [
            packed_total[0],
            packed_total[2],
            jnp.sum(middle_rows[:, 6], axis=0),
            hidden_sums[0],
            jnp.sum(mlp_sums[:, 0], axis=0),
        ]
    ).astype(BF16)

    report = jnp.concatenate([style.reshape(-1), d_modulation.reshape(-1), bias_sums])
    report = jnp.stack([report, swap_with(report, "dp", 1)])
    reports = gather_line(report, "fsdp").reshape(2 * lines, -1)
    edge = slots * width
    style_group = reports[:, :edge].reshape(2 * lines * slots, width)
    mod_group = reports[:, edge : 7 * edge].reshape(2 * lines * slots, 6 * width)
    style_own = lax.dynamic_slice_in_dim(style_group, line * rows, rows, axis=1)
    grad_ada = dot_tn(style_own, mod_group)
    bias_group = jnp.concatenate(
        [
            jnp.sum(mod_group.astype(F32), axis=0),
            jnp.sum(reports[:, 7 * edge :].astype(F32), axis=0),
        ]
    )
    own_bias = biases.shape[0]
    grad_bias = lax.dynamic_slice_in_dim(bias_group, line * own_bias, own_bias, axis=0)

    def two_rows(own, other):
        first = jnp.where(pair == 0, own, other)
        second = jnp.where(pair == 0, other, own)
        return jnp.concatenate([first, second], axis=0)

    power = step_count[0].astype(F32)
    fix_one = 1.0 - jnp.power(BETA_ONE, power)
    fix_two = 1.0 - jnp.power(BETA_TWO, power)
    rates = learning_rates(D, FF)
    reduced = [None] * 6
    firsts_out = [None] * 6
    seconds_out = [None] * 6
    deltas_out = [None] * 6
    outers_out = [None] * 6
    weights_out = [None] * 6

    def moments_next(first, second, gradient):
        first_next = BETA_ONE * first + (1.0 - BETA_ONE) * gradient
        second_next = BETA_TWO * second + (1.0 - BETA_TWO) * gradient * gradient
        return first_next, second_next

    def local_delta(master, first, second, gradient, rate):
        first_next, second_next = moments_next(first, second, gradient)
        local = master - rate * (
            first_next / fix_one / (jnp.sqrt(second_next / fix_two) + ADAM_EPS)
            + WEIGHT_DECAY * master
        )
        return (master - local).astype(BF16)

    low = rep % 2

    def sum_near(mine):
        mine = mine.reshape(2, mine.shape[0] // 2, mine.shape[1])
        keep = lax.dynamic_index_in_dim(mine, low, 0, keepdims=False)
        give = lax.dynamic_index_in_dim(mine, 1 - low, 0, keepdims=False)
        return (keep.astype(F32) + swap_with(give, "rep", 1).astype(F32)).astype(BF16)

    def sum_far(total):
        return (total.astype(F32) + swap_with(total, "rep", 2).astype(F32)).astype(BF16)

    def sum_rep(mine):
        if mine.ndim == 1:
            total = (mine.astype(F32) + swap_with(mine, "rep", 1).astype(F32)).astype(BF16)
            return total.astype(F32) + swap_with(total, "rep", 2).astype(F32)
        return sum_far(sum_near(mine))

    def join_cores(total):
        other = swap_with(total, "rep", 1)
        first = jnp.where(low == 0, total, other)
        second = jnp.where(low == 0, other, total)
        return jnp.stack([first, second], axis=1).reshape(-1, total.shape[2]).astype(F32)

    def join_pair(total):
        return join_cores(two_rows(total[None], swap_with(total, "dp", 1)[None]))

    def own_rows(value):
        count = value.shape[0] // 2
        return lax.dynamic_slice_in_dim(value, pair * count, count, axis=0)

    def own_delta(index, own_gradient):
        master, first, second = masters[index], firsts[index][0], seconds[index][0]
        return local_delta(
            own_rows(master), own_rows(first), own_rows(second), own_gradient.astype(F32), rates[index]
        )

    def keep_moments(index, gradient):
        reduced[index] = gradient
        first_next, second_next = moments_next(firsts[index][0], seconds[index][0], gradient)
        firsts_out[index] = first_next[None]
        seconds_out[index] = second_next[None]

    def outer_step(index, summed):
        delta = summed / groups
        outer_next = OUTER_MOMENTUM * outers[index] + delta
        deltas_out[index] = delta
        outers_out[index] = outer_next
        weights_out[index] = masters[index] - OUTER_RATE * (delta + OUTER_MOMENTUM * outer_next)

    ada_delta = local_delta(w_ada, first_ada[0], second_ada[0], grad_ada, rates[0])
    one_half, there_attn, two_line, ada_delta, grad_bias = after(
        one_half, there_attn, two_line, ada_delta, grad_bias
    )
    attn_both = jnp.concatenate(
        [pair_sum(grad_qkv, there_attn), pair_sum(grad_proj, there_proj)], axis=2
    )
    attn_both, two_line, one_half, ada_delta = after(attn_both, two_line, one_half, ada_delta)
    attn_half = line_sum(attn_both)
    two_there = swap_with(two_line, "dp", 1)
    ada_total = sum_rep(ada_delta)
    one_total = sum_rep(own_delta(3, one_half))
    one_other = swap_with(one_total, "dp", 1)
    two_there, one_other, one_half = after(two_there, one_other, one_half)
    one_there = swap_with(one_half, "dp", 1)
    grad_two = two_line.astype(F32) + two_there.astype(F32)
    two_delta = local_delta(w_fc2, first_fc2[0], second_fc2[0], grad_two, rates[4])
    bias_delta = local_delta(biases, first_bias[0], second_bias[0], grad_bias, rates[5])
    bias_total = sum_rep(bias_delta)
    keep_moments(0, grad_ada)
    keep_moments(5, grad_bias)
    keep_moments(4, grad_two)
    outer_step(5, bias_total)
    attn_half, one_other, ada_total, two_delta = after(attn_half, one_other, ada_total, two_delta)
    two_total = sum_rep(two_delta)
    outer_step(0, join_cores(ada_total[None]))
    keep_moments(3, two_rows(one_half, one_there).astype(F32))
    edge = 3 * width
    attn_total = sum_rep(
        jnp.concatenate([own_delta(1, attn_half[:, :edge]), own_delta(2, attn_half[:, edge:])], axis=1)
    )
    attn_there = swap_with(attn_half, "dp", 1)
    outer_step(4, join_cores(two_total[None]))
    outer_step(3, join_cores(two_rows(one_total[None], one_other[None])))
    attn_full = two_rows(attn_half, attn_there).astype(F32)
    keep_moments(1, attn_full[:, :edge])
    keep_moments(2, attn_full[:, edge:])
    summed = join_pair(attn_total)
    outer_step(1, summed[:, :edge])
    outer_step(2, summed[:, edge:])
    grads_out = tuple((gradient[None] for gradient in reduced))
    return (
        (result.reshape(images.shape), in_grad.reshape(images.shape))
        + grads_out
        + tuple(firsts_out)
        + tuple(seconds_out)
        + tuple(deltas_out)
        + tuple(outers_out)
        + tuple(weights_out)
    )


def solution(mesh):
    in_specs = (
        P(("rep", "dp", "fsdp"), None, None),
        P(("rep", "dp", "fsdp"), None, None),
        P(("rep", "dp", "fsdp")),
        P(("rep", "dp", "fsdp")),
        P(("rep", "dp", "fsdp")),
        P(),
        P(),
        P("fsdp", None),
        P("fsdp", None),
        P("fsdp", None),
        P("fsdp", None),
        P("fsdp", None),
        P("fsdp"),
        P("rep", "fsdp", None),
        P("rep", "fsdp", None),
        P("rep", "fsdp", None),
        P("rep", "fsdp", None),
        P("rep", "fsdp", None),
        P("rep", "fsdp"),
        P("rep", "fsdp", None),
        P("rep", "fsdp", None),
        P("rep", "fsdp", None),
        P("rep", "fsdp", None),
        P("rep", "fsdp", None),
        P("rep", "fsdp"),
        P("fsdp", None),
        P("fsdp", None),
        P("fsdp", None),
        P("fsdp", None),
        P("fsdp", None),
        P("fsdp"),
    )
    out_specs = (
        P(("rep", "dp", "fsdp"), None, None),
        P(("rep", "dp", "fsdp"), None, None),
        P("rep", "fsdp", None),
        P("rep", "fsdp", None),
        P("rep", "fsdp", None),
        P("rep", "fsdp", None),
        P("rep", "fsdp", None),
        P("rep", "fsdp"),
        P("rep", "fsdp", None),
        P("rep", "fsdp", None),
        P("rep", "fsdp", None),
        P("rep", "fsdp", None),
        P("rep", "fsdp", None),
        P("rep", "fsdp"),
        P("rep", "fsdp", None),
        P("rep", "fsdp", None),
        P("rep", "fsdp", None),
        P("rep", "fsdp", None),
        P("rep", "fsdp", None),
        P("rep", "fsdp"),
        P("fsdp", None),
        P("fsdp", None),
        P("fsdp", None),
        P("fsdp", None),
        P("fsdp", None),
        P("fsdp"),
        P("fsdp", None),
        P("fsdp", None),
        P("fsdp", None),
        P("fsdp", None),
        P("fsdp", None),
        P("fsdp"),
        P("fsdp", None),
        P("fsdp", None),
        P("fsdp", None),
        P("fsdp", None),
        P("fsdp", None),
        P("fsdp"),
    )
    return jax.shard_map(body, mesh=mesh, in_specs=in_specs, out_specs=out_specs, check_vma=False)
```

```python
import functools
import math

import jax
import jax.numpy as jnp
from jax import lax
from jax.experimental import pallas as pl
from jax.experimental.pallas import tpu as pltpu
from jax.sharding import PartitionSpec as P

D = 1152
HEADS = 16
FF = 4608


NORM_EPS = 1e-06
BETA_ONE = 0.9
BETA_TWO = 0.95
ADAM_EPS = 1e-08
WEIGHT_DECAY = 0.1
OUTER_RATE = 0.7
OUTER_MOMENTUM = 0.9
FEW = 8

F32 = jnp.float32
BF16 = jnp.bfloat16
SMALL = pl.CostEstimate(flops=1024, bytes_accessed=1024, transcendentals=0)


def dot(left, right):
    return jnp.dot(left, right, preferred_element_type=F32)


def dot_nt(left, right):
    return lax.dot_general(left, right, (((1,), (1,)), ((), ())), preferred_element_type=F32)


def dot_tn(left, right):
    return lax.dot_general(left, right, (((0,), (0,)), ((), ())), preferred_element_type=F32)


def time_embed(steps, width):
    half = width // 2
    frequency = jnp.exp(-math.log(10000.0) * jnp.arange(half).astype(F32) / half)
    angles = steps.astype(F32)[:, None] * frequency[None, :]
    return jnp.concatenate([jnp.cos(angles), jnp.sin(angles)], axis=1)


def learning_rates(width, hidden):
    return (
        2.0 / math.sqrt(width),
        2.0 / math.sqrt(width),
        2.0 / math.sqrt(width // 32),
        2.0 / math.sqrt(width),
        2.0 / math.sqrt(hidden),
        0.3,
    )


def shift_by(value, axis, step):
    size = lax.axis_size(axis)
    return lax.ppermute(value, axis, [(i, (i + step) % size) for i in range(size)])


def swap_with(value, axis, bit):
    size = lax.axis_size(axis)
    return lax.ppermute(value, axis, [(i, i ^ bit) for i in range(size)])


def gather_line(value, axis):
    size = lax.axis_size(axis)
    if size > FEW:
        return lax.all_gather(value, axis, axis=0)
    place = lax.axis_index(axis)
    result = jnp.zeros((size,) + value.shape, value.dtype)
    for step in range(size):
        piece = value if step == 0 else shift_by(value, axis, step)
        result = lax.dynamic_update_index_in_dim(result, piece, (place - step) % size, 0)
    return result


def scatter_line(value, axis):
    size = lax.axis_size(axis)
    if size > FEW:
        return lax.psum_scatter(value, axis, scatter_dimension=0, tiled=False)
    place = lax.axis_index(axis)
    total = lax.dynamic_index_in_dim(value, place, 0, keepdims=False)
    for step in range(1, size):
        piece = lax.dynamic_index_in_dim(value, (place + step) % size, 0, keepdims=False)
        total = total + shift_by(piece, axis, step)
    return total


def moments(values):
    center = values - jnp.mean(values, axis=-1, keepdims=True)
    inverse = lax.rsqrt(jnp.mean(center * center, axis=-1, keepdims=True) + NORM_EPS)
    return center * inverse, inverse


def norm_back(normed, inverse, upstream):
    first = jnp.mean(upstream, axis=-1, keepdims=True)
    second = jnp.mean(upstream * normed, axis=-1, keepdims=True)
    return (upstream - first - normed * second) * inverse


def gelu_pair(h):
    c = math.sqrt(2.0 / math.pi)
    inner = c * (h + 0.044715 * h * h * h)
    t = jnp.tanh(inner)
    value = 0.5 * h * (1.0 + t)
    slope = 0.5 * (1.0 + t) + 0.5 * h * (1.0 - t * t) * c * (1.0 + 3.0 * 0.044715 * h * h)
    return value, slope


def head_window(head, head_dim):
    low = head * head_dim
    start = low // 128 * 128
    stop = -(-(low + head_dim) // 128) * 128
    return start, stop, low - start


def head_mask(shape, offset, head_dim):
    lane = lax.broadcasted_iota(jnp.int32, shape, 1)
    return (lane >= offset) & (lane < offset + head_dim)


def attention_forward_kernel(
    x_ref, cot_ref, mod_ref, bias_ref, weight_ref,
    attn_in_ref, packed_ref, attended_ref, log_ref, attn_ref, x1_ref, mlp_in_ref, d_mlp_ref, sums_ref,
    gather_ref,
):
    length, width = x_ref.shape
    head_dim = width // HEADS
    factor = 1.0 / math.sqrt(head_dim)
    residual = x_ref[...].astype(F32)
    normed, _ = moments(residual)
    attn_in_ref[...] = (normed * (1.0 + mod_ref[0, 1:2]) + mod_ref[0, 0:1]).astype(BF16)
    for unit in range(3):
        piece = dot(attn_in_ref[...], weight_ref[unit]) + bias_ref[unit : unit + 1]
        packed_ref[:, unit * width : (unit + 1) * width] = piece.astype(BF16)
    for head in range(HEADS):
        start, stop, offset = head_window(head, head_dim)
        mask = head_mask((length, stop - start), offset, head_dim)
        query = packed_ref[:, start:stop]
        query = jnp.where(mask, query, jnp.zeros_like(query))
        keys = packed_ref[:, width + start : width + stop]
        values = packed_ref[:, 2 * width + start : 2 * width + stop]
        scores = dot_nt(query, keys) * factor
        top = jnp.max(scores, axis=-1, keepdims=True)
        raised = jnp.exp(scores - top)
        summed = jnp.sum(raised, axis=-1, keepdims=True)
        probs = (raised * (1.0 / summed)).astype(BF16)
        log_ref[:, head : head + 1] = top + jnp.log(summed)
        out = dot(probs, values)
        if offset == 0:
            gather_ref[:, start:stop] = out
        else:
            gather_ref[:, start:stop] = jnp.where(mask, out, gather_ref[:, start:stop])
    attended_ref[...] = gather_ref[...].astype(BF16)
    attn = dot(attended_ref[...], weight_ref[3]) + bias_ref[3:4]
    attn_ref[...] = attn
    middle = residual + mod_ref[0, 2:3] * attn
    x1_ref[...] = middle
    normed_two, _ = moments(middle)
    mlp_in_ref[...] = (normed_two * (1.0 + mod_ref[0, 4:5]) + mod_ref[0, 3:4]).astype(BF16)
    d_mlp = (mod_ref[0, 5:6] * (cot_ref[...].astype(F32) * mod_ref[0, 6:7])).astype(BF16)
    d_mlp_ref[...] = d_mlp
    sums_ref[0, 0:1] = jnp.sum(d_mlp.astype(F32), axis=0, keepdims=True)


def rows_spec(length, width):
    return pl.BlockSpec((length, width), lambda i: (i, 0))


def whole_spec(shape):
    return pl.BlockSpec(shape, lambda i: (0,) * len(shape), pipeline_mode=pl.Buffered(1))


def lead_spec(rows, width):
    return pl.BlockSpec((1, rows, width), lambda i: (i, 0, 0))


def params(megabytes):
    return pltpu.CompilerParams(vmem_limit_bytes=megabytes << 20)


def attention_forward(x, cot, mod, bias, weights, slots, length, width):
    tokens = slots * length
    row = rows_spec(length, width)
    return pl.pallas_call(
        attention_forward_kernel,
        grid=(slots,),
        in_specs=[row, row, lead_spec(8, width), whole_spec((8, width)), whole_spec((4, width, width))],
        out_specs=[
            row, rows_spec(length, 3 * width), row, rows_spec(length, 128), row, row, row, row,
            lead_spec(8, width),
        ],
        out_shape=[
            jax.ShapeDtypeStruct((tokens, width), BF16),
            jax.ShapeDtypeStruct((tokens, 3 * width), BF16),
            jax.ShapeDtypeStruct((tokens, width), BF16),
            jax.ShapeDtypeStruct((tokens, 128), F32),
            jax.ShapeDtypeStruct((tokens, width), F32),
            jax.ShapeDtypeStruct((tokens, width), F32),
            jax.ShapeDtypeStruct((tokens, width), BF16),
            jax.ShapeDtypeStruct((tokens, width), BF16),
            jax.ShapeDtypeStruct((slots, 8, width), F32),
        ],
        scratch_shapes=[pltpu.VMEM((length, width), F32)],
        compiler_params=params(48),
        cost_estimate=pl.CostEstimate(
            flops=2 * tokens * width * width * 4, bytes_accessed=40 << 20, transcendentals=0
        ),
    )(x, cot, mod, bias, weights)


def one_spec(joint):
    lines, rows, width = joint.shape[1], joint.shape[4], joint.shape[5]
    return pl.BlockSpec((1, lines, 2, 1, rows, width), lambda u: (u, 0, 0, 0, 0, 0))


def two_spec(joint):
    groups, lines, _, _, rows, width = joint.shape
    return pl.BlockSpec((groups, lines // groups, 2, 1, rows, width), lambda u: (0, u, 0, 1, 0, 0))


def one_of(ref):
    return ref[...].reshape(ref.shape[-1], ref.shape[-1])


def two_of(ref):
    value = ref[...]
    if value.shape[1] > 1:
        value = jnp.swapaxes(value, 0, 1)
    return value.reshape(ref.shape[-1], ref.shape[-1])


def hidden_kernel(mlp_in_ref, weight_ref, bias_ref, act_ref, slope_ref):
    step = 256

    def chunk(index, carry):
        here = pl.ds(pl.multiple_of(index * step, step), step)
        hidden = dot(mlp_in_ref[here, :], one_of(weight_ref)) + bias_ref[0:1]
        value, slope = gelu_pair(hidden)
        act_ref[here, :] = value.astype(BF16)
        slope_ref[here, :] = slope.astype(BF16)
        return carry

    lax.fori_loop(0, mlp_in_ref.shape[0] // step, chunk, 0)


def hidden_forward(mlp_in, weights, bias):
    tokens, width = mlp_in.shape
    units = weights.shape[0]
    column = pl.BlockSpec((tokens, width), lambda u: (0, u))
    return pl.pallas_call(
        hidden_kernel,
        grid=(units,),
        in_specs=[whole_spec((tokens, width)), one_spec(weights), pl.BlockSpec((1, width), lambda u: (0, u))],
        out_specs=[column, column],
        out_shape=[jax.ShapeDtypeStruct((tokens, units * width), BF16)] * 2,
        compiler_params=params(48),
        cost_estimate=pl.CostEstimate(
            flops=2 * tokens * width * width * units, bytes_accessed=26 << 20, transcendentals=0
        ),
    )(mlp_in, weights, bias)


def hidden_back_kernel(d_mlp_ref, weight_ref, slope_ref, d_hidden_ref, sums_ref):
    step = 256

    def chunk(index, carry):
        here = pl.ds(pl.multiple_of(index * step, step), step)
        d_hidden = dot_nt(d_mlp_ref[here, :], two_of(weight_ref)) * slope_ref[here, :].astype(F32)
        d_hidden = d_hidden.astype(BF16)
        d_hidden_ref[here, :] = d_hidden
        return carry + jnp.sum(d_hidden.astype(F32), axis=0, keepdims=True)

    zero = jnp.zeros((1, slope_ref.shape[1]), F32)
    sums_ref[0:1] = lax.fori_loop(0, d_mlp_ref.shape[0] // step, chunk, zero)


def hidden_back(d_mlp, weights, slope):
    tokens, width = d_mlp.shape
    units = weights.shape[0]
    column = pl.BlockSpec((tokens, width), lambda u: (0, u))
    return pl.pallas_call(
        hidden_back_kernel,
        grid=(units,),
        in_specs=[whole_spec((tokens, width)), two_spec(weights), column],
        out_specs=[column, pl.BlockSpec((8, width), lambda u: (0, u))],
        out_shape=[
            jax.ShapeDtypeStruct((tokens, units * width), BF16),
            jax.ShapeDtypeStruct((8, units * width), F32),
        ],
        compiler_params=params(48),
        cost_estimate=pl.CostEstimate(
            flops=2 * tokens * width * width * units, bytes_accessed=26 << 20, transcendentals=0
        ),
    )(d_mlp, weights, slope)


def mlp_rest_kernel(act_ref, d_hidden_ref, two_ref, one_ref, mlp_ref, d_in_ref):
    step = 256

    @pl.when(pl.program_id(0) == 0)
    def _():
        mlp_ref[...] = jnp.zeros_like(mlp_ref)
        d_in_ref[...] = jnp.zeros_like(d_in_ref)

    def chunk(index, carry):
        here = pl.ds(pl.multiple_of(index * step, step), step)
        mlp_ref[here, :] += dot(act_ref[here, :], two_of(two_ref))
        d_in_ref[here, :] += dot_nt(d_hidden_ref[here, :], one_of(one_ref))
        return carry

    lax.fori_loop(0, act_ref.shape[0] // step, chunk, 0)


def mlp_rest(act, d_hidden, weights):
    tokens = act.shape[0]
    units, width = weights.shape[0], weights.shape[-1]
    column = pl.BlockSpec((tokens, width), lambda u: (0, u))
    total = pl.BlockSpec((tokens, width), lambda u: (0, 0))
    return pl.pallas_call(
        mlp_rest_kernel,
        grid=(units,),
        in_specs=[column, column, two_spec(weights), one_spec(weights)],
        out_specs=[total, total],
        out_shape=[jax.ShapeDtypeStruct((tokens, width), F32)] * 2,
        compiler_params=params(48),
        cost_estimate=pl.CostEstimate(
            flops=4 * tokens * width * width * units, bytes_accessed=42 << 20, transcendentals=0
        ),
    )(act, d_hidden, weights, weights)


def middle_back_kernel(
    mlp_ref, bias_ref, d_in_ref, x1_ref, attn_ref, cot_ref, mod_ref, weight_ref,
    out_ref, d_mid_ref, d_attn_ref, d_att_ref, rows_ref,
):
    live = mod_ref[0, 6:7]
    gate_two = mod_ref[0, 5:6]
    upstream = cot_ref[...].astype(F32) * live
    middle = x1_ref[...]
    mlp = mlp_ref[...] + bias_ref[4:5]
    out_ref[...] = ((middle + gate_two * mlp) * live).astype(BF16)
    rows_ref[0, 5:6] = jnp.sum(upstream * mlp, axis=0, keepdims=True)
    normed, inverse = moments(middle)
    d_in = d_in_ref[...]
    rows_ref[0, 3:4] = jnp.sum(d_in, axis=0, keepdims=True)
    rows_ref[0, 4:5] = jnp.sum(d_in * normed, axis=0, keepdims=True)
    d_mid = upstream + norm_back(normed, inverse, d_in * (1.0 + mod_ref[0, 4:5]))
    d_mid_ref[...] = d_mid
    rows_ref[0, 2:3] = jnp.sum(d_mid * attn_ref[...], axis=0, keepdims=True)
    d_attn = (mod_ref[0, 2:3] * d_mid).astype(BF16)
    d_attn_ref[...] = d_attn
    rows_ref[0, 6:7] = jnp.sum(d_attn.astype(F32), axis=0, keepdims=True)
    d_att_ref[...] = dot_nt(d_attn_ref[...], weight_ref[0]).astype(BF16)


def middle_back(mlp, bias, d_in, x1, attn, cot, mod, weights, slots, length, width):
    tokens = slots * length
    row = rows_spec(length, width)
    proj = pl.BlockSpec((1, width, width), lambda i: (3, 0, 0), pipeline_mode=pl.Buffered(1))
    return pl.pallas_call(
        middle_back_kernel,
        grid=(slots,),
        in_specs=[row, whole_spec((8, width)), row, row, row, row, lead_spec(8, width), proj],
        out_specs=[row, row, row, row, lead_spec(8, width)],
        out_shape=[
            jax.ShapeDtypeStruct((tokens, width), BF16),
            jax.ShapeDtypeStruct((tokens, width), F32),
            jax.ShapeDtypeStruct((tokens, width), BF16),
            jax.ShapeDtypeStruct((tokens, width), BF16),
            jax.ShapeDtypeStruct((slots, 8, width), F32),
        ],
        compiler_params=params(48),
        cost_estimate=pl.CostEstimate(
            flops=2 * tokens * width * width, bytes_accessed=30 << 20, transcendentals=0
        ),
    )(mlp, bias, d_in, x1, attn, cot, mod, weights)


def attention_back_kernel(packed_ref, d_att_ref, log_ref, d_packed_ref, sums_ref, q_ref, k_ref, v_ref):
    length, width = d_att_ref.shape
    head_dim = width // HEADS
    factor = 1.0 / math.sqrt(head_dim)
    for head in range(HEADS):
        start, stop, offset = head_window(head, head_dim)
        mask = head_mask((length, stop - start), offset, head_dim)
        query = packed_ref[:, start:stop]
        query_one = jnp.where(mask, query, jnp.zeros_like(query))
        keys = packed_ref[:, width + start : width + stop]
        values = packed_ref[:, 2 * width + start : 2 * width + stop]
        d_att = d_att_ref[:, start:stop]
        d_att = jnp.where(mask, d_att, jnp.zeros_like(d_att))
        weights = jnp.exp(dot_nt(query_one, keys) * factor - log_ref[:, head : head + 1])
        d_probs = dot_nt(d_att, values)
        inner = jnp.sum(weights * d_probs, axis=-1, keepdims=True)
        d_scores = (weights * (d_probs - inner)).astype(BF16)
        probs = weights.astype(BF16)
        pieces = (
            (q_ref, dot(d_scores, keys) * factor),
            (k_ref, dot_tn(d_scores, query) * factor),
            (v_ref, dot_tn(probs, d_att)),
        )
        for ref, piece in pieces:
            if offset == 0:
                ref[:, start:stop] = piece
            else:
                ref[:, start:stop] = jnp.where(mask, piece, ref[:, start:stop])
    for unit, ref in enumerate((q_ref, k_ref, v_ref)):
        piece = ref[...].astype(BF16)
        d_packed_ref[:, unit * width : (unit + 1) * width] = piece
        sums_ref[0, unit : unit + 1] = jnp.sum(piece.astype(F32), axis=0, keepdims=True)


def attention_back(packed, d_att, log, slots, length, width):
    tokens = slots * length
    return pl.pallas_call(
        attention_back_kernel,
        grid=(slots,),
        in_specs=[rows_spec(length, 3 * width), rows_spec(length, width), rows_spec(length, 128)],
        out_specs=[rows_spec(length, 3 * width), lead_spec(8, width)],
        out_shape=[
            jax.ShapeDtypeStruct((tokens, 3 * width), BF16),
            jax.ShapeDtypeStruct((slots, 8, width), F32),
        ],
        scratch_shapes=[pltpu.VMEM((length, width), F32)] * 3,
        compiler_params=params(48),
        cost_estimate=pl.CostEstimate(
            flops=10 * tokens * length * 256 * HEADS, bytes_accessed=14 << 20, transcendentals=0
        ),
    )(packed, d_att, log)


def input_back_kernel(d_packed_ref, weight_ref, x_ref, d_mid_ref, mod_ref, grad_ref, rows_ref):
    width = x_ref.shape[1]
    d_in = dot_nt(d_packed_ref[:, :width], weight_ref[0])
    for unit in (1, 2):
        d_in = d_in + dot_nt(d_packed_ref[:, unit * width : (unit + 1) * width], weight_ref[unit])
    normed, inverse = moments(x_ref[...].astype(F32))
    rows_ref[0, 0:1] = jnp.sum(d_in, axis=0, keepdims=True)
    rows_ref[0, 1:2] = jnp.sum(d_in * normed, axis=0, keepdims=True)
    back = norm_back(normed, inverse, d_in * (1.0 + mod_ref[0, 1:2]))
    grad_ref[...] = (d_mid_ref[...] + back).astype(BF16)


def input_back(d_packed, weights, x, d_mid, mod, slots, length, width):
    tokens = slots * length
    row = rows_spec(length, width)
    return pl.pallas_call(
        input_back_kernel,
        grid=(slots,),
        in_specs=[
            rows_spec(length, 3 * width), whole_spec((3, width, width)), row, row, lead_spec(8, width),
        ],
        out_specs=[row, lead_spec(8, width)],
        out_shape=[
            jax.ShapeDtypeStruct((tokens, width), BF16),
            jax.ShapeDtypeStruct((slots, 8, width), F32),
        ],
        compiler_params=params(48),
        cost_estimate=pl.CostEstimate(
            flops=6 * tokens * width * width, bytes_accessed=20 << 20, transcendentals=0
        ),
    )(d_packed, weights, x, d_mid, mod)


def grad_kernel(left_ref, right_ref, grad_ref):
    step = grad_ref.shape[0] // 3

    def chunk(index, carry):
        here = pl.ds(pl.multiple_of(index * step, step), step)
        grad_ref[here, :] = dot_tn(left_ref[:, here], right_ref[...]).astype(BF16)
        return carry

    lax.fori_loop(0, 3, chunk, 0)


def grad_columns(left, right):
    tokens, rows = left.shape
    width = right.shape[1]
    return pl.pallas_call(
        grad_kernel,
        grid=(width // rows,),
        in_specs=[whole_spec((tokens, rows)), pl.BlockSpec((tokens, rows), lambda u: (0, u))],
        out_specs=pl.BlockSpec((rows, rows), lambda u: (0, u)),
        out_shape=jax.ShapeDtypeStruct((rows, width), BF16),
        compiler_params=params(48),
        cost_estimate=pl.CostEstimate(
            flops=2 * tokens * rows * width, bytes_accessed=2 * rows * width + 4 * tokens * width, transcendentals=0
        ),
    )(left, right)


def grad_rows(left, right):
    tokens, rows = left.shape
    width = right.shape[1]
    return pl.pallas_call(
        grad_kernel,
        grid=(rows // width,),
        in_specs=[pl.BlockSpec((tokens, width), lambda u: (0, u)), whole_spec((tokens, width))],
        out_specs=rows_spec(width, width),
        out_shape=jax.ShapeDtypeStruct((rows, width), BF16),
        compiler_params=params(48),
        cost_estimate=pl.CostEstimate(
            flops=2 * tokens * rows * width, bytes_accessed=2 * rows * width + 4 * tokens * rows, transcendentals=0
        ),
    )(left, right)


def after(*values):
    return lax.optimization_barrier(values)


def adam_moments(first, second, gradient):
    first_next = BETA_ONE * first + (1.0 - BETA_ONE) * gradient
    second_next = BETA_TWO * second + (1.0 - BETA_TWO) * gradient * gradient
    return first_next, second_next


def adam_delta(master, first_next, second_next, rate, fix_one, fix_two):
    step = first_next / fix_one / (jnp.sqrt(second_next / fix_two) + ADAM_EPS)
    return (rate * (step + WEIGHT_DECAY * master)).astype(BF16)


def whole_kernel(mode, rate, where_ref, fix_ref, *refs):
    half = pl.program_id(2)
    if mode == "sum":
        a_ref, b_ref, master_ref, first_ref, second_ref, grad_ref, m_ref, v_ref, keep_ref, give_ref = refs
        gradient = a_ref[0].astype(F32) + b_ref[0].astype(F32)
        grad_ref[0] = gradient
    elif mode == "given":
        g_ref, master_ref, first_ref, second_ref, m_ref, v_ref, keep_ref, give_ref = refs
        gradient = g_ref[0]
    else:
        own_ref, other_ref, first_ref, second_ref, grad_ref, m_ref, v_ref = refs
        gradient = jnp.where(half == where_ref[0], own_ref[...].astype(F32), other_ref[...].astype(F32))
        grad_ref[0] = gradient
    first_next, second_next = adam_moments(first_ref[0], second_ref[0], gradient)
    m_ref[0] = first_next
    v_ref[0] = second_next
    if mode != "halves":
        delta = adam_delta(master_ref[0], first_next, second_next, rate, fix_ref[0], fix_ref[1])

        @pl.when(half == where_ref[1])
        def _():
            keep_ref[...] = delta

        @pl.when(half != where_ref[1])
        def _():
            give_ref[...] = delta


def row_block(rows):
    return 144 if rows % 144 == 0 else rows


def adam_whole(mode, where, fixes, gradients, master, first, second, rate, shift=0):
    rows, columns = master.shape
    half, width = rows // 2, D
    block = row_block(half)
    three = pl.BlockSpec((1, block, width), lambda c, r, h, w: (h, r, c))
    flat = pl.BlockSpec((block, width), lambda c, r, h, w: (r, c))
    moved = pl.BlockSpec((block, width), lambda c, r, h, w: (r, c + shift))
    view = (2, half, columns)
    state = [first.reshape(view), second.reshape(view)]
    if mode == "halves":
        operands = list(gradients) + state
        in_specs = [moved, moved, three, three]
    else:
        operands = [g.reshape(view) for g in gradients] + [master.reshape(view)] + state
        in_specs = [three] * len(operands)
    wide = jax.ShapeDtypeStruct(view, F32)
    thin = jax.ShapeDtypeStruct((half, columns), BF16)
    count = 2 if mode == "given" else 3
    extra = 0 if mode == "halves" else 2
    outs = pl.pallas_call(
        functools.partial(whole_kernel, mode, rate),
        grid_spec=pltpu.PrefetchScalarGridSpec(
            num_scalar_prefetch=1,
            grid=(columns // width, half // block, 2),
            in_specs=[pl.BlockSpec(memory_space=pltpu.SMEM)] + in_specs,
            out_specs=[three] * count + [flat] * extra,
        ),
        out_shape=[wide] * count + [thin] * extra,
        compiler_params=params(48),
        cost_estimate=SMALL,
    )(where, fixes, *operands)
    return [out.reshape(1, rows, columns) for out in outs[:count]] + list(outs[count:])


def own_kernel(rates, where_ref, fix_ref, g_ref, *refs):
    states, keep_ref, give_ref = refs[:-2], refs[-2], refs[-1]
    unit, core = pl.program_id(0), pl.program_id(1)

    def run(kind):
        master_ref, first_ref, second_ref = states[3 * kind : 3 * kind + 3]
        first_next, second_next = adam_moments(first_ref[0, 0], second_ref[0, 0], g_ref[0].astype(F32))
        delta = adam_delta(
            master_ref[0, 0], first_next, second_next, rates[kind][1], fix_ref[0], fix_ref[1]
        )

        @pl.when(core == where_ref[1])
        def _():
            keep_ref[...] = delta

        @pl.when(core != where_ref[1])
        def _():
            give_ref[...] = delta

    start = 0
    for kind, (units, _) in enumerate(rates):
        stop = start + units

        @pl.when((unit >= start) & (unit < stop))
        def _():
            run(kind)

        start = stop


def adam_own(where, fixes, gradient, weights):
    half, columns = gradient.shape
    quarter, width = half // 2, D
    operands, in_specs, rates = [gradient.reshape(2, quarter, columns)], [], []
    in_specs.append(pl.BlockSpec((1, quarter, width), lambda c, h, w: (h, 0, c)))
    start = 0
    for master, first, second, rate in weights:
        units = master.shape[1] // width
        low = start

        def place(c, h, w, low=low, units=units):
            return (w[0], h, 0, jnp.clip(c - low, 0, units - 1))

        for value in (master, first, second):
            operands.append(value.reshape(2, 2, quarter, value.shape[-1]))
            in_specs.append(pl.BlockSpec((1, 1, quarter, width), place))
        rates.append((units, rate))
        start += units
    flat = pl.BlockSpec((quarter, width), lambda c, h, w: (0, c))
    return pl.pallas_call(
        functools.partial(own_kernel, tuple(rates)),
        grid_spec=pltpu.PrefetchScalarGridSpec(
            num_scalar_prefetch=1,
            grid=(columns // width, 2),
            in_specs=[pl.BlockSpec(memory_space=pltpu.SMEM)] + in_specs,
            out_specs=[flat, flat],
        ),
        out_shape=[jax.ShapeDtypeStruct((quarter, columns), BF16)] * 2,
        compiler_params=params(48),
        cost_estimate=SMALL,
    )(where, fixes, *operands)


def outer_kernel(scale, where_ref, *refs):
    totals, master_ref, outer_ref, delta_ref, next_ref, weight_ref = refs[:-5], *refs[-5:]
    core = pl.program_id(2)
    if len(totals) == 2:
        own, other = totals[0][...], totals[1][...]
    else:
        mine = pl.program_id(1) == where_ref[0]
        own = jnp.where(mine, totals[0][...], totals[1][...])
        other = jnp.where(mine, totals[2][...], totals[3][...])
    delta = jnp.where(core == where_ref[1], own.astype(F32), other.astype(F32)) * scale
    outer_next = OUTER_MOMENTUM * outer_ref[...].reshape(delta.shape) + delta
    master = master_ref[...].reshape(delta.shape)
    delta_ref[...] = delta.reshape(delta_ref.shape)
    next_ref[...] = outer_next.reshape(next_ref.shape)
    weight = master - OUTER_RATE * (delta + OUTER_MOMENTUM * outer_next)
    weight_ref[...] = weight.reshape(weight_ref.shape)


def outer_whole(where, totals, master, outer, groups, shift=0):
    rows, columns = master.shape
    width = D
    if len(totals) == 2:
        part = rows // 2
        block = row_block(part)
        view = (2, part, columns)
        grid = (columns // width, part // block, 2)
        state = pl.BlockSpec((1, block, width), lambda c, r, h, w: (h, r, c))
        total = pl.BlockSpec((block, width), lambda c, r, h, w: (r, c + shift))
    else:
        part = rows // 4
        view = (2, 2, part, columns)
        grid = (columns // width, 2, 2)
        state = pl.BlockSpec((1, 1, part, width), lambda c, p, h, w: (p, h, 0, c))
        total = pl.BlockSpec((part, width), lambda c, p, h, w: (0, c + shift))
    outs = pl.pallas_call(
        functools.partial(outer_kernel, 1.0 / groups),
        grid_spec=pltpu.PrefetchScalarGridSpec(
            num_scalar_prefetch=1,
            grid=grid,
            in_specs=[total] * len(totals) + [state, state],
            out_specs=[state] * 3,
        ),
        out_shape=[jax.ShapeDtypeStruct(view, F32)] * 3,
        compiler_params=params(48),
        cost_estimate=SMALL,
    )(where, *totals, master.reshape(view), outer.reshape(view))
    return [out.reshape(rows, columns) for out in outs]


def place_kernel(order_ref, *refs):
    sources, target, held, came, left = refs[:-4], refs[-4], refs[-3], refs[-2], refs[-1]
    inward, outward = [], []
    for which, source in enumerate(sources):
        for block in range(source.shape[0]):
            index = which * source.shape[0] + block
            inward.append(pltpu.make_async_copy(source.at[block], held.at[index], came.at[index]))
            outward.append(
                pltpu.make_async_copy(held.at[index], target.at[order_ref[index]], left.at[index])
            )
    for copy in inward:
        copy.start()
    for first, second in zip(inward, outward):
        first.wait()
        second.start()
    for copy in outward:
        copy.wait()


def place_blocks(order, sources):
    blocks = sum(source.shape[0] for source in sources)
    shape = (blocks,) + sources[0].shape[1:]
    return pl.pallas_call(
        place_kernel,
        grid_spec=pltpu.PrefetchScalarGridSpec(
            num_scalar_prefetch=1,
            grid=(1,),
            in_specs=[pl.BlockSpec(memory_space=pl.ANY)] * len(sources),
            out_specs=pl.BlockSpec(memory_space=pl.ANY),
            scratch_shapes=[
                pltpu.VMEM(shape, sources[0].dtype),
                pltpu.SemaphoreType.DMA((blocks,)),
                pltpu.SemaphoreType.DMA((blocks,)),
            ],
        ),
        out_shape=jax.ShapeDtypeStruct(shape, sources[0].dtype),
        compiler_params=params(48),
        cost_estimate=pl.CostEstimate(
            flops=0, bytes_accessed=4 * blocks * shape[1] * shape[2], transcendentals=0
        ),
    )(order, *sources)


def hops_line(piece):
    near = jnp.stack([piece, shift_by(piece, "fsdp", 1)])
    far = jnp.stack([shift_by(piece, "fsdp", 2), shift_by(piece, "fsdp", 3)])
    return near, far


def hops_side(near, far):
    near = jnp.concatenate([near, swap_with(near, "rep", 2)])
    far = jnp.concatenate([far, swap_with(far, "dp", 1)])
    return near, far


def hops_other(near, far):
    return near, far, swap_with(near, "dp", 1), swap_with(far, "rep", 2)


def hops_core(sources):
    return tuple(sources) + tuple(swap_with(source, "rep", 1) for source in sources)


def hops_place(sources, weigh):
    size = lax.axis_size("fsdp")
    rep, pair, line = lax.axis_index("rep"), lax.axis_index("dp"), lax.axis_index("fsdp")
    order = []
    for core in (0, 1):
        for kind in range(4):
            for block in range(4):
                hop, step = block // 2, block % 2
                if kind in (0, 2):
                    flip_rep, flip_pair, back = hop, kind // 2, step
                else:
                    flip_rep, flip_pair, back = kind // 2, hop, 2 + step
                place = lax.rem(line - back + size, size) * weigh[0]
                place = place + (rep ^ (2 * flip_rep + core)) * weigh[1] + (pair ^ flip_pair) * weigh[2]
                order.append(place)
    return place_blocks(jnp.stack(order).astype(jnp.int32), sources)


def own_half(value, index):
    return lax.dynamic_index_in_dim(value, index, 1, keepdims=False)


def body(
    images,
    cotangent,
    counts,
    timesteps,
    labels,
    label_table,
    step_count,
    w_ada,
    w_qkv,
    w_proj,
    w_fc1,
    w_fc2,
    biases,
    first_ada,
    first_qkv,
    first_proj,
    first_fc1,
    first_fc2,
    first_bias,
    second_ada,
    second_qkv,
    second_proj,
    second_fc1,
    second_fc2,
    second_bias,
    outer_ada,
    outer_qkv,
    outer_proj,
    outer_fc1,
    outer_fc2,
    outer_bias,
):
    masters = (w_ada, w_qkv, w_proj, w_fc1, w_fc2, biases)
    firsts = (first_ada, first_qkv, first_proj, first_fc1, first_fc2, first_bias)
    seconds = (second_ada, second_qkv, second_proj, second_fc1, second_fc2, second_bias)
    outers = (outer_ada, outer_qkv, outer_proj, outer_fc1, outer_fc2, outer_bias)
    slots, length, width = images.shape
    tokens = slots * length
    rows = w_qkv.shape[0]
    rows_two = w_fc2.shape[0]
    lines = lax.axis_size("fsdp")
    groups = lax.axis_size("rep")
    rep = lax.axis_index("rep")
    pair = lax.axis_index("dp")
    line = lax.axis_index("fsdp")
    half = rows // 2
    everyone = ("rep", "fsdp", "dp")

    def rows_of(weight):
        return lax.dynamic_slice_in_dim(weight, pair * half, half, axis=0).astype(BF16)

    attention_cut = jnp.concatenate([rows_of(w_qkv), rows_of(w_proj)], axis=1)
    attention_cut = lax.dynamic_slice_in_dim(attention_cut, rep * width, width, axis=1)
    hops = lines == 4 and groups == 4
    one_cut = lax.dynamic_slice(w_fc1, (pair * half, rep * width), (half, width))
    eighth = rows_two // (2 * groups)
    two_cut = lax.dynamic_slice_in_dim(w_fc2, (rep * 2 + pair) * eighth, eighth, axis=0)
    mlp_cut = jnp.concatenate([one_cut, two_cut]).astype(BF16)
    w_mlp = lax.all_gather(mlp_cut, everyone, axis=0, tiled=True)
    w_mlp = w_mlp.reshape(groups, lines, 2, 2, half, width)
    live = (jnp.arange(slots) < counts[0]).astype(F32)
    condition = time_embed(timesteps, D) + jnp.take(label_table, labels, axis=0).astype(F32)
    style = jax.nn.silu(condition).astype(BF16)
    message = jnp.concatenate([style.reshape(-1), biases.astype(BF16)])
    heard = gather_line(message, "fsdp")
    if hops:
        attention_cut, message = after(attention_cut, message)
        attention_parts = hops_line(attention_cut)
        heard = after(heard, *attention_parts)[0]
        attention_parts = hops_side(*attention_parts)
    else:
        w_attn = lax.all_gather(attention_cut, everyone, axis=0, tiled=True)
    bias_all = heard[:, slots * width :].reshape(-1).astype(F32)
    style_line = heard[:, : slots * width].reshape(lines * slots, width)
    style_cut = lax.dynamic_slice_in_dim(style_line, line * rows, rows, axis=1)
    mod_part = dot(style_cut, w_ada.astype(BF16))
    if hops:
        attention_parts = hops_other(*attention_parts)
        attention_parts = after(*attention_parts, mod_part)[:-1]
        w_attn = hops_place(hops_core(attention_parts), (2, 8, 1))
    w_attn = w_attn.reshape(4, width, width)
    b_ada = bias_all[: 6 * width]
    modulation = scatter_line(mod_part.reshape(lines, slots, 6 * width), "fsdp") + b_ada
    mod = jnp.concatenate(
        [
            modulation.reshape(slots, 6, width),
            jnp.broadcast_to(live[:, None, None], (slots, 2, width)),
        ],
        axis=1,
    )
    b_rest = bias_all[6 * width : 9 * width].reshape(3, width)
    bias = jnp.zeros((8, width), F32)
    bias = bias.at[0].set(b_rest[0]).at[2].set(b_rest[1]).at[3].set(b_rest[2])
    bias = bias.at[4].set(bias_all[9 * width + FF :])
    b_fc1 = bias_all[9 * width : 9 * width + FF].reshape(1, FF)
    x = images.reshape(tokens, width)
    cot = cotangent.reshape(tokens, width)

    attn_in, packed, attended, log_total, attn_out, middle, mlp_in, d_mlp, mlp_sums = attention_forward(
        x, cot, mod, bias, w_attn, slots, length, width
    )
    activated, slope = hidden_forward(mlp_in, w_mlp, b_fc1)
    grad_two = grad_rows(activated, d_mlp)

    def halves(gradient):
        return gradient.reshape(lines, 2, gradient.shape[0] // (2 * lines), gradient.shape[1])

    def line_sum(both):
        return lax.psum_scatter(
            both.reshape(-1, both.shape[-1]), "fsdp", scatter_dimension=0, tiled=True
        )

    def pair_sum(gradient, there):
        return (own_half(halves(gradient), pair).astype(F32) + there.astype(F32)).astype(BF16)

    grad_two, d_mlp = after(grad_two, d_mlp)
    two_line = line_sum(grad_two)
    d_hidden, hidden_sums = hidden_back(d_mlp, w_mlp, slope)
    grad_one = grad_columns(mlp_in, d_hidden)
    give_one = own_half(halves(grad_one), 1 - pair)
    give_one, d_hidden = after(give_one, d_hidden)
    there_one = swap_with(give_one, "dp", 1)
    mlp_out, d_mlp_in = mlp_rest(activated, d_hidden, w_mlp)
    result, d_middle, d_attn, d_attended, middle_rows = middle_back(
        mlp_out, bias, d_mlp_in, middle, attn_out, cot, mod, w_attn, slots, length, width
    )
    grad_proj = grad_columns(attended, d_attn)
    grad_proj, d_attended = after(grad_proj, d_attended)
    d_packed, packed_sums = attention_back(packed, d_attended, log_total, slots, length, width)
    grad_qkv = grad_columns(attn_in, d_packed)
    give_attn = own_half(halves(grad_qkv), 1 - pair)
    give_proj = own_half(halves(grad_proj), 1 - pair)
    give_attn, give_proj, d_packed = after(give_attn, give_proj, d_packed)
    there_proj = swap_with(give_proj, "dp", 1)
    in_grad, input_rows = input_back(d_packed, w_attn, x, d_middle, mod, slots, length, width)

    there_one, give_attn, in_grad, input_rows = after(there_one, give_attn, in_grad, input_rows)
    there_attn = swap_with(give_attn, "dp", 1)
    one_both = pair_sum(grad_one, there_one)
    one_half = line_sum(one_both)
    two_line, one_both, there_proj, input_rows = after(two_line, one_both, there_proj, input_rows)

    d_modulation = jnp.concatenate([input_rows[:, :2], middle_rows[:, 2:6]], axis=1).astype(BF16)
    packed_total = jnp.sum(packed_sums, axis=0)
    bias_sums = jnp.concatenate(
        [
            packed_total[0],
            packed_total[2],
            jnp.sum(middle_rows[:, 6], axis=0),
            hidden_sums[0],
            jnp.sum(mlp_sums[:, 0], axis=0),
        ]
    ).astype(BF16)

    report = jnp.concatenate([style.reshape(-1), d_modulation.reshape(-1), bias_sums])
    report = jnp.stack([report, swap_with(report, "dp", 1)])
    reports = gather_line(report, "fsdp").reshape(2 * lines, -1)
    edge = slots * width
    style_group = reports[:, :edge].reshape(2 * lines * slots, width)
    mod_group = reports[:, edge : 7 * edge].reshape(2 * lines * slots, 6 * width)
    style_own = lax.dynamic_slice_in_dim(style_group, line * rows, rows, axis=1)
    grad_ada = dot_tn(style_own, mod_group)
    bias_group = jnp.concatenate(
        [
            jnp.sum(mod_group.astype(F32), axis=0),
            jnp.sum(reports[:, 7 * edge :].astype(F32), axis=0),
        ]
    )
    own_bias = biases.shape[0]
    grad_bias = lax.dynamic_slice_in_dim(bias_group, line * own_bias, own_bias, axis=0)

    power = step_count[0].astype(F32)
    fix_one = 1.0 - jnp.power(BETA_ONE, power)
    fix_two = 1.0 - jnp.power(BETA_TWO, power)
    rates = learning_rates(D, FF)
    reduced = [None] * 6
    firsts_out = [None] * 6
    seconds_out = [None] * 6
    deltas_out = [None] * 6
    outers_out = [None] * 6
    weights_out = [None] * 6

    low = rep % 2
    where = jnp.stack([pair, low]).astype(jnp.int32)
    fixes = jnp.stack([fix_one, fix_two])

    def local_delta(master, first, second, gradient, rate):
        first_next, second_next = adam_moments(first, second, gradient)
        delta = adam_delta(master, first_next, second_next, rate, fix_one, fix_two)
        return delta, first_next, second_next

    def state(index):
        return masters[index], firsts[index][0], seconds[index][0], rates[index]

    def sum_near(keep, give):
        return (keep.astype(F32) + swap_with(give, "rep", 1).astype(F32)).astype(BF16)

    def sum_far(total):
        return (total.astype(F32) + swap_with(total, "rep", 2).astype(F32)).astype(BF16)

    def outer_step(index, totals, shift=0):
        deltas_out[index], outers_out[index], weights_out[index] = outer_whole(
            where, totals, masters[index], outers[index], groups, shift
        )

    reduced[0] = grad_ada
    firsts_out[0], seconds_out[0], ada_keep, ada_give = adam_whole(
        "given", where, fixes, [grad_ada], *state(0)
    )
    one_half, there_attn, two_line, ada_keep, ada_give, grad_bias = after(
        one_half, there_attn, two_line, ada_keep, ada_give, grad_bias
    )
    attn_both = jnp.concatenate(
        [pair_sum(grad_qkv, there_attn), pair_sum(grad_proj, there_proj)], axis=2
    )
    attn_both, two_line, one_half, ada_give, grad_bias = after(
        attn_both, two_line, one_half, ada_give, grad_bias
    )
    attn_half = line_sum(attn_both)
    ada_total = sum_far(sum_near(ada_keep, ada_give))
    one_total = sum_far(sum_near(*adam_own(where, fixes, one_half, [state(3)])))
    two_there = swap_with(two_line, "dp", 1)
    two_there, one_half = after(two_there, one_half)
    one_there = swap_with(one_half, "dp", 1)
    outer_step(0, [ada_total, swap_with(ada_total, "rep", 1)])
    two_there, weights_out[0], one_total = after(two_there, weights_out[0], one_total)
    one_pair = swap_with(one_total, "dp", 1)
    reduced[4], firsts_out[4], seconds_out[4], two_keep, two_give = adam_whole(
        "sum", where, fixes, [two_line, two_there], *state(4)
    )
    bias_delta, bias_first, bias_second = local_delta(
        biases, first_bias[0], second_bias[0], grad_bias, rates[5]
    )
    reduced[5] = grad_bias
    firsts_out[5], seconds_out[5] = bias_first[None], bias_second[None]
    bias_total = (bias_delta.astype(F32) + swap_with(bias_delta, "rep", 1).astype(F32)).astype(BF16)
    bias_total = bias_total.astype(F32) + swap_with(bias_total, "rep", 2).astype(F32)
    deltas_out[5] = bias_total / groups
    outers_out[5] = OUTER_MOMENTUM * outer_bias + deltas_out[5]
    weights_out[5] = biases - OUTER_RATE * (deltas_out[5] + OUTER_MOMENTUM * outers_out[5])
    attn_half, two_keep, two_give = after(attn_half, two_keep, two_give, one_pair, one_there)[:3]
    attn_near = sum_near(*adam_own(where, fixes, attn_half, [state(1), state(2)]))
    attn_there = swap_with(attn_half, "dp", 1)
    attn_far = swap_with(attn_near, "rep", 2)
    reduced[3], firsts_out[3], seconds_out[3] = adam_whole(
        "halves", where, fixes, [one_half, one_there], *state(3)
    )
    attn_far, attn_there, firsts_out[3] = after(attn_far, attn_there, firsts_out[3])
    attn_total = (attn_near.astype(F32) + attn_far.astype(F32)).astype(BF16)
    attn_pair = swap_with(attn_total, "dp", 1)
    two_near, attn_total = after(sum_near(two_keep, two_give), attn_total)
    two_far = swap_with(two_near, "rep", 2)
    outer_step(
        3, [one_total, one_pair, swap_with(one_total, "rep", 1), swap_with(one_pair, "rep", 1)]
    )
    attn_pair, weights_out[3] = after(attn_pair, weights_out[3])
    attn_units = 3
    for index, shift in ((1, 0), (2, attn_units)):
        reduced[index], firsts_out[index], seconds_out[index] = adam_whole(
            "halves", where, fixes, [attn_half, attn_there], *state(index), shift=shift
        )
    two_far, firsts_out[1], firsts_out[2], weights_out[3] = after(
        two_far, firsts_out[1], firsts_out[2], weights_out[3]
    )
    two_total = (two_near.astype(F32) + two_far.astype(F32)).astype(BF16)
    outer_step(4, [two_total, swap_with(two_total, "rep", 1)])
    totals = [attn_total, attn_pair, swap_with(attn_total, "rep", 1), swap_with(attn_pair, "rep", 1)]
    outer_step(1, totals)
    outer_step(2, totals, attn_units)
    grads_out = tuple((g if g.ndim == f.ndim else g[None] for g, f in zip(reduced, firsts)))
    return (
        (result.reshape(images.shape), in_grad.reshape(images.shape))
        + grads_out
        + tuple(firsts_out)
        + tuple(seconds_out)
        + tuple(deltas_out)
        + tuple(outers_out)
        + tuple(weights_out)
    )


def solution(mesh):
    in_specs = (
        P(("rep", "dp", "fsdp"), None, None),
        P(("rep", "dp", "fsdp"), None, None),
        P(("rep", "dp", "fsdp")),
        P(("rep", "dp", "fsdp")),
        P(("rep", "dp", "fsdp")),
        P(),
        P(),
        P("fsdp", None),
        P("fsdp", None),
        P("fsdp", None),
        P("fsdp", None),
        P("fsdp", None),
        P("fsdp"),
        P("rep", "fsdp", None),
        P("rep", "fsdp", None),
        P("rep", "fsdp", None),
        P("rep", "fsdp", None),
        P("rep", "fsdp", None),
        P("rep", "fsdp"),
        P("rep", "fsdp", None),
        P("rep", "fsdp", None),
        P("rep", "fsdp", None),
        P("rep", "fsdp", None),
        P("rep", "fsdp", None),
        P("rep", "fsdp"),
        P("fsdp", None),
        P("fsdp", None),
        P("fsdp", None),
        P("fsdp", None),
        P("fsdp", None),
        P("fsdp"),
    )
    out_specs = (
        P(("rep", "dp", "fsdp"), None, None),
        P(("rep", "dp", "fsdp"), None, None),
        P("rep", "fsdp", None),
        P("rep", "fsdp", None),
        P("rep", "fsdp", None),
        P("rep", "fsdp", None),
        P("rep", "fsdp", None),
        P("rep", "fsdp"),
        P("rep", "fsdp", None),
        P("rep", "fsdp", None),
        P("rep", "fsdp", None),
        P("rep", "fsdp", None),
        P("rep", "fsdp", None),
        P("rep", "fsdp"),
        P("rep", "fsdp", None),
        P("rep", "fsdp", None),
        P("rep", "fsdp", None),
        P("rep", "fsdp", None),
        P("rep", "fsdp", None),
        P("rep", "fsdp"),
        P("fsdp", None),
        P("fsdp", None),
        P("fsdp", None),
        P("fsdp", None),
        P("fsdp", None),
        P("fsdp"),
        P("fsdp", None),
        P("fsdp", None),
        P("fsdp", None),
        P("fsdp", None),
        P("fsdp", None),
        P("fsdp"),
        P("fsdp", None),
        P("fsdp", None),
        P("fsdp", None),
        P("fsdp", None),
        P("fsdp", None),
        P("fsdp"),
    )
    return jax.shard_map(body, mesh=mesh, in_specs=in_specs, out_specs=out_specs, check_vma=False)
```

```python
import functools
import math

import jax
import jax.numpy as jnp
from jax import lax
from jax.experimental import pallas as pl
from jax.experimental.pallas import tpu as pltpu
from jax.sharding import PartitionSpec as P

D = 1152
HEADS = 16
FF = 4608


NORM_EPS = 1e-06
BETA_ONE = 0.9
BETA_TWO = 0.95
ADAM_EPS = 1e-08
WEIGHT_DECAY = 0.1
OUTER_RATE = 0.7
OUTER_MOMENTUM = 0.9
FEW = 8

F32 = jnp.float32
BF16 = jnp.bfloat16
SMALL = pl.CostEstimate(flops=1024, bytes_accessed=1024, transcendentals=0)


def dot(left, right):
    return jnp.dot(left, right, preferred_element_type=F32)


def dot_nt(left, right):
    return lax.dot_general(left, right, (((1,), (1,)), ((), ())), preferred_element_type=F32)


def dot_tn(left, right):
    return lax.dot_general(left, right, (((0,), (0,)), ((), ())), preferred_element_type=F32)


def time_embed(steps, width):
    half = width // 2
    frequency = jnp.exp(-math.log(10000.0) * jnp.arange(half).astype(F32) / half)
    angles = steps.astype(F32)[:, None] * frequency[None, :]
    return jnp.concatenate([jnp.cos(angles), jnp.sin(angles)], axis=1)


def learning_rates(width, hidden):
    return (
        2.0 / math.sqrt(width),
        2.0 / math.sqrt(width),
        2.0 / math.sqrt(width // 32),
        2.0 / math.sqrt(width),
        2.0 / math.sqrt(hidden),
        0.3,
    )


def shift_by(value, axis, step):
    size = lax.axis_size(axis)
    return lax.ppermute(value, axis, [(i, (i + step) % size) for i in range(size)])


def swap_with(value, axis, bit):
    size = lax.axis_size(axis)
    return lax.ppermute(value, axis, [(i, i ^ bit) for i in range(size)])


def gather_line(value, axis):
    size = lax.axis_size(axis)
    if size > FEW:
        return lax.all_gather(value, axis, axis=0)
    place = lax.axis_index(axis)
    result = jnp.zeros((size,) + value.shape, value.dtype)
    for step in range(size):
        piece = value if step == 0 else shift_by(value, axis, step)
        result = lax.dynamic_update_index_in_dim(result, piece, (place - step) % size, 0)
    return result


def scatter_line(value, axis):
    size = lax.axis_size(axis)
    if size > FEW:
        return lax.psum_scatter(value, axis, scatter_dimension=0, tiled=False)
    place = lax.axis_index(axis)
    total = lax.dynamic_index_in_dim(value, place, 0, keepdims=False)
    for step in range(1, size):
        piece = lax.dynamic_index_in_dim(value, (place + step) % size, 0, keepdims=False)
        total = total + shift_by(piece, axis, step)
    return total


def moments(values):
    center = values - jnp.mean(values, axis=-1, keepdims=True)
    inverse = lax.rsqrt(jnp.mean(center * center, axis=-1, keepdims=True) + NORM_EPS)
    return center * inverse, inverse


def norm_back(normed, inverse, upstream):
    first = jnp.mean(upstream, axis=-1, keepdims=True)
    second = jnp.mean(upstream * normed, axis=-1, keepdims=True)
    return (upstream - first - normed * second) * inverse


def gelu_pair(h):
    c = math.sqrt(2.0 / math.pi)
    inner = c * (h + 0.044715 * h * h * h)
    t = jnp.tanh(inner)
    value = 0.5 * h * (1.0 + t)
    slope = 0.5 * (1.0 + t) + 0.5 * h * (1.0 - t * t) * c * (1.0 + 3.0 * 0.044715 * h * h)
    return value, slope


def head_window(head, head_dim):
    low = head * head_dim
    start = low // 128 * 128
    stop = -(-(low + head_dim) // 128) * 128
    return start, stop, low - start


def head_mask(shape, offset, head_dim):
    lane = lax.broadcasted_iota(jnp.int32, shape, 1)
    return (lane >= offset) & (lane < offset + head_dim)


def attention_forward_kernel(
    x_ref, cot_ref, mod_ref, bias_ref, weight_ref,
    attn_in_ref, packed_ref, attended_ref, log_ref, attn_ref, x1_ref, mlp_in_ref, d_mlp_ref, sums_ref,
    gather_ref,
):
    length, width = x_ref.shape
    head_dim = width // HEADS
    factor = 1.0 / math.sqrt(head_dim)
    residual = x_ref[...].astype(F32)
    normed, _ = moments(residual)
    attn_in_ref[...] = (normed * (1.0 + mod_ref[0, 1:2]) + mod_ref[0, 0:1]).astype(BF16)
    for unit in range(3):
        piece = dot(attn_in_ref[...], weight_ref[unit]) + bias_ref[unit : unit + 1]
        packed_ref[:, unit * width : (unit + 1) * width] = piece.astype(BF16)
    for head in range(HEADS):
        start, stop, offset = head_window(head, head_dim)
        mask = head_mask((length, stop - start), offset, head_dim)
        query = packed_ref[:, start:stop]
        query = jnp.where(mask, query, jnp.zeros_like(query))
        keys = packed_ref[:, width + start : width + stop]
        values = packed_ref[:, 2 * width + start : 2 * width + stop]
        scores = dot_nt(query, keys) * factor
        top = jnp.max(scores, axis=-1, keepdims=True)
        raised = jnp.exp(scores - top)
        summed = jnp.sum(raised, axis=-1, keepdims=True)
        probs = (raised * (1.0 / summed)).astype(BF16)
        log_ref[:, head : head + 1] = top + jnp.log(summed)
        out = dot(probs, values)
        if offset == 0:
            gather_ref[:, start:stop] = out
        else:
            gather_ref[:, start:stop] = jnp.where(mask, out, gather_ref[:, start:stop])
    attended_ref[...] = gather_ref[...].astype(BF16)
    attn = dot(attended_ref[...], weight_ref[3]) + bias_ref[3:4]
    attn_ref[...] = attn
    middle = residual + mod_ref[0, 2:3] * attn
    x1_ref[...] = middle
    normed_two, _ = moments(middle)
    mlp_in_ref[...] = (normed_two * (1.0 + mod_ref[0, 4:5]) + mod_ref[0, 3:4]).astype(BF16)
    d_mlp = (mod_ref[0, 5:6] * (cot_ref[...].astype(F32) * mod_ref[0, 6:7])).astype(BF16)
    d_mlp_ref[...] = d_mlp
    sums_ref[0, 0:1] = jnp.sum(d_mlp.astype(F32), axis=0, keepdims=True)


def rows_spec(length, width):
    return pl.BlockSpec((length, width), lambda i: (i, 0))


def whole_spec(shape):
    return pl.BlockSpec(shape, lambda i: (0,) * len(shape), pipeline_mode=pl.Buffered(1))


def lead_spec(rows, width):
    return pl.BlockSpec((1, rows, width), lambda i: (i, 0, 0))


def params(megabytes):
    return pltpu.CompilerParams(vmem_limit_bytes=megabytes << 20)


def attention_forward(x, cot, mod, bias, weights, slots, length, width):
    tokens = slots * length
    row = rows_spec(length, width)
    return pl.pallas_call(
        attention_forward_kernel,
        grid=(slots,),
        in_specs=[row, row, lead_spec(8, width), whole_spec((8, width)), whole_spec((4, width, width))],
        out_specs=[
            row, rows_spec(length, 3 * width), row, rows_spec(length, 128), row, row, row, row,
            lead_spec(8, width),
        ],
        out_shape=[
            jax.ShapeDtypeStruct((tokens, width), BF16),
            jax.ShapeDtypeStruct((tokens, 3 * width), BF16),
            jax.ShapeDtypeStruct((tokens, width), BF16),
            jax.ShapeDtypeStruct((tokens, 128), F32),
            jax.ShapeDtypeStruct((tokens, width), F32),
            jax.ShapeDtypeStruct((tokens, width), F32),
            jax.ShapeDtypeStruct((tokens, width), BF16),
            jax.ShapeDtypeStruct((tokens, width), BF16),
            jax.ShapeDtypeStruct((slots, 8, width), F32),
        ],
        scratch_shapes=[pltpu.VMEM((length, width), F32)],
        compiler_params=params(48),
        cost_estimate=pl.CostEstimate(
            flops=2 * tokens * width * width * 4, bytes_accessed=40 << 20, transcendentals=0
        ),
    )(x, cot, mod, bias, weights)


def one_spec(joint):
    lines, rows, width = joint.shape[1], joint.shape[4], joint.shape[5]
    return pl.BlockSpec((1, lines, 2, 1, rows, width), lambda u: (u, 0, 0, 0, 0, 0))


def two_spec(joint):
    groups, lines, _, _, rows, width = joint.shape
    return pl.BlockSpec((groups, lines // groups, 2, 1, rows, width), lambda u: (0, u, 0, 1, 0, 0))


def one_of(ref):
    return ref[...].reshape(ref.shape[-1], ref.shape[-1])


def two_of(ref):
    value = ref[...]
    if value.shape[1] > 1:
        value = jnp.swapaxes(value, 0, 1)
    return value.reshape(ref.shape[-1], ref.shape[-1])


def hidden_kernel(mlp_in_ref, weight_ref, bias_ref, act_ref, slope_ref):
    step = 256

    def chunk(index, carry):
        here = pl.ds(pl.multiple_of(index * step, step), step)
        hidden = dot(mlp_in_ref[here, :], one_of(weight_ref)) + bias_ref[0:1]
        value, slope = gelu_pair(hidden)
        act_ref[here, :] = value.astype(BF16)
        slope_ref[here, :] = slope.astype(BF16)
        return carry

    lax.fori_loop(0, mlp_in_ref.shape[0] // step, chunk, 0)


def hidden_forward(mlp_in, weights, bias):
    tokens, width = mlp_in.shape
    units = weights.shape[0]
    column = pl.BlockSpec((tokens, width), lambda u: (0, u))
    return pl.pallas_call(
        hidden_kernel,
        grid=(units,),
        in_specs=[whole_spec((tokens, width)), one_spec(weights), pl.BlockSpec((1, width), lambda u: (0, u))],
        out_specs=[column, column],
        out_shape=[jax.ShapeDtypeStruct((tokens, units * width), BF16)] * 2,
        compiler_params=params(48),
        cost_estimate=pl.CostEstimate(
            flops=2 * tokens * width * width * units, bytes_accessed=26 << 20, transcendentals=0
        ),
    )(mlp_in, weights, bias)


def hidden_back_kernel(d_mlp_ref, weight_ref, slope_ref, d_hidden_ref, sums_ref):
    step = 256

    def chunk(index, carry):
        here = pl.ds(pl.multiple_of(index * step, step), step)
        d_hidden = dot_nt(d_mlp_ref[here, :], two_of(weight_ref)) * slope_ref[here, :].astype(F32)
        d_hidden = d_hidden.astype(BF16)
        d_hidden_ref[here, :] = d_hidden
        return carry + jnp.sum(d_hidden.astype(F32), axis=0, keepdims=True)

    zero = jnp.zeros((1, slope_ref.shape[1]), F32)
    sums_ref[0:1] = lax.fori_loop(0, d_mlp_ref.shape[0] // step, chunk, zero)


def hidden_back(d_mlp, weights, slope):
    tokens, width = d_mlp.shape
    units = weights.shape[0]
    column = pl.BlockSpec((tokens, width), lambda u: (0, u))
    return pl.pallas_call(
        hidden_back_kernel,
        grid=(units,),
        in_specs=[whole_spec((tokens, width)), two_spec(weights), column],
        out_specs=[column, pl.BlockSpec((8, width), lambda u: (0, u))],
        out_shape=[
            jax.ShapeDtypeStruct((tokens, units * width), BF16),
            jax.ShapeDtypeStruct((8, units * width), F32),
        ],
        compiler_params=params(48),
        cost_estimate=pl.CostEstimate(
            flops=2 * tokens * width * width * units, bytes_accessed=26 << 20, transcendentals=0
        ),
    )(d_mlp, weights, slope)


def mlp_rest_kernel(act_ref, d_hidden_ref, two_ref, one_ref, mlp_ref, d_in_ref):
    step = 256

    @pl.when(pl.program_id(0) == 0)
    def _():
        mlp_ref[...] = jnp.zeros_like(mlp_ref)
        d_in_ref[...] = jnp.zeros_like(d_in_ref)

    def chunk(index, carry):
        here = pl.ds(pl.multiple_of(index * step, step), step)
        mlp_ref[here, :] += dot(act_ref[here, :], two_of(two_ref))
        d_in_ref[here, :] += dot_nt(d_hidden_ref[here, :], one_of(one_ref))
        return carry

    lax.fori_loop(0, act_ref.shape[0] // step, chunk, 0)


def mlp_rest(act, d_hidden, weights):
    tokens = act.shape[0]
    units, width = weights.shape[0], weights.shape[-1]
    column = pl.BlockSpec((tokens, width), lambda u: (0, u))
    total = pl.BlockSpec((tokens, width), lambda u: (0, 0))
    return pl.pallas_call(
        mlp_rest_kernel,
        grid=(units,),
        in_specs=[column, column, two_spec(weights), one_spec(weights)],
        out_specs=[total, total],
        out_shape=[jax.ShapeDtypeStruct((tokens, width), F32)] * 2,
        compiler_params=params(48),
        cost_estimate=pl.CostEstimate(
            flops=4 * tokens * width * width * units, bytes_accessed=42 << 20, transcendentals=0
        ),
    )(act, d_hidden, weights, weights)


def middle_back_kernel(
    mlp_ref, bias_ref, d_in_ref, x1_ref, attn_ref, cot_ref, mod_ref, weight_ref,
    out_ref, d_mid_ref, d_attn_ref, d_att_ref, rows_ref,
):
    live = mod_ref[0, 6:7]
    gate_two = mod_ref[0, 5:6]
    upstream = cot_ref[...].astype(F32) * live
    middle = x1_ref[...]
    mlp = mlp_ref[...] + bias_ref[4:5]
    out_ref[...] = ((middle + gate_two * mlp) * live).astype(BF16)
    rows_ref[0, 5:6] = jnp.sum(upstream * mlp, axis=0, keepdims=True)
    normed, inverse = moments(middle)
    d_in = d_in_ref[...]
    rows_ref[0, 3:4] = jnp.sum(d_in, axis=0, keepdims=True)
    rows_ref[0, 4:5] = jnp.sum(d_in * normed, axis=0, keepdims=True)
    d_mid = upstream + norm_back(normed, inverse, d_in * (1.0 + mod_ref[0, 4:5]))
    d_mid_ref[...] = d_mid
    rows_ref[0, 2:3] = jnp.sum(d_mid * attn_ref[...], axis=0, keepdims=True)
    d_attn = (mod_ref[0, 2:3] * d_mid).astype(BF16)
    d_attn_ref[...] = d_attn
    rows_ref[0, 6:7] = jnp.sum(d_attn.astype(F32), axis=0, keepdims=True)
    d_att_ref[...] = dot_nt(d_attn_ref[...], weight_ref[0]).astype(BF16)


def middle_back(mlp, bias, d_in, x1, attn, cot, mod, weights, slots, length, width):
    tokens = slots * length
    row = rows_spec(length, width)
    proj = pl.BlockSpec((1, width, width), lambda i: (3, 0, 0), pipeline_mode=pl.Buffered(1))
    return pl.pallas_call(
        middle_back_kernel,
        grid=(slots,),
        in_specs=[row, whole_spec((8, width)), row, row, row, row, lead_spec(8, width), proj],
        out_specs=[row, row, row, row, lead_spec(8, width)],
        out_shape=[
            jax.ShapeDtypeStruct((tokens, width), BF16),
            jax.ShapeDtypeStruct((tokens, width), F32),
            jax.ShapeDtypeStruct((tokens, width), BF16),
            jax.ShapeDtypeStruct((tokens, width), BF16),
            jax.ShapeDtypeStruct((slots, 8, width), F32),
        ],
        compiler_params=params(48),
        cost_estimate=pl.CostEstimate(
            flops=2 * tokens * width * width, bytes_accessed=30 << 20, transcendentals=0
        ),
    )(mlp, bias, d_in, x1, attn, cot, mod, weights)


def attention_back_kernel(packed_ref, d_att_ref, log_ref, d_packed_ref, sums_ref, q_ref, k_ref, v_ref):
    length, width = d_att_ref.shape
    head_dim = width // HEADS
    factor = 1.0 / math.sqrt(head_dim)
    for head in range(HEADS):
        start, stop, offset = head_window(head, head_dim)
        mask = head_mask((length, stop - start), offset, head_dim)
        query = packed_ref[:, start:stop]
        query_one = jnp.where(mask, query, jnp.zeros_like(query))
        keys = packed_ref[:, width + start : width + stop]
        values = packed_ref[:, 2 * width + start : 2 * width + stop]
        d_att = d_att_ref[:, start:stop]
        d_att = jnp.where(mask, d_att, jnp.zeros_like(d_att))
        weights = jnp.exp(dot_nt(query_one, keys) * factor - log_ref[:, head : head + 1])
        d_probs = dot_nt(d_att, values)
        inner = jnp.sum(weights * d_probs, axis=-1, keepdims=True)
        d_scores = (weights * (d_probs - inner)).astype(BF16)
        probs = weights.astype(BF16)
        pieces = (
            (q_ref, dot(d_scores, keys) * factor),
            (k_ref, dot_tn(d_scores, query) * factor),
            (v_ref, dot_tn(probs, d_att)),
        )
        for ref, piece in pieces:
            if offset == 0:
                ref[:, start:stop] = piece
            else:
                ref[:, start:stop] = jnp.where(mask, piece, ref[:, start:stop])
    for unit, ref in enumerate((q_ref, k_ref, v_ref)):
        piece = ref[...].astype(BF16)
        d_packed_ref[:, unit * width : (unit + 1) * width] = piece
        sums_ref[0, unit : unit + 1] = jnp.sum(piece.astype(F32), axis=0, keepdims=True)


def attention_back(packed, d_att, log, slots, length, width):
    tokens = slots * length
    return pl.pallas_call(
        attention_back_kernel,
        grid=(slots,),
        in_specs=[rows_spec(length, 3 * width), rows_spec(length, width), rows_spec(length, 128)],
        out_specs=[rows_spec(length, 3 * width), lead_spec(8, width)],
        out_shape=[
            jax.ShapeDtypeStruct((tokens, 3 * width), BF16),
            jax.ShapeDtypeStruct((slots, 8, width), F32),
        ],
        scratch_shapes=[pltpu.VMEM((length, width), F32)] * 3,
        compiler_params=params(48),
        cost_estimate=pl.CostEstimate(
            flops=10 * tokens * length * 256 * HEADS, bytes_accessed=14 << 20, transcendentals=0
        ),
    )(packed, d_att, log)


def input_back_kernel(d_packed_ref, weight_ref, x_ref, d_mid_ref, mod_ref, grad_ref, rows_ref):
    width = x_ref.shape[1]
    d_in = dot_nt(d_packed_ref[:, :width], weight_ref[0])
    for unit in (1, 2):
        d_in = d_in + dot_nt(d_packed_ref[:, unit * width : (unit + 1) * width], weight_ref[unit])
    normed, inverse = moments(x_ref[...].astype(F32))
    rows_ref[0, 0:1] = jnp.sum(d_in, axis=0, keepdims=True)
    rows_ref[0, 1:2] = jnp.sum(d_in * normed, axis=0, keepdims=True)
    back = norm_back(normed, inverse, d_in * (1.0 + mod_ref[0, 1:2]))
    grad_ref[...] = (d_mid_ref[...] + back).astype(BF16)


def input_back(d_packed, weights, x, d_mid, mod, slots, length, width):
    tokens = slots * length
    row = rows_spec(length, width)
    return pl.pallas_call(
        input_back_kernel,
        grid=(slots,),
        in_specs=[
            rows_spec(length, 3 * width), whole_spec((3, width, width)), row, row, lead_spec(8, width),
        ],
        out_specs=[row, lead_spec(8, width)],
        out_shape=[
            jax.ShapeDtypeStruct((tokens, width), BF16),
            jax.ShapeDtypeStruct((slots, 8, width), F32),
        ],
        compiler_params=params(48),
        cost_estimate=pl.CostEstimate(
            flops=6 * tokens * width * width, bytes_accessed=20 << 20, transcendentals=0
        ),
    )(d_packed, weights, x, d_mid, mod)


def grad_kernel(left_ref, right_ref, grad_ref):
    step = grad_ref.shape[0] // 3

    def chunk(index, carry):
        here = pl.ds(pl.multiple_of(index * step, step), step)
        grad_ref[here, :] = dot_tn(left_ref[:, here], right_ref[...]).astype(BF16)
        return carry

    lax.fori_loop(0, 3, chunk, 0)


def grad_columns(left, right):
    tokens, rows = left.shape
    width = right.shape[1]
    return pl.pallas_call(
        grad_kernel,
        grid=(width // rows,),
        in_specs=[whole_spec((tokens, rows)), pl.BlockSpec((tokens, rows), lambda u: (0, u))],
        out_specs=pl.BlockSpec((rows, rows), lambda u: (0, u)),
        out_shape=jax.ShapeDtypeStruct((rows, width), BF16),
        compiler_params=params(48),
        cost_estimate=pl.CostEstimate(
            flops=2 * tokens * rows * width, bytes_accessed=2 * rows * width + 4 * tokens * width, transcendentals=0
        ),
    )(left, right)


def grad_rows(left, right):
    tokens, rows = left.shape
    width = right.shape[1]
    return pl.pallas_call(
        grad_kernel,
        grid=(rows // width,),
        in_specs=[pl.BlockSpec((tokens, width), lambda u: (0, u)), whole_spec((tokens, width))],
        out_specs=rows_spec(width, width),
        out_shape=jax.ShapeDtypeStruct((rows, width), BF16),
        compiler_params=params(48),
        cost_estimate=pl.CostEstimate(
            flops=2 * tokens * rows * width, bytes_accessed=2 * rows * width + 4 * tokens * rows, transcendentals=0
        ),
    )(left, right)


def after(*values):
    return lax.optimization_barrier(values)


def adam_moments(first, second, gradient):
    first_next = BETA_ONE * first + (1.0 - BETA_ONE) * gradient
    second_next = BETA_TWO * second + (1.0 - BETA_TWO) * gradient * gradient
    return first_next, second_next


def adam_delta(master, first_next, second_next, rate, fix_one, fix_two):
    step = first_next / fix_one / (jnp.sqrt(second_next / fix_two) + ADAM_EPS)
    return (rate * (step + WEIGHT_DECAY * master)).astype(BF16)


def whole_kernel(mode, rate, where_ref, fix_ref, *refs):
    half = pl.program_id(2)
    if mode == "sum":
        a_ref, b_ref, master_ref, first_ref, second_ref, grad_ref, m_ref, v_ref, keep_ref, give_ref = refs
        gradient = a_ref[0].astype(F32) + b_ref[0].astype(F32)
        grad_ref[0] = gradient
    elif mode == "given":
        g_ref, master_ref, first_ref, second_ref, m_ref, v_ref, keep_ref, give_ref = refs
        gradient = g_ref[0]
    else:
        own_ref, other_ref, first_ref, second_ref, grad_ref, m_ref, v_ref = refs
        gradient = jnp.where(half == where_ref[0], own_ref[...].astype(F32), other_ref[...].astype(F32))
        grad_ref[0] = gradient
    first_next, second_next = adam_moments(first_ref[0], second_ref[0], gradient)
    m_ref[0] = first_next
    v_ref[0] = second_next
    if mode != "halves":
        delta = adam_delta(master_ref[0], first_next, second_next, rate, fix_ref[0], fix_ref[1])

        @pl.when(half == where_ref[1])
        def _():
            keep_ref[...] = delta

        @pl.when(half != where_ref[1])
        def _():
            give_ref[...] = delta


def row_block(rows):
    return 144 if rows % 144 == 0 else rows


def adam_whole(mode, where, fixes, gradients, master, first, second, rate, shift=0):
    rows, columns = master.shape
    half, width = rows // 2, D
    block = row_block(half)
    three = pl.BlockSpec((1, block, width), lambda c, r, h, w: (h, r, c))
    flat = pl.BlockSpec((block, width), lambda c, r, h, w: (r, c))
    moved = pl.BlockSpec((block, width), lambda c, r, h, w: (r, c + shift))
    view = (2, half, columns)
    state = [first.reshape(view), second.reshape(view)]
    if mode == "halves":
        operands = list(gradients) + state
        in_specs = [moved, moved, three, three]
    else:
        operands = [g.reshape(view) for g in gradients] + [master.reshape(view)] + state
        in_specs = [three] * len(operands)
    wide = jax.ShapeDtypeStruct(view, F32)
    thin = jax.ShapeDtypeStruct((half, columns), BF16)
    count = 2 if mode == "given" else 3
    extra = 0 if mode == "halves" else 2
    outs = pl.pallas_call(
        functools.partial(whole_kernel, mode, rate),
        grid_spec=pltpu.PrefetchScalarGridSpec(
            num_scalar_prefetch=1,
            grid=(columns // width, half // block, 2),
            in_specs=[pl.BlockSpec(memory_space=pltpu.SMEM)] + in_specs,
            out_specs=[three] * count + [flat] * extra,
        ),
        out_shape=[wide] * count + [thin] * extra,
        compiler_params=params(48),
        cost_estimate=SMALL,
    )(where, fixes, *operands)
    return [out.reshape(1, rows, columns) for out in outs[:count]] + list(outs[count:])


def own_kernel(rates, where_ref, fix_ref, g_ref, *refs):
    states, keep_ref, give_ref = refs[:-2], refs[-2], refs[-1]
    unit, core = pl.program_id(0), pl.program_id(1)

    def run(kind):
        master_ref, first_ref, second_ref = states[3 * kind : 3 * kind + 3]
        first_next, second_next = adam_moments(first_ref[0, 0], second_ref[0, 0], g_ref[0].astype(F32))
        delta = adam_delta(
            master_ref[0, 0], first_next, second_next, rates[kind][1], fix_ref[0], fix_ref[1]
        )

        @pl.when(core == where_ref[1])
        def _():
            keep_ref[...] = delta

        @pl.when(core != where_ref[1])
        def _():
            give_ref[...] = delta

    start = 0
    for kind, (units, _) in enumerate(rates):
        stop = start + units

        @pl.when((unit >= start) & (unit < stop))
        def _():
            run(kind)

        start = stop


def adam_own(where, fixes, gradient, weights):
    half, columns = gradient.shape
    quarter, width = half // 2, D
    operands, in_specs, rates = [gradient.reshape(2, quarter, columns)], [], []
    in_specs.append(pl.BlockSpec((1, quarter, width), lambda c, h, w: (h, 0, c)))
    start = 0
    for master, first, second, rate in weights:
        units = master.shape[1] // width
        low = start

        def place(c, h, w, low=low, units=units):
            return (w[0], h, 0, jnp.clip(c - low, 0, units - 1))

        for value in (master, first, second):
            operands.append(value.reshape(2, 2, quarter, value.shape[-1]))
            in_specs.append(pl.BlockSpec((1, 1, quarter, width), place))
        rates.append((units, rate))
        start += units
    flat = pl.BlockSpec((quarter, width), lambda c, h, w: (0, c))
    return pl.pallas_call(
        functools.partial(own_kernel, tuple(rates)),
        grid_spec=pltpu.PrefetchScalarGridSpec(
            num_scalar_prefetch=1,
            grid=(columns // width, 2),
            in_specs=[pl.BlockSpec(memory_space=pltpu.SMEM)] + in_specs,
            out_specs=[flat, flat],
        ),
        out_shape=[jax.ShapeDtypeStruct((quarter, columns), BF16)] * 2,
        compiler_params=params(48),
        cost_estimate=SMALL,
    )(where, fixes, *operands)


def outer_kernel(scale, where_ref, *refs):
    totals, master_ref, outer_ref, delta_ref, next_ref, weight_ref = refs[:-5], *refs[-5:]
    core = pl.program_id(2)
    if len(totals) == 2:
        own, other = totals[0][...], totals[1][...]
    else:
        mine = pl.program_id(1) == where_ref[0]
        own = jnp.where(mine, totals[0][...], totals[1][...])
        other = jnp.where(mine, totals[2][...], totals[3][...])
    delta = jnp.where(core == where_ref[1], own.astype(F32), other.astype(F32)) * scale
    outer_next = OUTER_MOMENTUM * outer_ref[...].reshape(delta.shape) + delta
    master = master_ref[...].reshape(delta.shape)
    delta_ref[...] = delta.reshape(delta_ref.shape)
    next_ref[...] = outer_next.reshape(next_ref.shape)
    weight = master - OUTER_RATE * (delta + OUTER_MOMENTUM * outer_next)
    weight_ref[...] = weight.reshape(weight_ref.shape)


def outer_whole(where, totals, master, outer, groups, shift=0):
    rows, columns = master.shape
    width = D
    if len(totals) == 2:
        part = rows // 2
        block = row_block(part)
        view = (2, part, columns)
        grid = (columns // width, part // block, 2)
        state = pl.BlockSpec((1, block, width), lambda c, r, h, w: (h, r, c))
        total = pl.BlockSpec((block, width), lambda c, r, h, w: (r, c + shift))
    else:
        part = rows // 4
        view = (2, 2, part, columns)
        grid = (columns // width, 2, 2)
        state = pl.BlockSpec((1, 1, part, width), lambda c, p, h, w: (p, h, 0, c))
        total = pl.BlockSpec((part, width), lambda c, p, h, w: (0, c + shift))
    outs = pl.pallas_call(
        functools.partial(outer_kernel, 1.0 / groups),
        grid_spec=pltpu.PrefetchScalarGridSpec(
            num_scalar_prefetch=1,
            grid=grid,
            in_specs=[total] * len(totals) + [state, state],
            out_specs=[state] * 3,
        ),
        out_shape=[jax.ShapeDtypeStruct(view, F32)] * 3,
        compiler_params=params(48),
        cost_estimate=SMALL,
    )(where, *totals, master.reshape(view), outer.reshape(view))
    return [out.reshape(rows, columns) for out in outs]


def place_kernel(order_ref, *refs):
    sources, target, held, came, left = refs[:-4], refs[-4], refs[-3], refs[-2], refs[-1]
    inward, outward = [], []
    for which, source in enumerate(sources):
        for block in range(source.shape[0]):
            index = which * source.shape[0] + block
            inward.append(pltpu.make_async_copy(source.at[block], held.at[index], came.at[index]))
            outward.append(
                pltpu.make_async_copy(held.at[index], target.at[order_ref[index]], left.at[index])
            )
    for copy in inward:
        copy.start()
    for first, second in zip(inward, outward):
        first.wait()
        second.start()
    for copy in outward:
        copy.wait()


def place_blocks(order, sources):
    blocks = sum(source.shape[0] for source in sources)
    shape = (blocks,) + sources[0].shape[1:]
    return pl.pallas_call(
        place_kernel,
        grid_spec=pltpu.PrefetchScalarGridSpec(
            num_scalar_prefetch=1,
            grid=(1,),
            in_specs=[pl.BlockSpec(memory_space=pl.ANY)] * len(sources),
            out_specs=pl.BlockSpec(memory_space=pl.ANY),
            scratch_shapes=[
                pltpu.VMEM(shape, sources[0].dtype),
                pltpu.SemaphoreType.DMA((blocks,)),
                pltpu.SemaphoreType.DMA((blocks,)),
            ],
        ),
        out_shape=jax.ShapeDtypeStruct(shape, sources[0].dtype),
        compiler_params=params(48),
        cost_estimate=pl.CostEstimate(
            flops=0, bytes_accessed=4 * blocks * shape[1] * shape[2], transcendentals=0
        ),
    )(order, *sources)


def hops_line(piece):
    near = jnp.stack([piece, shift_by(piece, "fsdp", 1)])
    far = jnp.stack([shift_by(piece, "fsdp", 2), shift_by(piece, "fsdp", 3)])
    return near, far


def hops_side(near, far):
    near = jnp.concatenate([near, swap_with(near, "rep", 2)])
    far = jnp.concatenate([far, swap_with(far, "dp", 1)])
    return near, far


def hops_other(near, far):
    return near, far, swap_with(near, "dp", 1), swap_with(far, "rep", 2)


def hops_core(sources):
    return tuple(sources) + tuple(swap_with(source, "rep", 1) for source in sources)


def hops_place(sources, weigh):
    size = lax.axis_size("fsdp")
    rep, pair, line = lax.axis_index("rep"), lax.axis_index("dp"), lax.axis_index("fsdp")
    order = []
    for core in (0, 1):
        for kind in range(4):
            for block in range(4):
                hop, step = block // 2, block % 2
                if kind in (0, 2):
                    flip_rep, flip_pair, back = hop, kind // 2, step
                else:
                    flip_rep, flip_pair, back = kind // 2, hop, 2 + step
                place = lax.rem(line - back + size, size) * weigh[0]
                place = place + (rep ^ (2 * flip_rep + core)) * weigh[1] + (pair ^ flip_pair) * weigh[2]
                order.append(place)
    return place_blocks(jnp.stack(order).astype(jnp.int32), sources)


def own_half(value, index):
    return lax.dynamic_index_in_dim(value, index, 1, keepdims=False)


def body(
    images,
    cotangent,
    counts,
    timesteps,
    labels,
    label_table,
    step_count,
    w_ada,
    w_qkv,
    w_proj,
    w_fc1,
    w_fc2,
    biases,
    first_ada,
    first_qkv,
    first_proj,
    first_fc1,
    first_fc2,
    first_bias,
    second_ada,
    second_qkv,
    second_proj,
    second_fc1,
    second_fc2,
    second_bias,
    outer_ada,
    outer_qkv,
    outer_proj,
    outer_fc1,
    outer_fc2,
    outer_bias,
):
    masters = (w_ada, w_qkv, w_proj, w_fc1, w_fc2, biases)
    firsts = (first_ada, first_qkv, first_proj, first_fc1, first_fc2, first_bias)
    seconds = (second_ada, second_qkv, second_proj, second_fc1, second_fc2, second_bias)
    outers = (outer_ada, outer_qkv, outer_proj, outer_fc1, outer_fc2, outer_bias)
    slots, length, width = images.shape
    tokens = slots * length
    rows = w_qkv.shape[0]
    rows_two = w_fc2.shape[0]
    lines = lax.axis_size("fsdp")
    groups = lax.axis_size("rep")
    rep = lax.axis_index("rep")
    pair = lax.axis_index("dp")
    line = lax.axis_index("fsdp")
    half = rows // 2
    everyone = ("rep", "fsdp", "dp")

    def rows_of(weight):
        return lax.dynamic_slice_in_dim(weight, pair * half, half, axis=0).astype(BF16)

    attention_cut = jnp.concatenate([rows_of(w_qkv), rows_of(w_proj)], axis=1)
    attention_cut = lax.dynamic_slice_in_dim(attention_cut, rep * width, width, axis=1)
    hops = lines == 4 and groups == 4
    one_cut = lax.dynamic_slice(w_fc1, (pair * half, rep * width), (half, width))
    eighth = rows_two // (2 * groups)
    two_cut = lax.dynamic_slice_in_dim(w_fc2, (rep * 2 + pair) * eighth, eighth, axis=0)
    mlp_cut = jnp.concatenate([one_cut, two_cut]).astype(BF16)
    w_mlp = lax.all_gather(mlp_cut, everyone, axis=0, tiled=True)
    w_mlp = w_mlp.reshape(groups, lines, 2, 2, half, width)
    live = (jnp.arange(slots) < counts[0]).astype(F32)
    condition = time_embed(timesteps, D) + jnp.take(label_table, labels, axis=0).astype(F32)
    style = jax.nn.silu(condition).astype(BF16)
    message = jnp.concatenate([style.reshape(-1), biases.astype(BF16)])
    heard = gather_line(message, "fsdp")
    if hops:
        attention_cut, message = after(attention_cut, message)
        attention_parts = hops_line(attention_cut)
        heard = after(heard, *attention_parts)[0]
        attention_parts = hops_side(*attention_parts)
    else:
        w_attn = lax.all_gather(attention_cut, everyone, axis=0, tiled=True)
    bias_all = heard[:, slots * width :].reshape(-1).astype(F32)
    style_line = heard[:, : slots * width].reshape(lines * slots, width)
    style_cut = lax.dynamic_slice_in_dim(style_line, line * rows, rows, axis=1)
    mod_part = dot(style_cut, w_ada.astype(BF16))
    if hops:
        attention_parts = hops_other(*attention_parts)
        attention_parts = after(*attention_parts, mod_part)[:-1]
        w_attn = hops_place(hops_core(attention_parts), (2, 8, 1))
    w_attn = w_attn.reshape(4, width, width)
    b_ada = bias_all[: 6 * width]
    modulation = scatter_line(mod_part.reshape(lines, slots, 6 * width), "fsdp") + b_ada
    mod = jnp.concatenate(
        [
            modulation.reshape(slots, 6, width),
            jnp.broadcast_to(live[:, None, None], (slots, 2, width)),
        ],
        axis=1,
    )
    b_rest = bias_all[6 * width : 9 * width].reshape(3, width)
    bias = jnp.zeros((8, width), F32)
    bias = bias.at[0].set(b_rest[0]).at[2].set(b_rest[1]).at[3].set(b_rest[2])
    bias = bias.at[4].set(bias_all[9 * width + FF :])
    b_fc1 = bias_all[9 * width : 9 * width + FF].reshape(1, FF)
    x = images.reshape(tokens, width)
    cot = cotangent.reshape(tokens, width)

    attn_in, packed, attended, log_total, attn_out, middle, mlp_in, d_mlp, mlp_sums = attention_forward(
        x, cot, mod, bias, w_attn, slots, length, width
    )
    activated, slope = hidden_forward(mlp_in, w_mlp, b_fc1)
    grad_two = grad_rows(activated, d_mlp)

    def halves(gradient):
        return gradient.reshape(lines, 2, gradient.shape[0] // (2 * lines), gradient.shape[1])

    def line_sum(both):
        return lax.psum_scatter(
            both.reshape(-1, both.shape[-1]), "fsdp", scatter_dimension=0, tiled=True
        )

    def pair_sum(gradient, there):
        return (own_half(halves(gradient), pair).astype(F32) + there.astype(F32)).astype(BF16)

    grad_two, d_mlp = after(grad_two, d_mlp)
    two_line = line_sum(grad_two)
    d_hidden, hidden_sums = hidden_back(d_mlp, w_mlp, slope)
    grad_one = grad_columns(mlp_in, d_hidden)
    give_one = own_half(halves(grad_one), 1 - pair)
    give_one, d_hidden = after(give_one, d_hidden)
    there_one = swap_with(give_one, "dp", 1)
    mlp_out, d_mlp_in = mlp_rest(activated, d_hidden, w_mlp)
    result, d_middle, d_attn, d_attended, middle_rows = middle_back(
        mlp_out, bias, d_mlp_in, middle, attn_out, cot, mod, w_attn, slots, length, width
    )
    grad_proj = grad_columns(attended, d_attn)
    grad_proj, d_attended = after(grad_proj, d_attended)
    d_packed, packed_sums = attention_back(packed, d_attended, log_total, slots, length, width)
    grad_qkv = grad_columns(attn_in, d_packed)
    give_attn = own_half(halves(grad_qkv), 1 - pair)
    give_proj = own_half(halves(grad_proj), 1 - pair)
    give_attn, give_proj, d_packed = after(give_attn, give_proj, d_packed)
    there_proj = swap_with(give_proj, "dp", 1)
    in_grad, input_rows = input_back(d_packed, w_attn, x, d_middle, mod, slots, length, width)

    there_one, give_attn, in_grad, input_rows = after(there_one, give_attn, in_grad, input_rows)
    there_attn = swap_with(give_attn, "dp", 1)
    one_both = pair_sum(grad_one, there_one)
    one_half = line_sum(one_both)
    two_line, one_both, there_proj, input_rows = after(two_line, one_both, there_proj, input_rows)

    d_modulation = jnp.concatenate([input_rows[:, :2], middle_rows[:, 2:6]], axis=1).astype(BF16)
    packed_total = jnp.sum(packed_sums, axis=0)
    bias_sums = jnp.concatenate(
        [
            packed_total[0],
            packed_total[2],
            jnp.sum(middle_rows[:, 6], axis=0),
            hidden_sums[0],
            jnp.sum(mlp_sums[:, 0], axis=0),
        ]
    ).astype(BF16)

    report = jnp.concatenate([style.reshape(-1), d_modulation.reshape(-1), bias_sums])
    report = jnp.stack([report, swap_with(report, "dp", 1)])
    reports = gather_line(report, "fsdp").reshape(2 * lines, -1)
    edge = slots * width
    style_group = reports[:, :edge].reshape(2 * lines * slots, width)
    mod_group = reports[:, edge : 7 * edge].reshape(2 * lines * slots, 6 * width)
    style_own = lax.dynamic_slice_in_dim(style_group, line * rows, rows, axis=1)
    grad_ada = dot_tn(style_own, mod_group)
    bias_group = jnp.concatenate(
        [
            jnp.sum(mod_group.astype(F32), axis=0),
            jnp.sum(reports[:, 7 * edge :].astype(F32), axis=0),
        ]
    )
    own_bias = biases.shape[0]
    grad_bias = lax.dynamic_slice_in_dim(bias_group, line * own_bias, own_bias, axis=0)

    power = step_count[0].astype(F32)
    fix_one = 1.0 - jnp.power(BETA_ONE, power)
    fix_two = 1.0 - jnp.power(BETA_TWO, power)
    rates = learning_rates(D, FF)
    reduced = [None] * 6
    firsts_out = [None] * 6
    seconds_out = [None] * 6
    deltas_out = [None] * 6
    outers_out = [None] * 6
    weights_out = [None] * 6

    low = rep % 2
    where = jnp.stack([pair, low]).astype(jnp.int32)
    fixes = jnp.stack([fix_one, fix_two])

    def local_delta(master, first, second, gradient, rate):
        first_next, second_next = adam_moments(first, second, gradient)
        delta = adam_delta(master, first_next, second_next, rate, fix_one, fix_two)
        return delta, first_next, second_next

    def state(index):
        return masters[index], firsts[index][0], seconds[index][0], rates[index]

    def sum_near(keep, give):
        return (keep.astype(F32) + swap_with(give, "rep", 1).astype(F32)).astype(BF16)

    def sum_far(total):
        return (total.astype(F32) + swap_with(total, "rep", 2).astype(F32)).astype(BF16)

    def outer_step(index, totals, shift=0):
        deltas_out[index], outers_out[index], weights_out[index] = outer_whole(
            where, totals, masters[index], outers[index], groups, shift
        )

    reduced[0] = grad_ada
    firsts_out[0], seconds_out[0], ada_keep, ada_give = adam_whole(
        "given", where, fixes, [grad_ada], *state(0)
    )
    one_half, there_attn, two_line, ada_keep, ada_give, grad_bias = after(
        one_half, there_attn, two_line, ada_keep, ada_give, grad_bias
    )
    attn_both = jnp.concatenate(
        [pair_sum(grad_qkv, there_attn), pair_sum(grad_proj, there_proj)], axis=2
    )
    attn_both, two_line, one_half, ada_give, grad_bias = after(
        attn_both, two_line, one_half, ada_give, grad_bias
    )
    attn_half = line_sum(attn_both)
    ada_total = sum_far(sum_near(ada_keep, ada_give))
    one_near = sum_near(*adam_own(where, fixes, one_half, [state(3)]))
    one_far = swap_with(one_near, "rep", 2)
    two_there = swap_with(two_line, "dp", 1)
    ada_total, one_half = after(ada_total, one_half)
    one_there = swap_with(one_half, "dp", 1)
    outer_step(0, [ada_total, swap_with(ada_total, "rep", 1)])
    two_there, weights_out[0], one_far = after(two_there, weights_out[0], one_far)
    one_total = (one_near.astype(F32) + one_far.astype(F32)).astype(BF16)
    one_pair = swap_with(one_total, "dp", 1)
    reduced[4], firsts_out[4], seconds_out[4], two_keep, two_give = adam_whole(
        "sum", where, fixes, [two_line, two_there], *state(4)
    )
    bias_delta, bias_first, bias_second = local_delta(
        biases, first_bias[0], second_bias[0], grad_bias, rates[5]
    )
    reduced[5] = grad_bias
    firsts_out[5], seconds_out[5] = bias_first[None], bias_second[None]
    bias_total = (bias_delta.astype(F32) + swap_with(bias_delta, "rep", 1).astype(F32)).astype(BF16)
    bias_total = bias_total.astype(F32) + swap_with(bias_total, "rep", 2).astype(F32)
    deltas_out[5] = bias_total / groups
    outers_out[5] = OUTER_MOMENTUM * outer_bias + deltas_out[5]
    weights_out[5] = biases - OUTER_RATE * (deltas_out[5] + OUTER_MOMENTUM * outers_out[5])
    attn_half, two_keep, two_give, one_there, one_pair = after(
        attn_half, two_keep, two_give, one_there, one_pair
    )
    attn_near = sum_near(*adam_own(where, fixes, attn_half, [state(1), state(2)]))
    attn_there = swap_with(attn_half, "dp", 1)
    attn_far = swap_with(attn_near, "rep", 2)
    reduced[3], firsts_out[3], seconds_out[3] = adam_whole(
        "halves", where, fixes, [one_half, one_there], *state(3)
    )
    outer_step(
        3, [one_total, one_pair, swap_with(one_total, "rep", 1), swap_with(one_pair, "rep", 1)]
    )
    attn_far, attn_there, firsts_out[3], weights_out[3] = after(
        attn_far, attn_there, firsts_out[3], weights_out[3]
    )
    attn_total = (attn_near.astype(F32) + attn_far.astype(F32)).astype(BF16)
    attn_pair = swap_with(attn_total, "dp", 1)
    two_near, attn_total = after(sum_near(two_keep, two_give), attn_total)
    two_far = swap_with(two_near, "rep", 2)
    attn_units = 3
    for index, shift in ((1, 0), (2, attn_units)):
        reduced[index], firsts_out[index], seconds_out[index] = adam_whole(
            "halves", where, fixes, [attn_half, attn_there], *state(index), shift=shift
        )
    two_far, firsts_out[1], firsts_out[2] = after(two_far, firsts_out[1], firsts_out[2])
    two_total = (two_near.astype(F32) + two_far.astype(F32)).astype(BF16)
    outer_step(4, [two_total, swap_with(two_total, "rep", 1)])
    totals = [attn_total, attn_pair, swap_with(attn_total, "rep", 1), swap_with(attn_pair, "rep", 1)]
    outer_step(1, totals)
    outer_step(2, totals, attn_units)
    grads_out = tuple((g if g.ndim == f.ndim else g[None] for g, f in zip(reduced, firsts)))
    return (
        (result.reshape(images.shape), in_grad.reshape(images.shape))
        + grads_out
        + tuple(firsts_out)
        + tuple(seconds_out)
        + tuple(deltas_out)
        + tuple(outers_out)
        + tuple(weights_out)
    )


def solution(mesh):
    in_specs = (
        P(("rep", "dp", "fsdp"), None, None),
        P(("rep", "dp", "fsdp"), None, None),
        P(("rep", "dp", "fsdp")),
        P(("rep", "dp", "fsdp")),
        P(("rep", "dp", "fsdp")),
        P(),
        P(),
        P("fsdp", None),
        P("fsdp", None),
        P("fsdp", None),
        P("fsdp", None),
        P("fsdp", None),
        P("fsdp"),
        P("rep", "fsdp", None),
        P("rep", "fsdp", None),
        P("rep", "fsdp", None),
        P("rep", "fsdp", None),
        P("rep", "fsdp", None),
        P("rep", "fsdp"),
        P("rep", "fsdp", None),
        P("rep", "fsdp", None),
        P("rep", "fsdp", None),
        P("rep", "fsdp", None),
        P("rep", "fsdp", None),
        P("rep", "fsdp"),
        P("fsdp", None),
        P("fsdp", None),
        P("fsdp", None),
        P("fsdp", None),
        P("fsdp", None),
        P("fsdp"),
    )
    out_specs = (
        P(("rep", "dp", "fsdp"), None, None),
        P(("rep", "dp", "fsdp"), None, None),
        P("rep", "fsdp", None),
        P("rep", "fsdp", None),
        P("rep", "fsdp", None),
        P("rep", "fsdp", None),
        P("rep", "fsdp", None),
        P("rep", "fsdp"),
        P("rep", "fsdp", None),
        P("rep", "fsdp", None),
        P("rep", "fsdp", None),
        P("rep", "fsdp", None),
        P("rep", "fsdp", None),
        P("rep", "fsdp"),
        P("rep", "fsdp", None),
        P("rep", "fsdp", None),
        P("rep", "fsdp", None),
        P("rep", "fsdp", None),
        P("rep", "fsdp", None),
        P("rep", "fsdp"),
        P("fsdp", None),
        P("fsdp", None),
        P("fsdp", None),
        P("fsdp", None),
        P("fsdp", None),
        P("fsdp"),
        P("fsdp", None),
        P("fsdp", None),
        P("fsdp", None),
        P("fsdp", None),
        P("fsdp", None),
        P("fsdp"),
        P("fsdp", None),
        P("fsdp", None),
        P("fsdp", None),
        P("fsdp", None),
        P("fsdp", None),
        P("fsdp"),
    )
    return jax.shard_map(body, mesh=mesh, in_specs=in_specs, out_specs=out_specs, check_vma=False)
```

```python
import functools
import math

import jax
import jax.numpy as jnp
from jax import lax
from jax.experimental import pallas as pl
from jax.experimental.pallas import tpu as pltpu
from jax.sharding import PartitionSpec as P

D = 1152
HEADS = 16
FF = 4608


NORM_EPS = 1e-06
BETA_ONE = 0.9
BETA_TWO = 0.95
ADAM_EPS = 1e-08
WEIGHT_DECAY = 0.1
OUTER_RATE = 0.7
OUTER_MOMENTUM = 0.9
FEW = 8

F32 = jnp.float32
BF16 = jnp.bfloat16
SMALL = pl.CostEstimate(flops=1024, bytes_accessed=1024, transcendentals=0)


def dot(left, right):
    return jnp.dot(left, right, preferred_element_type=F32)


def dot_nt(left, right):
    return lax.dot_general(left, right, (((1,), (1,)), ((), ())), preferred_element_type=F32)


def dot_tn(left, right):
    return lax.dot_general(left, right, (((0,), (0,)), ((), ())), preferred_element_type=F32)


def time_embed(steps, width):
    half = width // 2
    frequency = jnp.exp(-math.log(10000.0) * jnp.arange(half).astype(F32) / half)
    angles = steps.astype(F32)[:, None] * frequency[None, :]
    return jnp.concatenate([jnp.cos(angles), jnp.sin(angles)], axis=1)


def learning_rates(width, hidden):
    return (
        2.0 / math.sqrt(width),
        2.0 / math.sqrt(width),
        2.0 / math.sqrt(width // 32),
        2.0 / math.sqrt(width),
        2.0 / math.sqrt(hidden),
        0.3,
    )


def shift_by(value, axis, step):
    size = lax.axis_size(axis)
    return lax.ppermute(value, axis, [(i, (i + step) % size) for i in range(size)])


def swap_with(value, axis, bit):
    size = lax.axis_size(axis)
    return lax.ppermute(value, axis, [(i, i ^ bit) for i in range(size)])


def gather_line(value, axis):
    size = lax.axis_size(axis)
    if size > FEW:
        return lax.all_gather(value, axis, axis=0)
    place = lax.axis_index(axis)
    result = jnp.zeros((size,) + value.shape, value.dtype)
    for step in range(size):
        piece = value if step == 0 else shift_by(value, axis, step)
        result = lax.dynamic_update_index_in_dim(result, piece, (place - step) % size, 0)
    return result


def scatter_line(value, axis):
    size = lax.axis_size(axis)
    if size > FEW:
        return lax.psum_scatter(value, axis, scatter_dimension=0, tiled=False)
    place = lax.axis_index(axis)
    total = lax.dynamic_index_in_dim(value, place, 0, keepdims=False)
    for step in range(1, size):
        piece = lax.dynamic_index_in_dim(value, (place + step) % size, 0, keepdims=False)
        total = total + shift_by(piece, axis, step)
    return total


def moments(values):
    center = values - jnp.mean(values, axis=-1, keepdims=True)
    inverse = lax.rsqrt(jnp.mean(center * center, axis=-1, keepdims=True) + NORM_EPS)
    return center * inverse, inverse


def norm_back(normed, inverse, upstream):
    first = jnp.mean(upstream, axis=-1, keepdims=True)
    second = jnp.mean(upstream * normed, axis=-1, keepdims=True)
    return (upstream - first - normed * second) * inverse


def gelu_pair(h):
    c = math.sqrt(2.0 / math.pi)
    inner = c * (h + 0.044715 * h * h * h)
    t = jnp.tanh(inner)
    value = 0.5 * h * (1.0 + t)
    slope = 0.5 * (1.0 + t) + 0.5 * h * (1.0 - t * t) * c * (1.0 + 3.0 * 0.044715 * h * h)
    return value, slope


def head_window(head, head_dim):
    low = head * head_dim
    start = low // 128 * 128
    stop = -(-(low + head_dim) // 128) * 128
    return start, stop, low - start


def head_mask(shape, offset, head_dim):
    lane = lax.broadcasted_iota(jnp.int32, shape, 1)
    return (lane >= offset) & (lane < offset + head_dim)


def attention_forward_kernel(
    x_ref, cot_ref, mod_ref, bias_ref, weight_ref,
    attn_in_ref, packed_ref, attended_ref, log_ref, attn_ref, x1_ref, mlp_in_ref, d_mlp_ref, sums_ref,
    gather_ref,
):
    length, width = x_ref.shape
    head_dim = width // HEADS
    factor = 1.0 / math.sqrt(head_dim)
    residual = x_ref[...].astype(F32)
    normed, _ = moments(residual)
    attn_in_ref[...] = (normed * (1.0 + mod_ref[0, 1:2]) + mod_ref[0, 0:1]).astype(BF16)
    for unit in range(3):
        piece = dot(attn_in_ref[...], weight_ref[unit]) + bias_ref[unit : unit + 1]
        packed_ref[:, unit * width : (unit + 1) * width] = piece.astype(BF16)
    for head in range(HEADS):
        start, stop, offset = head_window(head, head_dim)
        mask = head_mask((length, stop - start), offset, head_dim)
        query = packed_ref[:, start:stop]
        query = jnp.where(mask, query, jnp.zeros_like(query))
        keys = packed_ref[:, width + start : width + stop]
        values = packed_ref[:, 2 * width + start : 2 * width + stop]
        scores = dot_nt(query, keys) * factor
        top = jnp.max(scores, axis=-1, keepdims=True)
        raised = jnp.exp(scores - top)
        summed = jnp.sum(raised, axis=-1, keepdims=True)
        probs = (raised * (1.0 / summed)).astype(BF16)
        log_ref[:, head : head + 1] = top + jnp.log(summed)
        out = dot(probs, values)
        if offset == 0:
            gather_ref[:, start:stop] = out
        else:
            gather_ref[:, start:stop] = jnp.where(mask, out, gather_ref[:, start:stop])
    attended_ref[...] = gather_ref[...].astype(BF16)
    attn = dot(attended_ref[...], weight_ref[3]) + bias_ref[3:4]
    attn_ref[...] = attn
    middle = residual + mod_ref[0, 2:3] * attn
    x1_ref[...] = middle
    normed_two, _ = moments(middle)
    mlp_in_ref[...] = (normed_two * (1.0 + mod_ref[0, 4:5]) + mod_ref[0, 3:4]).astype(BF16)
    d_mlp = (mod_ref[0, 5:6] * (cot_ref[...].astype(F32) * mod_ref[0, 6:7])).astype(BF16)
    d_mlp_ref[...] = d_mlp
    sums_ref[0, 0:1] = jnp.sum(d_mlp.astype(F32), axis=0, keepdims=True)


def rows_spec(length, width):
    return pl.BlockSpec((length, width), lambda i: (i, 0))


def whole_spec(shape):
    return pl.BlockSpec(shape, lambda i: (0,) * len(shape), pipeline_mode=pl.Buffered(1))


def lead_spec(rows, width):
    return pl.BlockSpec((1, rows, width), lambda i: (i, 0, 0))


def params(megabytes):
    return pltpu.CompilerParams(vmem_limit_bytes=megabytes << 20)


def attention_forward(x, cot, mod, bias, weights, slots, length, width):
    tokens = slots * length
    row = rows_spec(length, width)
    return pl.pallas_call(
        attention_forward_kernel,
        grid=(slots,),
        in_specs=[row, row, lead_spec(8, width), whole_spec((8, width)), whole_spec((4, width, width))],
        out_specs=[
            row, rows_spec(length, 3 * width), row, rows_spec(length, 128), row, row, row, row,
            lead_spec(8, width),
        ],
        out_shape=[
            jax.ShapeDtypeStruct((tokens, width), BF16),
            jax.ShapeDtypeStruct((tokens, 3 * width), BF16),
            jax.ShapeDtypeStruct((tokens, width), BF16),
            jax.ShapeDtypeStruct((tokens, 128), F32),
            jax.ShapeDtypeStruct((tokens, width), F32),
            jax.ShapeDtypeStruct((tokens, width), F32),
            jax.ShapeDtypeStruct((tokens, width), BF16),
            jax.ShapeDtypeStruct((tokens, width), BF16),
            jax.ShapeDtypeStruct((slots, 8, width), F32),
        ],
        scratch_shapes=[pltpu.VMEM((length, width), F32)],
        compiler_params=params(48),
        cost_estimate=pl.CostEstimate(
            flops=2 * tokens * width * width * 4, bytes_accessed=40 << 20, transcendentals=0
        ),
    )(x, cot, mod, bias, weights)


def one_spec(joint):
    lines, rows, width = joint.shape[1], joint.shape[4], joint.shape[5]
    return pl.BlockSpec((1, lines, 2, 1, rows, width), lambda u: (u, 0, 0, 0, 0, 0))


def two_spec(joint):
    groups, lines, _, _, rows, width = joint.shape
    return pl.BlockSpec((groups, lines // groups, 2, 1, rows, width), lambda u: (0, u, 0, 1, 0, 0))


def one_of(ref):
    return ref[...].reshape(ref.shape[-1], ref.shape[-1])


def two_of(ref):
    value = ref[...]
    if value.shape[1] > 1:
        value = jnp.swapaxes(value, 0, 1)
    return value.reshape(ref.shape[-1], ref.shape[-1])


def hidden_kernel(mlp_in_ref, weight_ref, bias_ref, act_ref, slope_ref):
    step = 256

    def chunk(index, carry):
        here = pl.ds(pl.multiple_of(index * step, step), step)
        hidden = dot(mlp_in_ref[here, :], one_of(weight_ref)) + bias_ref[0:1]
        value, slope = gelu_pair(hidden)
        act_ref[here, :] = value.astype(BF16)
        slope_ref[here, :] = slope.astype(BF16)
        return carry

    lax.fori_loop(0, mlp_in_ref.shape[0] // step, chunk, 0)


def hidden_forward(mlp_in, weights, bias):
    tokens, width = mlp_in.shape
    units = weights.shape[0]
    column = pl.BlockSpec((tokens, width), lambda u: (0, u))
    return pl.pallas_call(
        hidden_kernel,
        grid=(units,),
        in_specs=[whole_spec((tokens, width)), one_spec(weights), pl.BlockSpec((1, width), lambda u: (0, u))],
        out_specs=[column, column],
        out_shape=[jax.ShapeDtypeStruct((tokens, units * width), BF16)] * 2,
        compiler_params=params(48),
        cost_estimate=pl.CostEstimate(
            flops=2 * tokens * width * width * units, bytes_accessed=26 << 20, transcendentals=0
        ),
    )(mlp_in, weights, bias)


def hidden_back_kernel(d_mlp_ref, weight_ref, slope_ref, d_hidden_ref, sums_ref):
    step = 256

    def chunk(index, carry):
        here = pl.ds(pl.multiple_of(index * step, step), step)
        d_hidden = dot_nt(d_mlp_ref[here, :], two_of(weight_ref)) * slope_ref[here, :].astype(F32)
        d_hidden = d_hidden.astype(BF16)
        d_hidden_ref[here, :] = d_hidden
        return carry + jnp.sum(d_hidden.astype(F32), axis=0, keepdims=True)

    zero = jnp.zeros((1, slope_ref.shape[1]), F32)
    sums_ref[0:1] = lax.fori_loop(0, d_mlp_ref.shape[0] // step, chunk, zero)


def hidden_back(d_mlp, weights, slope):
    tokens, width = d_mlp.shape
    units = weights.shape[0]
    column = pl.BlockSpec((tokens, width), lambda u: (0, u))
    return pl.pallas_call(
        hidden_back_kernel,
        grid=(units,),
        in_specs=[whole_spec((tokens, width)), two_spec(weights), column],
        out_specs=[column, pl.BlockSpec((8, width), lambda u: (0, u))],
        out_shape=[
            jax.ShapeDtypeStruct((tokens, units * width), BF16),
            jax.ShapeDtypeStruct((8, units * width), F32),
        ],
        compiler_params=params(48),
        cost_estimate=pl.CostEstimate(
            flops=2 * tokens * width * width * units, bytes_accessed=26 << 20, transcendentals=0
        ),
    )(d_mlp, weights, slope)


def mlp_rest_kernel(act_ref, d_hidden_ref, two_ref, one_ref, mlp_ref, d_in_ref):
    step = 256

    @pl.when(pl.program_id(0) == 0)
    def _():
        mlp_ref[...] = jnp.zeros_like(mlp_ref)
        d_in_ref[...] = jnp.zeros_like(d_in_ref)

    def chunk(index, carry):
        here = pl.ds(pl.multiple_of(index * step, step), step)
        mlp_ref[here, :] += dot(act_ref[here, :], two_of(two_ref))
        d_in_ref[here, :] += dot_nt(d_hidden_ref[here, :], one_of(one_ref))
        return carry

    lax.fori_loop(0, act_ref.shape[0] // step, chunk, 0)


def mlp_rest(act, d_hidden, weights):
    tokens = act.shape[0]
    units, width = weights.shape[0], weights.shape[-1]
    column = pl.BlockSpec((tokens, width), lambda u: (0, u))
    total = pl.BlockSpec((tokens, width), lambda u: (0, 0))
    return pl.pallas_call(
        mlp_rest_kernel,
        grid=(units,),
        in_specs=[column, column, two_spec(weights), one_spec(weights)],
        out_specs=[total, total],
        out_shape=[jax.ShapeDtypeStruct((tokens, width), F32)] * 2,
        compiler_params=params(48),
        cost_estimate=pl.CostEstimate(
            flops=4 * tokens * width * width * units, bytes_accessed=42 << 20, transcendentals=0
        ),
    )(act, d_hidden, weights, weights)


def middle_back_kernel(
    mlp_ref, bias_ref, d_in_ref, x1_ref, attn_ref, cot_ref, mod_ref, weight_ref,
    out_ref, d_mid_ref, d_attn_ref, d_att_ref, rows_ref,
):
    live = mod_ref[0, 6:7]
    gate_two = mod_ref[0, 5:6]
    upstream = cot_ref[...].astype(F32) * live
    middle = x1_ref[...]
    mlp = mlp_ref[...] + bias_ref[4:5]
    out_ref[...] = ((middle + gate_two * mlp) * live).astype(BF16)
    rows_ref[0, 5:6] = jnp.sum(upstream * mlp, axis=0, keepdims=True)
    normed, inverse = moments(middle)
    d_in = d_in_ref[...]
    rows_ref[0, 3:4] = jnp.sum(d_in, axis=0, keepdims=True)
    rows_ref[0, 4:5] = jnp.sum(d_in * normed, axis=0, keepdims=True)
    d_mid = upstream + norm_back(normed, inverse, d_in * (1.0 + mod_ref[0, 4:5]))
    d_mid_ref[...] = d_mid
    rows_ref[0, 2:3] = jnp.sum(d_mid * attn_ref[...], axis=0, keepdims=True)
    d_attn = (mod_ref[0, 2:3] * d_mid).astype(BF16)
    d_attn_ref[...] = d_attn
    rows_ref[0, 6:7] = jnp.sum(d_attn.astype(F32), axis=0, keepdims=True)
    d_att_ref[...] = dot_nt(d_attn_ref[...], weight_ref[0]).astype(BF16)


def middle_back(mlp, bias, d_in, x1, attn, cot, mod, weights, slots, length, width):
    tokens = slots * length
    row = rows_spec(length, width)
    proj = pl.BlockSpec((1, width, width), lambda i: (3, 0, 0), pipeline_mode=pl.Buffered(1))
    return pl.pallas_call(
        middle_back_kernel,
        grid=(slots,),
        in_specs=[row, whole_spec((8, width)), row, row, row, row, lead_spec(8, width), proj],
        out_specs=[row, row, row, row, lead_spec(8, width)],
        out_shape=[
            jax.ShapeDtypeStruct((tokens, width), BF16),
            jax.ShapeDtypeStruct((tokens, width), F32),
            jax.ShapeDtypeStruct((tokens, width), BF16),
            jax.ShapeDtypeStruct((tokens, width), BF16),
            jax.ShapeDtypeStruct((slots, 8, width), F32),
        ],
        compiler_params=params(48),
        cost_estimate=pl.CostEstimate(
            flops=2 * tokens * width * width, bytes_accessed=30 << 20, transcendentals=0
        ),
    )(mlp, bias, d_in, x1, attn, cot, mod, weights)


def attention_back_kernel(packed_ref, d_att_ref, log_ref, d_packed_ref, sums_ref, q_ref, k_ref, v_ref):
    length, width = d_att_ref.shape
    head_dim = width // HEADS
    factor = 1.0 / math.sqrt(head_dim)
    for head in range(HEADS):
        start, stop, offset = head_window(head, head_dim)
        mask = head_mask((length, stop - start), offset, head_dim)
        query = packed_ref[:, start:stop]
        query_one = jnp.where(mask, query, jnp.zeros_like(query))
        keys = packed_ref[:, width + start : width + stop]
        values = packed_ref[:, 2 * width + start : 2 * width + stop]
        d_att = d_att_ref[:, start:stop]
        d_att = jnp.where(mask, d_att, jnp.zeros_like(d_att))
        weights = jnp.exp(dot_nt(query_one, keys) * factor - log_ref[:, head : head + 1])
        d_probs = dot_nt(d_att, values)
        inner = jnp.sum(weights * d_probs, axis=-1, keepdims=True)
        d_scores = (weights * (d_probs - inner)).astype(BF16)
        probs = weights.astype(BF16)
        pieces = (
            (q_ref, dot(d_scores, keys) * factor),
            (k_ref, dot_tn(d_scores, query) * factor),
            (v_ref, dot_tn(probs, d_att)),
        )
        for ref, piece in pieces:
            if offset == 0:
                ref[:, start:stop] = piece
            else:
                ref[:, start:stop] = jnp.where(mask, piece, ref[:, start:stop])
    for unit, ref in enumerate((q_ref, k_ref, v_ref)):
        piece = ref[...].astype(BF16)
        d_packed_ref[:, unit * width : (unit + 1) * width] = piece
        sums_ref[0, unit : unit + 1] = jnp.sum(piece.astype(F32), axis=0, keepdims=True)


def attention_back(packed, d_att, log, slots, length, width):
    tokens = slots * length
    return pl.pallas_call(
        attention_back_kernel,
        grid=(slots,),
        in_specs=[rows_spec(length, 3 * width), rows_spec(length, width), rows_spec(length, 128)],
        out_specs=[rows_spec(length, 3 * width), lead_spec(8, width)],
        out_shape=[
            jax.ShapeDtypeStruct((tokens, 3 * width), BF16),
            jax.ShapeDtypeStruct((slots, 8, width), F32),
        ],
        scratch_shapes=[pltpu.VMEM((length, width), F32)] * 3,
        compiler_params=params(48),
        cost_estimate=pl.CostEstimate(
            flops=10 * tokens * length * 256 * HEADS, bytes_accessed=14 << 20, transcendentals=0
        ),
    )(packed, d_att, log)


def input_back_kernel(d_packed_ref, weight_ref, x_ref, d_mid_ref, mod_ref, grad_ref, rows_ref):
    width = x_ref.shape[1]
    d_in = dot_nt(d_packed_ref[:, :width], weight_ref[0])
    for unit in (1, 2):
        d_in = d_in + dot_nt(d_packed_ref[:, unit * width : (unit + 1) * width], weight_ref[unit])
    normed, inverse = moments(x_ref[...].astype(F32))
    rows_ref[0, 0:1] = jnp.sum(d_in, axis=0, keepdims=True)
    rows_ref[0, 1:2] = jnp.sum(d_in * normed, axis=0, keepdims=True)
    back = norm_back(normed, inverse, d_in * (1.0 + mod_ref[0, 1:2]))
    grad_ref[...] = (d_mid_ref[...] + back).astype(BF16)


def input_back(d_packed, weights, x, d_mid, mod, slots, length, width):
    tokens = slots * length
    row = rows_spec(length, width)
    return pl.pallas_call(
        input_back_kernel,
        grid=(slots,),
        in_specs=[
            rows_spec(length, 3 * width), whole_spec((3, width, width)), row, row, lead_spec(8, width),
        ],
        out_specs=[row, lead_spec(8, width)],
        out_shape=[
            jax.ShapeDtypeStruct((tokens, width), BF16),
            jax.ShapeDtypeStruct((slots, 8, width), F32),
        ],
        compiler_params=params(48),
        cost_estimate=pl.CostEstimate(
            flops=6 * tokens * width * width, bytes_accessed=20 << 20, transcendentals=0
        ),
    )(d_packed, weights, x, d_mid, mod)


def grad_kernel(left_ref, right_ref, grad_ref):
    step = grad_ref.shape[0] // 3

    def chunk(index, carry):
        here = pl.ds(pl.multiple_of(index * step, step), step)
        grad_ref[here, :] = dot_tn(left_ref[:, here], right_ref[...]).astype(BF16)
        return carry

    lax.fori_loop(0, 3, chunk, 0)


def grad_columns(left, right):
    tokens, rows = left.shape
    width = right.shape[1]
    return pl.pallas_call(
        grad_kernel,
        grid=(width // rows,),
        in_specs=[whole_spec((tokens, rows)), pl.BlockSpec((tokens, rows), lambda u: (0, u))],
        out_specs=pl.BlockSpec((rows, rows), lambda u: (0, u)),
        out_shape=jax.ShapeDtypeStruct((rows, width), BF16),
        compiler_params=params(48),
        cost_estimate=pl.CostEstimate(
            flops=2 * tokens * rows * width, bytes_accessed=2 * rows * width + 4 * tokens * width, transcendentals=0
        ),
    )(left, right)


def grad_rows(left, right):
    tokens, rows = left.shape
    width = right.shape[1]
    return pl.pallas_call(
        grad_kernel,
        grid=(rows // width,),
        in_specs=[pl.BlockSpec((tokens, width), lambda u: (0, u)), whole_spec((tokens, width))],
        out_specs=rows_spec(width, width),
        out_shape=jax.ShapeDtypeStruct((rows, width), BF16),
        compiler_params=params(48),
        cost_estimate=pl.CostEstimate(
            flops=2 * tokens * rows * width, bytes_accessed=2 * rows * width + 4 * tokens * rows, transcendentals=0
        ),
    )(left, right)


def after(*values):
    return lax.optimization_barrier(values)


def adam_moments(first, second, gradient):
    first_next = BETA_ONE * first + (1.0 - BETA_ONE) * gradient
    second_next = BETA_TWO * second + (1.0 - BETA_TWO) * gradient * gradient
    return first_next, second_next


def adam_delta(master, first_next, second_next, rate, fix_one, fix_two):
    step = first_next / fix_one / (jnp.sqrt(second_next / fix_two) + ADAM_EPS)
    return (rate * (step + WEIGHT_DECAY * master)).astype(BF16)


def whole_kernel(mode, rate, where_ref, fix_ref, *refs):
    half = pl.program_id(2)
    if mode == "sum":
        a_ref, b_ref, master_ref, first_ref, second_ref, grad_ref, m_ref, v_ref, keep_ref, give_ref = refs
        gradient = a_ref[0].astype(F32) + b_ref[0].astype(F32)
        grad_ref[0] = gradient
    elif mode == "given":
        g_ref, master_ref, first_ref, second_ref, m_ref, v_ref, keep_ref, give_ref = refs
        gradient = g_ref[0]
    else:
        own_ref, other_ref, first_ref, second_ref, grad_ref, m_ref, v_ref = refs
        gradient = jnp.where(half == where_ref[0], own_ref[...].astype(F32), other_ref[...].astype(F32))
        grad_ref[0] = gradient
    first_next, second_next = adam_moments(first_ref[0], second_ref[0], gradient)
    m_ref[0] = first_next
    v_ref[0] = second_next
    if mode != "halves":
        delta = adam_delta(master_ref[0], first_next, second_next, rate, fix_ref[0], fix_ref[1])

        @pl.when(half == where_ref[1])
        def _():
            keep_ref[...] = delta

        @pl.when(half != where_ref[1])
        def _():
            give_ref[...] = delta


def row_block(rows):
    return 144 if rows % 144 == 0 else rows


def adam_whole(mode, where, fixes, gradients, master, first, second, rate, shift=0):
    rows, columns = master.shape
    half, width = rows // 2, D
    block = row_block(half)
    three = pl.BlockSpec((1, block, width), lambda c, r, h, w: (h, r, c))
    flat = pl.BlockSpec((block, width), lambda c, r, h, w: (r, c))
    moved = pl.BlockSpec((block, width), lambda c, r, h, w: (r, c + shift))
    view = (2, half, columns)
    state = [first.reshape(view), second.reshape(view)]
    if mode == "halves":
        operands = list(gradients) + state
        in_specs = [moved, moved, three, three]
    else:
        operands = [g.reshape(view) for g in gradients] + [master.reshape(view)] + state
        in_specs = [three] * len(operands)
    wide = jax.ShapeDtypeStruct(view, F32)
    thin = jax.ShapeDtypeStruct((half, columns), BF16)
    count = 2 if mode == "given" else 3
    extra = 0 if mode == "halves" else 2
    outs = pl.pallas_call(
        functools.partial(whole_kernel, mode, rate),
        grid_spec=pltpu.PrefetchScalarGridSpec(
            num_scalar_prefetch=1,
            grid=(columns // width, half // block, 2),
            in_specs=[pl.BlockSpec(memory_space=pltpu.SMEM)] + in_specs,
            out_specs=[three] * count + [flat] * extra,
        ),
        out_shape=[wide] * count + [thin] * extra,
        compiler_params=params(48),
        cost_estimate=SMALL,
    )(where, fixes, *operands)
    return [out.reshape(1, rows, columns) for out in outs[:count]] + list(outs[count:])


def own_kernel(rates, where_ref, fix_ref, g_ref, *refs):
    states, keep_ref, give_ref = refs[:-2], refs[-2], refs[-1]
    unit, core = pl.program_id(0), pl.program_id(1)

    def run(kind):
        master_ref, first_ref, second_ref = states[3 * kind : 3 * kind + 3]
        first_next, second_next = adam_moments(first_ref[0, 0], second_ref[0, 0], g_ref[0].astype(F32))
        delta = adam_delta(
            master_ref[0, 0], first_next, second_next, rates[kind][1], fix_ref[0], fix_ref[1]
        )

        @pl.when(core == where_ref[1])
        def _():
            keep_ref[...] = delta

        @pl.when(core != where_ref[1])
        def _():
            give_ref[...] = delta

    start = 0
    for kind, (units, _) in enumerate(rates):
        stop = start + units

        @pl.when((unit >= start) & (unit < stop))
        def _():
            run(kind)

        start = stop


def adam_own(where, fixes, gradient, weights):
    half, columns = gradient.shape
    quarter, width = half // 2, D
    operands, in_specs, rates = [gradient.reshape(2, quarter, columns)], [], []
    in_specs.append(pl.BlockSpec((1, quarter, width), lambda c, h, w: (h, 0, c)))
    start = 0
    for master, first, second, rate in weights:
        units = master.shape[1] // width
        low = start

        def place(c, h, w, low=low, units=units):
            return (w[0], h, 0, jnp.clip(c - low, 0, units - 1))

        for value in (master, first, second):
            operands.append(value.reshape(2, 2, quarter, value.shape[-1]))
            in_specs.append(pl.BlockSpec((1, 1, quarter, width), place))
        rates.append((units, rate))
        start += units
    flat = pl.BlockSpec((quarter, width), lambda c, h, w: (0, c))
    return pl.pallas_call(
        functools.partial(own_kernel, tuple(rates)),
        grid_spec=pltpu.PrefetchScalarGridSpec(
            num_scalar_prefetch=1,
            grid=(columns // width, 2),
            in_specs=[pl.BlockSpec(memory_space=pltpu.SMEM)] + in_specs,
            out_specs=[flat, flat],
        ),
        out_shape=[jax.ShapeDtypeStruct((quarter, columns), BF16)] * 2,
        compiler_params=params(48),
        cost_estimate=SMALL,
    )(where, fixes, *operands)


def outer_kernel(scale, where_ref, *refs):
    totals, master_ref, outer_ref, delta_ref, next_ref, weight_ref = refs[:-5], *refs[-5:]
    core = pl.program_id(2)
    if len(totals) == 2:
        own, other = totals[0][...], totals[1][...]
    else:
        mine = pl.program_id(1) == where_ref[0]
        own = jnp.where(mine, totals[0][...], totals[1][...])
        other = jnp.where(mine, totals[2][...], totals[3][...])
    delta = jnp.where(core == where_ref[1], own.astype(F32), other.astype(F32)) * scale
    outer_next = OUTER_MOMENTUM * outer_ref[...].reshape(delta.shape) + delta
    master = master_ref[...].reshape(delta.shape)
    delta_ref[...] = delta.reshape(delta_ref.shape)
    next_ref[...] = outer_next.reshape(next_ref.shape)
    weight = master - OUTER_RATE * (delta + OUTER_MOMENTUM * outer_next)
    weight_ref[...] = weight.reshape(weight_ref.shape)


def outer_whole(where, totals, master, outer, groups, shift=0):
    rows, columns = master.shape
    width = D
    if len(totals) == 2:
        part = rows // 2
        block = row_block(part)
        view = (2, part, columns)
        grid = (columns // width, part // block, 2)
        state = pl.BlockSpec((1, block, width), lambda c, r, h, w: (h, r, c))
        total = pl.BlockSpec((block, width), lambda c, r, h, w: (r, c + shift))
    else:
        part = rows // 4
        view = (2, 2, part, columns)
        grid = (columns // width, 2, 2)
        state = pl.BlockSpec((1, 1, part, width), lambda c, p, h, w: (p, h, 0, c))
        total = pl.BlockSpec((part, width), lambda c, p, h, w: (0, c + shift))
    outs = pl.pallas_call(
        functools.partial(outer_kernel, 1.0 / groups),
        grid_spec=pltpu.PrefetchScalarGridSpec(
            num_scalar_prefetch=1,
            grid=grid,
            in_specs=[total] * len(totals) + [state, state],
            out_specs=[state] * 3,
        ),
        out_shape=[jax.ShapeDtypeStruct(view, F32)] * 3,
        compiler_params=params(48),
        cost_estimate=SMALL,
    )(where, *totals, master.reshape(view), outer.reshape(view))
    return [out.reshape(rows, columns) for out in outs]


def place_kernel(order_ref, *refs):
    sources, target, held, came, left = refs[:-4], refs[-4], refs[-3], refs[-2], refs[-1]
    inward, outward = [], []
    for which, source in enumerate(sources):
        for block in range(source.shape[0]):
            index = which * source.shape[0] + block
            inward.append(pltpu.make_async_copy(source.at[block], held.at[index], came.at[index]))
            outward.append(
                pltpu.make_async_copy(held.at[index], target.at[order_ref[index]], left.at[index])
            )
    for copy in inward:
        copy.start()
    for first, second in zip(inward, outward):
        first.wait()
        second.start()
    for copy in outward:
        copy.wait()


def place_blocks(order, sources):
    blocks = sum(source.shape[0] for source in sources)
    shape = (blocks,) + sources[0].shape[1:]
    return pl.pallas_call(
        place_kernel,
        grid_spec=pltpu.PrefetchScalarGridSpec(
            num_scalar_prefetch=1,
            grid=(1,),
            in_specs=[pl.BlockSpec(memory_space=pl.ANY)] * len(sources),
            out_specs=pl.BlockSpec(memory_space=pl.ANY),
            scratch_shapes=[
                pltpu.VMEM(shape, sources[0].dtype),
                pltpu.SemaphoreType.DMA((blocks,)),
                pltpu.SemaphoreType.DMA((blocks,)),
            ],
        ),
        out_shape=jax.ShapeDtypeStruct(shape, sources[0].dtype),
        compiler_params=params(48),
        cost_estimate=pl.CostEstimate(
            flops=0, bytes_accessed=4 * blocks * shape[1] * shape[2], transcendentals=0
        ),
    )(order, *sources)


def hops_line(piece):
    near = jnp.stack([piece, shift_by(piece, "fsdp", 1)])
    far = jnp.stack([shift_by(piece, "fsdp", 2), shift_by(piece, "fsdp", 3)])
    return near, far


def hops_side(near, far):
    near = jnp.concatenate([near, swap_with(near, "rep", 2)])
    far = jnp.concatenate([far, swap_with(far, "dp", 1)])
    return near, far


def hops_other(near, far):
    return near, far, swap_with(near, "dp", 1), swap_with(far, "rep", 2)


def hops_core(sources):
    return tuple(sources) + tuple(swap_with(source, "rep", 1) for source in sources)


def hops_place(sources, weigh):
    size = lax.axis_size("fsdp")
    rep, pair, line = lax.axis_index("rep"), lax.axis_index("dp"), lax.axis_index("fsdp")
    order = []
    for core in (0, 1):
        for kind in range(4):
            for block in range(4):
                hop, step = block // 2, block % 2
                if kind in (0, 2):
                    flip_rep, flip_pair, back = hop, kind // 2, step
                else:
                    flip_rep, flip_pair, back = kind // 2, hop, 2 + step
                place = lax.rem(line - back + size, size) * weigh[0]
                place = place + (rep ^ (2 * flip_rep + core)) * weigh[1] + (pair ^ flip_pair) * weigh[2]
                order.append(place)
    return place_blocks(jnp.stack(order).astype(jnp.int32), sources)


def own_half(value, index):
    return lax.dynamic_index_in_dim(value, index, 1, keepdims=False)


def body(
    images,
    cotangent,
    counts,
    timesteps,
    labels,
    label_table,
    step_count,
    w_ada,
    w_qkv,
    w_proj,
    w_fc1,
    w_fc2,
    biases,
    first_ada,
    first_qkv,
    first_proj,
    first_fc1,
    first_fc2,
    first_bias,
    second_ada,
    second_qkv,
    second_proj,
    second_fc1,
    second_fc2,
    second_bias,
    outer_ada,
    outer_qkv,
    outer_proj,
    outer_fc1,
    outer_fc2,
    outer_bias,
):
    masters = (w_ada, w_qkv, w_proj, w_fc1, w_fc2, biases)
    firsts = (first_ada, first_qkv, first_proj, first_fc1, first_fc2, first_bias)
    seconds = (second_ada, second_qkv, second_proj, second_fc1, second_fc2, second_bias)
    outers = (outer_ada, outer_qkv, outer_proj, outer_fc1, outer_fc2, outer_bias)
    slots, length, width = images.shape
    tokens = slots * length
    rows = w_qkv.shape[0]
    rows_two = w_fc2.shape[0]
    lines = lax.axis_size("fsdp")
    groups = lax.axis_size("rep")
    rep = lax.axis_index("rep")
    pair = lax.axis_index("dp")
    line = lax.axis_index("fsdp")
    half = rows // 2
    everyone = ("rep", "fsdp", "dp")

    def rows_of(weight):
        return lax.dynamic_slice_in_dim(weight, pair * half, half, axis=0).astype(BF16)

    attention_cut = jnp.concatenate([rows_of(w_qkv), rows_of(w_proj)], axis=1)
    attention_cut = lax.dynamic_slice_in_dim(attention_cut, rep * width, width, axis=1)
    hops = lines == 4 and groups == 4
    one_cut = lax.dynamic_slice(w_fc1, (pair * half, rep * width), (half, width))
    eighth = rows_two // (2 * groups)
    two_cut = lax.dynamic_slice_in_dim(w_fc2, (rep * 2 + pair) * eighth, eighth, axis=0)
    mlp_cut = jnp.concatenate([one_cut, two_cut]).astype(BF16)
    w_mlp = lax.all_gather(mlp_cut, everyone, axis=0, tiled=True)
    w_mlp = w_mlp.reshape(groups, lines, 2, 2, half, width)
    live = (jnp.arange(slots) < counts[0]).astype(F32)
    condition = time_embed(timesteps, D) + jnp.take(label_table, labels, axis=0).astype(F32)
    style = jax.nn.silu(condition).astype(BF16)
    message = jnp.concatenate([style.reshape(-1), biases.astype(BF16)])
    heard = gather_line(message, "fsdp")
    if hops:
        attention_cut, message = after(attention_cut, message)
        attention_parts = hops_line(attention_cut)
        heard = after(heard, *attention_parts)[0]
        attention_parts = hops_side(*attention_parts)
    else:
        w_attn = lax.all_gather(attention_cut, everyone, axis=0, tiled=True)
    bias_all = heard[:, slots * width :].reshape(-1).astype(F32)
    style_line = heard[:, : slots * width].reshape(lines * slots, width)
    style_cut = lax.dynamic_slice_in_dim(style_line, line * rows, rows, axis=1)
    mod_part = dot(style_cut, w_ada.astype(BF16))
    if hops:
        attention_parts = hops_other(*attention_parts)
        attention_parts = after(*attention_parts, mod_part)[:-1]
        w_attn = hops_place(hops_core(attention_parts), (2, 8, 1))
    w_attn = w_attn.reshape(4, width, width)
    b_ada = bias_all[: 6 * width]
    modulation = scatter_line(mod_part.reshape(lines, slots, 6 * width), "fsdp") + b_ada
    mod = jnp.concatenate(
        [
            modulation.reshape(slots, 6, width),
            jnp.broadcast_to(live[:, None, None], (slots, 2, width)),
        ],
        axis=1,
    )
    b_rest = bias_all[6 * width : 9 * width].reshape(3, width)
    bias = jnp.zeros((8, width), F32)
    bias = bias.at[0].set(b_rest[0]).at[2].set(b_rest[1]).at[3].set(b_rest[2])
    bias = bias.at[4].set(bias_all[9 * width + FF :])
    b_fc1 = bias_all[9 * width : 9 * width + FF].reshape(1, FF)
    x = images.reshape(tokens, width)
    cot = cotangent.reshape(tokens, width)

    attn_in, packed, attended, log_total, attn_out, middle, mlp_in, d_mlp, mlp_sums = attention_forward(
        x, cot, mod, bias, w_attn, slots, length, width
    )
    activated, slope = hidden_forward(mlp_in, w_mlp, b_fc1)
    grad_two = grad_rows(activated, d_mlp)

    def halves(gradient):
        return gradient.reshape(lines, 2, gradient.shape[0] // (2 * lines), gradient.shape[1])

    def line_sum(both):
        return lax.psum_scatter(
            both.reshape(-1, both.shape[-1]), "fsdp", scatter_dimension=0, tiled=True
        )

    def pair_sum(gradient, there):
        return (own_half(halves(gradient), pair).astype(F32) + there.astype(F32)).astype(BF16)

    grad_two, d_mlp = after(grad_two, d_mlp)
    two_line = line_sum(grad_two)
    d_hidden, hidden_sums = hidden_back(d_mlp, w_mlp, slope)
    grad_one = grad_columns(mlp_in, d_hidden)
    give_one = own_half(halves(grad_one), 1 - pair)
    give_one, d_hidden = after(give_one, d_hidden)
    there_one = swap_with(give_one, "dp", 1)
    mlp_out, d_mlp_in = mlp_rest(activated, d_hidden, w_mlp)
    result, d_middle, d_attn, d_attended, middle_rows = middle_back(
        mlp_out, bias, d_mlp_in, middle, attn_out, cot, mod, w_attn, slots, length, width
    )
    grad_proj = grad_columns(attended, d_attn)
    grad_proj, d_attended = after(grad_proj, d_attended)
    d_packed, packed_sums = attention_back(packed, d_attended, log_total, slots, length, width)
    grad_qkv = grad_columns(attn_in, d_packed)
    give_attn = own_half(halves(grad_qkv), 1 - pair)
    give_proj = own_half(halves(grad_proj), 1 - pair)
    give_attn, give_proj, d_packed = after(give_attn, give_proj, d_packed)
    there_proj = swap_with(give_proj, "dp", 1)
    in_grad, input_rows = input_back(d_packed, w_attn, x, d_middle, mod, slots, length, width)

    there_one, give_attn, in_grad, input_rows = after(there_one, give_attn, in_grad, input_rows)
    there_attn = swap_with(give_attn, "dp", 1)
    one_both = pair_sum(grad_one, there_one)
    one_half = line_sum(one_both)
    two_line, one_both, there_proj, input_rows = after(two_line, one_both, there_proj, input_rows)

    d_modulation = jnp.concatenate([input_rows[:, :2], middle_rows[:, 2:6]], axis=1).astype(BF16)
    packed_total = jnp.sum(packed_sums, axis=0)
    bias_sums = jnp.concatenate(
        [
            packed_total[0],
            packed_total[2],
            jnp.sum(middle_rows[:, 6], axis=0),
            hidden_sums[0],
            jnp.sum(mlp_sums[:, 0], axis=0),
        ]
    ).astype(BF16)

    report = jnp.concatenate([style.reshape(-1), d_modulation.reshape(-1), bias_sums])
    report = jnp.stack([report, swap_with(report, "dp", 1)])
    reports = gather_line(report, "fsdp").reshape(2 * lines, -1)
    edge = slots * width
    style_group = reports[:, :edge].reshape(2 * lines * slots, width)
    mod_group = reports[:, edge : 7 * edge].reshape(2 * lines * slots, 6 * width)
    style_own = lax.dynamic_slice_in_dim(style_group, line * rows, rows, axis=1)
    grad_ada = dot_tn(style_own, mod_group)
    bias_group = jnp.concatenate(
        [
            jnp.sum(mod_group.astype(F32), axis=0),
            jnp.sum(reports[:, 7 * edge :].astype(F32), axis=0),
        ]
    )
    own_bias = biases.shape[0]
    grad_bias = lax.dynamic_slice_in_dim(bias_group, line * own_bias, own_bias, axis=0)

    power = step_count[0].astype(F32)
    fix_one = 1.0 - jnp.power(BETA_ONE, power)
    fix_two = 1.0 - jnp.power(BETA_TWO, power)
    rates = learning_rates(D, FF)
    reduced = [None] * 6
    firsts_out = [None] * 6
    seconds_out = [None] * 6
    deltas_out = [None] * 6
    outers_out = [None] * 6
    weights_out = [None] * 6

    low = rep % 2
    where = jnp.stack([pair, low]).astype(jnp.int32)
    fixes = jnp.stack([fix_one, fix_two])

    def local_delta(master, first, second, gradient, rate):
        first_next, second_next = adam_moments(first, second, gradient)
        delta = adam_delta(master, first_next, second_next, rate, fix_one, fix_two)
        return delta, first_next, second_next

    def state(index):
        return masters[index], firsts[index][0], seconds[index][0], rates[index]

    def sum_near(keep, give):
        return (keep.astype(F32) + swap_with(give, "rep", 1).astype(F32)).astype(BF16)

    def sum_far(total):
        return (total.astype(F32) + swap_with(total, "rep", 2).astype(F32)).astype(BF16)

    def outer_step(index, totals, shift=0):
        deltas_out[index], outers_out[index], weights_out[index] = outer_whole(
            where, totals, masters[index], outers[index], groups, shift
        )

    reduced[0] = grad_ada
    firsts_out[0], seconds_out[0], ada_keep, ada_give = adam_whole(
        "given", where, fixes, [grad_ada], *state(0)
    )
    one_half, there_attn, two_line, ada_keep, ada_give, grad_bias = after(
        one_half, there_attn, two_line, ada_keep, ada_give, grad_bias
    )
    attn_both = jnp.concatenate(
        [pair_sum(grad_qkv, there_attn), pair_sum(grad_proj, there_proj)], axis=2
    )
    attn_both, two_line, one_half, ada_give, grad_bias = after(
        attn_both, two_line, one_half, ada_give, grad_bias
    )
    attn_half = line_sum(attn_both)
    ada_total = sum_far(sum_near(ada_keep, ada_give))
    one_near = sum_near(*adam_own(where, fixes, one_half, [state(3)]))
    one_far = swap_with(one_near, "rep", 2)
    two_there = swap_with(two_line, "dp", 1)
    ada_total, one_half = after(ada_total, one_half)
    one_there = swap_with(one_half, "dp", 1)
    outer_step(0, [ada_total, swap_with(ada_total, "rep", 1)])
    two_there, weights_out[0], one_far = after(two_there, weights_out[0], one_far)
    one_total = (one_near.astype(F32) + one_far.astype(F32)).astype(BF16)
    one_pair = swap_with(one_total, "dp", 1)
    reduced[4], firsts_out[4], seconds_out[4], two_keep, two_give = adam_whole(
        "sum", where, fixes, [two_line, two_there], *state(4)
    )
    bias_delta, bias_first, bias_second = local_delta(
        biases, first_bias[0], second_bias[0], grad_bias, rates[5]
    )
    reduced[5] = grad_bias
    firsts_out[5], seconds_out[5] = bias_first[None], bias_second[None]
    bias_total = (bias_delta.astype(F32) + swap_with(bias_delta, "rep", 1).astype(F32)).astype(BF16)
    bias_total = bias_total.astype(F32) + swap_with(bias_total, "rep", 2).astype(F32)
    deltas_out[5] = bias_total / groups
    outers_out[5] = OUTER_MOMENTUM * outer_bias + deltas_out[5]
    weights_out[5] = biases - OUTER_RATE * (deltas_out[5] + OUTER_MOMENTUM * outers_out[5])
    attn_half, two_keep, two_give, one_there = after(attn_half, two_keep, two_give, one_there)
    attn_near = sum_near(*adam_own(where, fixes, attn_half, [state(1), state(2)]))
    attn_there = swap_with(attn_half, "dp", 1)
    attn_far = swap_with(attn_near, "rep", 2)
    reduced[3], firsts_out[3], seconds_out[3] = adam_whole(
        "halves", where, fixes, [one_half, one_there], *state(3)
    )
    outer_step(
        3, [one_total, one_pair, swap_with(one_total, "rep", 1), swap_with(one_pair, "rep", 1)]
    )
    attn_far, attn_there, firsts_out[3], weights_out[3] = after(
        attn_far, attn_there, firsts_out[3], weights_out[3]
    )
    attn_total = (attn_near.astype(F32) + attn_far.astype(F32)).astype(BF16)
    attn_pair = swap_with(attn_total, "dp", 1)
    two_near = sum_near(two_keep, two_give)
    two_far = swap_with(two_near, "rep", 2)
    attn_units = 3
    for index, shift in ((1, 0), (2, attn_units)):
        reduced[index], firsts_out[index], seconds_out[index] = adam_whole(
            "halves", where, fixes, [attn_half, attn_there], *state(index), shift=shift
        )
    two_far, firsts_out[1], firsts_out[2] = after(two_far, firsts_out[1], firsts_out[2])
    two_total = (two_near.astype(F32) + two_far.astype(F32)).astype(BF16)
    outer_step(4, [two_total, swap_with(two_total, "rep", 1)])
    totals = [attn_total, attn_pair, swap_with(attn_total, "rep", 1), swap_with(attn_pair, "rep", 1)]
    outer_step(1, totals)
    outer_step(2, totals, attn_units)
    grads_out = tuple((g if g.ndim == f.ndim else g[None] for g, f in zip(reduced, firsts)))
    return (
        (result.reshape(images.shape), in_grad.reshape(images.shape))
        + grads_out
        + tuple(firsts_out)
        + tuple(seconds_out)
        + tuple(deltas_out)
        + tuple(outers_out)
        + tuple(weights_out)
    )


def solution(mesh):
    in_specs = (
        P(("rep", "dp", "fsdp"), None, None),
        P(("rep", "dp", "fsdp"), None, None),
        P(("rep", "dp", "fsdp")),
        P(("rep", "dp", "fsdp")),
        P(("rep", "dp", "fsdp")),
        P(),
        P(),
        P("fsdp", None),
        P("fsdp", None),
        P("fsdp", None),
        P("fsdp", None),
        P("fsdp", None),
        P("fsdp"),
        P("rep", "fsdp", None),
        P("rep", "fsdp", None),
        P("rep", "fsdp", None),
        P("rep", "fsdp", None),
        P("rep", "fsdp", None),
        P("rep", "fsdp"),
        P("rep", "fsdp", None),
        P("rep", "fsdp", None),
        P("rep", "fsdp", None),
        P("rep", "fsdp", None),
        P("rep", "fsdp", None),
        P("rep", "fsdp"),
        P("fsdp", None),
        P("fsdp", None),
        P("fsdp", None),
        P("fsdp", None),
        P("fsdp", None),
        P("fsdp"),
    )
    out_specs = (
        P(("rep", "dp", "fsdp"), None, None),
        P(("rep", "dp", "fsdp"), None, None),
        P("rep", "fsdp", None),
        P("rep", "fsdp", None),
        P("rep", "fsdp", None),
        P("rep", "fsdp", None),
        P("rep", "fsdp", None),
        P("rep", "fsdp"),
        P("rep", "fsdp", None),
        P("rep", "fsdp", None),
        P("rep", "fsdp", None),
        P("rep", "fsdp", None),
        P("rep", "fsdp", None),
        P("rep", "fsdp"),
        P("rep", "fsdp", None),
        P("rep", "fsdp", None),
        P("rep", "fsdp", None),
        P("rep", "fsdp", None),
        P("rep", "fsdp", None),
        P("rep", "fsdp"),
        P("fsdp", None),
        P("fsdp", None),
        P("fsdp", None),
        P("fsdp", None),
        P("fsdp", None),
        P("fsdp"),
        P("fsdp", None),
        P("fsdp", None),
        P("fsdp", None),
        P("fsdp", None),
        P("fsdp", None),
        P("fsdp"),
        P("fsdp", None),
        P("fsdp", None),
        P("fsdp", None),
        P("fsdp", None),
        P("fsdp", None),
        P("fsdp"),
    )
    return jax.shard_map(body, mesh=mesh, in_specs=in_specs, out_specs=out_specs, check_vma=False)
```
